32 devices in a mesh: seq: 2 (over y), shard: 16 (over z, x, core).
Axes of the slice: x: 2, y: 2, z: 4, core: 2. Of those that a mesh axis runs over, the one named last changes fastest.
Arguments:
- tokens: bfloat16 [32768, 768], P(('seq', 'shard')), may hold values from -6 to 6
- qkv_weight: bfloat16 [2, 768, 2304], P(None, 'shard'), may hold values from -0.21875 to 0.21875
- out_weight: bfloat16 [2, 768, 768], P(None, 'shard'), may hold values from -0.875 to 0.875
- up_weight: bfloat16 [2, 768, 3072], P(None, 'shard'), may hold values from -0.21875 to 0.21875
- down_weight: bfloat16 [2, 3072, 768], P(None, 'shard'), may hold values from -0.109375 to 0.109375
- norm_gains: bfloat16 [2, 2, 768], P(None, None, 'shard'), may hold values from 0.5 to 1.5
- biases: bfloat16 [2, 5, 768], P(None, None, 'shard'), may hold values from -2.5 to 2.5
- up_bias: bfloat16 [2, 3072], P(None, 'shard'), may hold values from -2.5 to 2.5
- position_table: bfloat16 [64, 768], P(None, 'shard'), may hold values from -4 to 4
- segment_docs: int32 [2, 128], P('seq'), may hold values from 0 to 7, never falling along the last dimension, each value on 1 to 64 neighbouring positions
- cotangent: bfloat16 [32768, 768], P(('seq', 'shard')), may hold values from -6 to 6
Outputs:
- merged: bfloat16 [32768, 768], P(('seq', 'shard'))
- grad_tokens: bfloat16 [32768, 768], P(('seq', 'shard'))
- grad_qkv: float32 [2, 768, 2304], P(None, 'shard')
- grad_out: float32 [2, 768, 768], P(None, 'shard')
- grad_up: float32 [2, 768, 3072], P(None, 'shard')
- grad_down: float32 [2, 3072, 768], P(None, 'shard')
- grad_gains: float32 [2, 2, 768], P(None, None, 'shard')
- grad_biases: float32 [2, 5, 768], P(None, None, 'shard')
- grad_up_bias: float32 [2, 3072], P(None, 'shard')
- grad_table: float32 [64, 768], P(None, 'shard')
The draws below stay inside these ranges and needn't reach their ends.
Inputs may be any that keep to these rules, and one draw needn't show every extreme that they name: `segment_docs`: along each sequence the document numbers never fall, each document covers 1 to 64 segments, and one covers exactly 64.
All inputs are finite; a program needn't handle non-finite values.
Results may differ from the reference program's by a relative error of at most 0.024.
Values may be sent and summed in bfloat16 or wider, within the bound.
No kernel may reach another device: no remote copies, remote signals or barrier semaphores. Data moves between devices by JAX's collectives and lax.ppermute only.
A program may use at most 256 MiB of HBM per device.

```python
import math
import jax
import jax.numpy as jnp
import numpy as np
from jax import lax

D = 768
HEADS = 12
HEAD = 64
FF = 3072
SEG = 128
MAXSEG = 64
SEQS = 2
SEGS = 128
TOKENS = 32768
DOCS = 8
DOC_MOST = 64


def block_levels(rng, dims, shards, smallest, top_value):
    level, own = 1.0, jax.random.fold_in(rng, 6)
    for dim, parts in shards:
        heights = jnp.exp(jax.random.uniform(jax.random.fold_in(own, dim), (parts,), jnp.float32, smallest / len(shards), top_value / len(shards)))
        level = level * jnp.repeat(heights, dims[dim] // parts).reshape([-1 if axis == dim else 1 for axis in range(len(dims))])
    return level


def length_profile(count, total, limit, lean):
    weights = [(1 << 20) // math.isqrt(standing ** lean) + 1 for standing in range(2, count + 1)]
    spare, given = total - limit - (count - 1), [1] * (count - 1)
    while spare > 0:
        free = [i for i in range(count - 1) if given[i] < limit]
        pool, left = sum([weights[i] for i in free]), spare
        for i in free:
            more = min(limit - given[i], max(1, left * weights[i] // pool), spare)
            given[i] = given[i] + more
            spare = spare - more
    return np.array([limit] + given)


def uneven_parts(rng, number_of, total, most, slope):
    if number_of == 2:
        one = jax.random.randint(rng, (), max(1, total - most), min(most, total - 1) + 1)
        return jnp.stack([one, total - one])
    sizes = jnp.asarray(length_profile(number_of, total, most, slope), jnp.int32)
    couples = (number_of - 1) // 2
    donor, taker = sizes[1:1 + 2 * couples:2], sizes[2:2 + 2 * couples:2]
    room = jnp.minimum(donor - 1, most - taker)
    passed = jax.random.randint(jax.random.fold_in(rng, 1), (couples,), 0, 1 << 20) % (room + 1)
    sizes = sizes.at[1:1 + 2 * couples:2].set(donor - passed).at[2:2 + 2 * couples:2].set(taker + passed)
    return sizes[jax.random.permutation(jax.random.fold_in(rng, 2), number_of)]


def scatter_about(own_key, extent, scale, reach, cuts=(), kind=jnp.bfloat16):
    level = block_levels(own_key, extent, cuts, -0.22, 0.18) if cuts else 1.0
    array = jax.random.normal(own_key, extent, jnp.float32) * scale * level
    return jnp.minimum(jnp.maximum(array, -reach), reach).astype(kind)


def setup_inputs(seed: int = 0) -> dict:
    arg_keys = jax.random.split(jax.random.key(seed), 12)
    return {
        "tokens": scatter_about(arg_keys[0], (TOKENS, D), 1.0, 6.0, ((0, 32),)),
        "qkv_weight": scatter_about(arg_keys[1], (2, D, 3 * D), D ** -0.5, 0.21875, ((1, 16),)),
        "out_weight": scatter_about(arg_keys[2], (2, D, D), (D // 16) ** -0.5, 0.875, ((1, 16),)),
        "up_weight": scatter_about(arg_keys[3], (2, D, FF), D ** -0.5, 0.21875, ((1, 16),)),
        "down_weight": scatter_about(arg_keys[4], (2, FF, D), FF ** -0.5, 0.109375, ((1, 16),)),
        "norm_gains": jnp.clip(1.0 + 0.1 * jax.random.normal(arg_keys[5], (2, 2, D), jnp.float32), 0.5, 1.5).astype(jnp.bfloat16),
        "biases": scatter_about(arg_keys[6], (2, 5, D), 0.3, 2.5, ((2, 16),)),
        "up_bias": scatter_about(arg_keys[7], (2, FF), 0.3, 2.5, ((1, 16),)),
        "position_table": scatter_about(arg_keys[8], (MAXSEG, D), 0.5, 4.0, ((1, 16),)),
        "segment_docs": jax.vmap(lambda own: jnp.searchsorted(jnp.cumsum(uneven_parts(own, DOCS, SEGS, DOC_MOST, 0)), jnp.arange(SEGS), side="right"))(jax.random.split(arg_keys[9], SEQS)).reshape((SEQS, SEGS)).astype(jnp.int32),
        "cotangent": scatter_about(arg_keys[10], (TOKENS, D), 1.0, 6.0, ((0, 32),)),
    }


@jax.custom_vjp
def low(v):
    return lax.optimization_barrier(v.astype(jnp.bfloat16)).astype(jnp.float32)

@jax.custom_vjp
def low_back(v):
    return v

def low_keep(v):
    return (low(v), None)

def low_pass(kept, grad):
    return (grad,)

def back_keep(v):
    return (v, None)

def back_low(kept, grad):
    return (low(grad),)
low.defvjp(low_keep, low_pass)
low_back.defvjp(back_keep, back_low)
EPSILON = 1e-05
HIGHEST = lax.Precision.HIGHEST
MASKED = -1e+30

def norm_rows(summed, norm_gain, norm_shift):
    centred = summed - lax.optimization_barrier(jnp.mean(summed, axis=-1, keepdims=True))
    spread = lax.optimization_barrier(jnp.mean(centred * centred, axis=-1, keepdims=True))
    return centred * lax.rsqrt(spread + EPSILON) * norm_gain + norm_shift

def attend(queries, key_rows, value_rows, allowed):
    scores = jnp.einsum('brhe,bkhe->bhrk', queries, key_rows, precision=HIGHEST) * HEAD ** (-0.5)
    scores = low_back(scores)
    scores = jnp.where(allowed, scores, MASKED)
    weights = jax.nn.softmax(scores, axis=-1)
    return jnp.einsum('bhrk,bkhe->brhe', low(weights), value_rows, precision=HIGHEST)

def block(inputs, block_params, allowed, group_count, group_rows):
    qkv_full, out_full, up_full, down_full, gain_full, bias_full, up_bias_full = block_params
    row_count = inputs.shape[0]
    entry_rows = low(inputs)
    projected = jnp.dot(entry_rows, qkv_full, precision=HIGHEST)
    queries = low_back(low(projected[:, :D]))
    key_rows = low_back(low(projected[:, D:2 * D]))
    value_rows = low_back(low(projected[:, 2 * D:] + bias_full[0]))
    view_shape = (group_count, group_rows, HEADS, HEAD)
    attended = attend(queries.reshape(view_shape), key_rows.reshape(view_shape), value_rows.reshape(view_shape), allowed)
    attended = low_back(low(attended.reshape(row_count, D)))
    branch = low_back(jnp.dot(attended, out_full, precision=HIGHEST) + bias_full[1])
    first_out = norm_rows(inputs + branch, gain_full[0], bias_full[3])
    hidden = low_back(jnp.dot(low(first_out), up_full, precision=HIGHEST) + up_bias_full)
    active = low(jax.nn.gelu(hidden, approximate=False))
    feed_out = low_back(jnp.dot(active, down_full, precision=HIGHEST) + bias_full[2])
    return norm_rows(first_out + feed_out, gain_full[1], bias_full[4])

def layer(tokens, qkv_weight, out_weight, up_weight, down_weight, norm_gains, biases, up_bias, position_table, segment_docs):
    token_count = tokens.shape[0]
    seq_count = segment_docs.shape[0]
    seg_count = segment_docs.shape[1]
    all_segs = token_count // SEG

    def block_params(index):
        return (qkv_weight[index], out_weight[index], up_weight[index], down_weight[index], norm_gains[index], biases[index], up_bias[index])
    everywhere = jnp.ones((1, 1, 1, 1), dtype=bool)
    seg_out = block(tokens, block_params(0), everywhere, all_segs, SEG).reshape(all_segs, SEG, D)
    heads_in = low(seg_out[:, 0, :]).reshape(seq_count, seg_count, D)
    same_doc = segment_docs[:, :, None] == segment_docs[:, None, :]
    ordinal = jnp.arange(seg_count, dtype=jnp.int32)
    earlier = ordinal[:, None] > ordinal[None, :]
    position = lax.optimization_barrier(jnp.sum((same_doc & earlier[None]).astype(jnp.int32), axis=-1))
    cross_in = heads_in + position_table[position]
    cross_out = block(cross_in.reshape(seq_count * seg_count, D), block_params(1), same_doc[:, None], seq_count, seg_count)
    merged = seg_out.at[:, 0, :].set(cross_out)
    return merged.reshape(token_count, D)

def reference(tokens, qkv_weight, out_weight, up_weight, down_weight, norm_gains, biases, up_bias, position_table, segment_docs, cotangent):
    inputs = (tokens.astype(jnp.float32), qkv_weight.astype(jnp.float32), out_weight.astype(jnp.float32), up_weight.astype(jnp.float32), down_weight.astype(jnp.float32), norm_gains.astype(jnp.float32), biases.astype(jnp.float32), up_bias.astype(jnp.float32), position_table.astype(jnp.float32))

    def run_layer(*values):
        return layer(*values, segment_docs)
    result, pull_back = jax.vjp(run_layer, *inputs)
    grads = pull_back(cotangent.astype(jnp.float32))
    return (result.astype(jnp.bfloat16), grads[0].astype(jnp.bfloat16), grads[1], grads[2], grads[3], grads[4], grads[5], grads[6], grads[7], grads[8])
```

```python
from functools import partial

import jax
import jax.numpy as jnp
from jax import lax
from jax.experimental import pallas as pl
from jax.experimental.pallas import tpu as pltpu
from jax.sharding import PartitionSpec as P

HEAD = 64
SEG = 128
EPSILON = 1e-05
MASKED = -1e30
BF = jnp.bfloat16
F32 = jnp.float32
TILE = 256
VMEM_LIMIT = 60 * 1024 * 1024

GAIN1, GAIN2, BIAS_V, BIAS_O, BIAS_D, SHIFT1, SHIFT2, UP0 = 0, 1, 2, 3, 4, 5, 6, 7
VEC_ROWS = 16


def dot_nn(a, b):
    return lax.dot_general(a, b, (((1,), (0,)), ((), ())), preferred_element_type=F32)


def dot_nt(a, b):
    return lax.dot_general(a, b, (((1,), (1,)), ((), ())), preferred_element_type=F32)


def dot_tn(a, b):
    return lax.dot_general(a, b, (((0,), (0,)), ((), ())), preferred_element_type=F32)


def row_mean(x):
    return jnp.mean(x, axis=-1, keepdims=True)


def col_sum(x):
    return jnp.sum(x.astype(F32), axis=0, keepdims=True)


def norm_rows(z):
    centred = z - row_mean(z)
    inverse = lax.rsqrt(row_mean(centred * centred) + EPSILON)
    return centred * inverse, inverse


def norm_back(scaled, normed, inverse):
    return inverse * (scaled - row_mean(scaled) - normed * row_mean(scaled * normed))


def gelu_both(u):
    phi = 0.5 + 0.5 * lax.erf(u * (2.0**-0.5))
    return u * phi, phi + u * jnp.exp(-0.5 * u * u) * 0.3989422804014327


def halves(pair):
    lane = lax.broadcasted_iota(jnp.int32, pair.shape, 1)
    zero = jnp.zeros_like(pair)
    return jnp.concatenate([jnp.where(lane < HEAD, pair, zero), jnp.where(lane < HEAD, zero, pair)], axis=0)


def side_by_side(stacked):
    rows = stacked.shape[0] // 2
    return jnp.concatenate([stacked[:rows], stacked[rows:]], axis=1)


def pair_forward(q, k, v, allowed):
    scores = dot_nt(halves(q), k) * (HEAD**-0.5)
    if allowed is not None:
        scores = jnp.where(allowed, scores, MASKED)
    top = jnp.max(scores, axis=-1, keepdims=True)
    powers = jnp.exp(scores - top)
    weights = (powers / jnp.sum(powers, axis=-1, keepdims=True)).astype(BF)
    return weights, dot_nn(side_by_side(weights), halves(v)).astype(BF)


def pair_backward(q, k, v, weights, d_out):
    d_stack = halves(d_out)
    d_weights = dot_nt(d_stack, v)
    wide = weights.astype(F32)
    inner = jnp.sum(wide * d_weights, axis=-1, keepdims=True)
    d_scores = (wide * (d_weights - inner)).astype(BF)
    scale = HEAD**-0.5
    d_q = dot_nn(side_by_side(d_scores), halves(k)) * scale
    d_k = dot_tn(d_scores, halves(q)) * scale
    d_v = dot_tn(weights, d_stack)
    return d_q.astype(BF), d_k.astype(BF), d_v.astype(BF)


class Pieces:
    def __init__(self, entries, chunk):
        self.arrays = [e[0] for e in entries]
        self.meta = [(e[1], e[2], e[0].shape[0]) for e in entries]
        self.chunk = chunk

    def copies(self, refs, origin, sems, col, width, dst, group=1, block=0):
        out = []
        for n, (ref, (entry, first, rows)) in enumerate(zip(refs, self.meta)):
            start = pl.multiple_of((origin[entry] * group + block) * self.chunk + first, 16)
            out.append(pltpu.make_async_copy(ref.at[:, pl.ds(col, width)], dst.at[pl.ds(start, rows), :], sems.at[n]))
        return out


def start_all(copies):
    for c in copies:
        c.start()


def wait_all(copies):
    for c in copies:
        c.wait()


ANY = pl.BlockSpec(memory_space=pl.ANY)
SMEM = pl.BlockSpec(memory_space=pltpu.SMEM)


def whole(shape):
    return pl.BlockSpec(shape, lambda *i: (0,) * len(shape), pipeline_mode=pl.Buffered(1))


def whole_out(shape):
    return pl.BlockSpec(shape, lambda *i: (0,) * len(shape))


def tile(*shape):
    return pl.BlockSpec(shape, lambda i: (i,) + (0,) * (len(shape) - 1))


def cost(flops, nbytes):
    return pl.CostEstimate(flops=int(flops), bytes_accessed=int(nbytes), transcendentals=0)


def attention_kernel(pieces, width, *refs):
    n = len(pieces.arrays)
    origin, x_ref, vec = refs[0], refs[1], refs[2]
    srcs = refs[3 : 3 + n]
    qkv_ref, a_ref, o_ref, h_ref, hb_ref, n_ref, r_ref = refs[3 + n : 10 + n]
    wqkv, wout, sem1, sem2 = refs[10 + n :]

    @pl.when(pl.program_id(0) == 0)
    def _():
        first = pieces.copies(srcs, origin, sem1, 0, 3 * width, wqkv)
        second = pieces.copies(srcs, origin, sem2, 3 * width, width, wout)
        start_all(first)
        start_all(second)
        wait_all(first)
        wait_all(second)

    x = x_ref[...]
    qkv = dot_nn(x, wqkv[...])
    qkv_ref[:, : 2 * width] = qkv[:, : 2 * width].astype(BF)
    qkv_ref[:, 2 * width :] = (qkv[:, 2 * width :] + vec[BIAS_V : BIAS_V + 1, :]).astype(BF)
    for s in range(TILE // SEG):
        rows = pl.ds(s * SEG, SEG)
        for p in range(width // 128):
            q = qkv_ref[rows, pl.ds(p * 128, 128)]
            k = qkv_ref[rows, pl.ds(width + p * 128, 128)]
            v = qkv_ref[rows, pl.ds(2 * width + p * 128, 128)]
            weights, out = pair_forward(q, k, v, None)
            a_ref[s, p] = weights
            o_ref[rows, pl.ds(p * 128, 128)] = out
    z = x.astype(F32) + dot_nn(o_ref[...], wout[...]) + vec[BIAS_O : BIAS_O + 1, :]
    normed, inverse = norm_rows(z)
    h = normed * vec[GAIN1 : GAIN1 + 1, :] + vec[SHIFT1 : SHIFT1 + 1, :]
    h_ref[...] = h
    hb_ref[...] = h.astype(BF)
    n_ref[...] = normed.astype(BF)
    r_ref[...] = inverse


def attention_call(origin, x, vec, pieces):
    rows, width = x.shape
    n = len(pieces.arrays)
    segs = rows // SEG
    pairs = width // 128
    return pl.pallas_call(
        partial(attention_kernel, pieces, width),
        grid=(rows // TILE,),
        in_specs=[SMEM, tile(TILE, width), whole(vec.shape)] + [ANY] * n,
        out_specs=[
            tile(TILE, 3 * width),
            tile(TILE // SEG, pairs, 2 * SEG, SEG),
            tile(TILE, width),
            tile(TILE, width),
            tile(TILE, width),
            tile(TILE, width),
            tile(TILE, 1),
        ],
        out_shape=[
            jax.ShapeDtypeStruct((rows, 3 * width), BF),
            jax.ShapeDtypeStruct((segs, pairs, 2 * SEG, SEG), BF),
            jax.ShapeDtypeStruct((rows, width), BF),
            jax.ShapeDtypeStruct((rows, width), F32),
            jax.ShapeDtypeStruct((rows, width), BF),
            jax.ShapeDtypeStruct((rows, width), BF),
            jax.ShapeDtypeStruct((rows, 1), F32),
        ],
        scratch_shapes=[
            pltpu.VMEM((width, 3 * width), BF),
            pltpu.VMEM((width, width), BF),
            pltpu.SemaphoreType.DMA((n,)),
            pltpu.SemaphoreType.DMA((n,)),
        ],
        compiler_params=pltpu.CompilerParams(vmem_limit_bytes=VMEM_LIMIT),
        cost_estimate=cost(2 * rows * width * 5 * width, 16 * rows * width),
        name="segment_attention",
    )(origin, x, vec, *pieces.arrays)


def up_down_copies(pieces, srcs, origin, sem_up, sem_down, width, ff, wup, wdown):
    ups = pieces.copies(srcs, origin, sem_up, 0, ff, wup)
    downs = []
    group = ff // width
    for j in range(group):
        downs += pieces.copies(srcs, origin, sem_down.at[j], ff + j * width, width, wdown, group, j)
    return ups, downs


def feed_kernel(pieces, width, ff, *refs):
    n = len(pieces.arrays)
    origin, h_ref, c_ref, o_ref, n_ref, r_ref, vec, upb = refs[:8]
    srcs = refs[8 : 8 + n]
    y_ref, g_ref, gp_ref, dz_ref, pay_ref, sums_ref = refs[8 + n : 14 + n]
    wup, wdown, sem_up, sem_down = refs[14 + n :]
    step = pl.program_id(0)

    @pl.when(step == 0)
    def _():
        ups, downs = up_down_copies(pieces, srcs, origin, sem_up, sem_down, width, ff, wup, wdown)
        start_all(ups)
        start_all(downs)
        wait_all(ups)
        wait_all(downs)
        sums_ref[...] = jnp.zeros_like(sums_ref)

    h = h_ref[...]
    hb = h.astype(BF)
    block = 512
    total = jnp.zeros((TILE, width), F32)
    u = dot_nn(hb, wup[:, :block]) + upb[:, :block]
    for j in range(ff // block):
        cols = slice(j * block, (j + 1) * block)
        if (j + 1) * block < ff:
            later = slice((j + 1) * block, (j + 2) * block)
            u_next = dot_nn(hb, wup[:, later]) + upb[:, later]
        active, slope = gelu_both(u)
        active = active.astype(BF)
        g_ref[:, cols] = active
        gp_ref[:, cols] = slope.astype(BF)
        total = total + dot_nn(active, wdown[cols, :])
        u = u_next
    normed, inverse = norm_rows(h + total + vec[BIAS_D : BIAS_D + 1, :])
    gain = vec[GAIN2 : GAIN2 + 1, :]
    y = normed * gain + vec[SHIFT2 : SHIFT2 + 1, :]
    y_ref[...] = y.astype(BF)
    row = lax.broadcasted_iota(jnp.int32, (TILE, 1), 0)
    dy = jnp.where(row % SEG == 0, 0.0, c_ref[...].astype(F32))
    dz = norm_back(dy * gain, normed, inverse)
    dz_ref[...] = dz
    sums_ref[0:1, :] += col_sum(dy * normed)
    sums_ref[1:2, :] += col_sum(dy)
    sums_ref[2:3, :] += col_sum(dz.astype(BF))
    lane = lax.broadcasted_iota(jnp.int32, (1, 128), 1)
    for s in range(TILE // SEG):
        here = slice(s * SEG, s * SEG + 1)
        at = slice(s, s + 1)
        pay_ref[0, at, 0:width] = y[here]
        pay_ref[0, at, width : 2 * width] = h[here]
        pay_ref[0, at, 2 * width : 3 * width] = o_ref[s * SEG : s * SEG + 16, :].astype(F32)[:1]
        pay_ref[0, at, 3 * width : 4 * width] = n_ref[s * SEG : s * SEG + 16, :].astype(F32)[:1]
        r = r_ref[here]
        r_high = r.astype(BF).astype(F32)
        pay_ref[0, at, 4 * width :] = jnp.where(lane == 0, r_high, jnp.where(lane == 1, r - r_high, 0.0))


def feed_call(origin, h, cot, o, n1, r1, vec, upb, pieces, ff):
    rows, width = h.shape
    n = len(pieces.arrays)
    group = ff // width
    return pl.pallas_call(
        partial(feed_kernel, pieces, width, ff),
        grid=(rows // TILE,),
        in_specs=[
            SMEM,
            tile(TILE, width),
            tile(TILE, width),
            tile(TILE, width),
            tile(TILE, width),
            tile(TILE, 1),
            whole(vec.shape),
            whole(upb.shape),
        ]
        + [ANY] * n,
        out_specs=[
            tile(TILE, width),
            tile(TILE, ff),
            tile(TILE, ff),
            tile(TILE, width),
            pl.BlockSpec((1, TILE // SEG, 4 * width + 128), lambda i: (i, 0, 0)),
            whole_out((8, width)),
        ],
        out_shape=[
            jax.ShapeDtypeStruct((rows, width), BF),
            jax.ShapeDtypeStruct((rows, ff), BF),
            jax.ShapeDtypeStruct((rows, ff), BF),
            jax.ShapeDtypeStruct((rows, width), F32),
            jax.ShapeDtypeStruct((rows // TILE, TILE // SEG, 4 * width + 128), F32),
            jax.ShapeDtypeStruct((8, width), F32),
        ],
        scratch_shapes=[
            pltpu.VMEM((width, ff), BF),
            pltpu.VMEM((ff, width), BF),
            pltpu.SemaphoreType.DMA((n,)),
            pltpu.SemaphoreType.DMA((group, n)),
        ],
        compiler_params=pltpu.CompilerParams(vmem_limit_bytes=VMEM_LIMIT),
        cost_estimate=cost(4 * rows * width * ff, 4 * rows * ff),
        name="segment_feed",
    )(origin, h, cot, o, n1, r1, vec, upb, *pieces.arrays)


def feed_back_kernel(pieces, pieces_out, width, ff, *refs):
    n, m = len(pieces.arrays), len(pieces_out.arrays)
    origin, dz_ref, gp_ref, n_ref, r_ref, vec = refs[:6]
    srcs = refs[6 : 6 + n]
    srcs_out = refs[6 + n : 6 + n + m]
    dm_ref, du_ref, dz1_ref, db_ref, do_ref, sums_ref, upsum_ref = refs[6 + n + m : 13 + n + m]
    wup, wdown, wout, sem_up, sem_down, sem_out = refs[13 + n + m :]

    @pl.when(pl.program_id(0) == 0)
    def _():
        ups, downs = up_down_copies(pieces, srcs, origin, sem_up, sem_down, width, ff, wup, wdown)
        outs = pieces_out.copies(srcs_out, origin, sem_out, 3 * width, width, wout)
        start_all(downs)
        start_all(ups)
        start_all(outs)
        wait_all(downs)
        wait_all(ups)
        wait_all(outs)
        sums_ref[...] = jnp.zeros_like(sums_ref)
        upsum_ref[...] = jnp.zeros_like(upsum_ref)

    dz = dz_ref[...]
    dm = dz.astype(BF)
    dm_ref[...] = dm
    block = 512
    total = dz
    dg = dot_nt(dm, wdown[:block, :])
    for j in range(ff // block):
        cols = slice(j * block, (j + 1) * block)
        if (j + 1) * block < ff:
            dg_next = dot_nt(dm, wdown[(j + 1) * block : (j + 2) * block, :])
        du = (dg * gp_ref[:, cols].astype(F32)).astype(BF)
        du_ref[:, cols] = du
        upsum_ref[0:1, cols] += col_sum(du)
        total = total + dot_nt(du, wup[:, cols])
        dg = dg_next
    normed = n_ref[...].astype(F32)
    dz1 = norm_back(total * vec[GAIN1 : GAIN1 + 1, :], normed, r_ref[...])
    dz1_ref[...] = dz1
    db = dz1.astype(BF)
    db_ref[...] = db
    do_ref[...] = dot_nt(db, wout[...]).astype(BF)
    sums_ref[0:1, :] += col_sum(total * normed)
    sums_ref[1:2, :] += col_sum(total)
    sums_ref[2:3, :] += col_sum(db)


def feed_back_call(origin, dz, gp, n1, r1, vec, pieces, pieces_out):
    rows, width = dz.shape
    ff = gp.shape[1]
    n, m = len(pieces.arrays), len(pieces_out.arrays)
    return pl.pallas_call(
        partial(feed_back_kernel, pieces, pieces_out, width, ff),
        grid=(rows // TILE,),
        in_specs=[SMEM, tile(TILE, width), tile(TILE, ff), tile(TILE, width), tile(TILE, 1), whole(vec.shape)]
        + [ANY] * (n + m),
        out_specs=[
            tile(TILE, width),
            tile(TILE, ff),
            tile(TILE, width),
            tile(TILE, width),
            tile(TILE, width),
            whole_out((8, width)),
            whole_out((8, ff)),
        ],
        out_shape=[
            jax.ShapeDtypeStruct((rows, width), BF),
            jax.ShapeDtypeStruct((rows, ff), BF),
            jax.ShapeDtypeStruct((rows, width), F32),
            jax.ShapeDtypeStruct((rows, width), BF),
            jax.ShapeDtypeStruct((rows, width), BF),
            jax.ShapeDtypeStruct((8, width), F32),
            jax.ShapeDtypeStruct((8, ff), F32),
        ],
        scratch_shapes=[
            pltpu.VMEM((width, ff), BF),
            pltpu.VMEM((ff, width), BF),
            pltpu.VMEM((width, width), BF),
            pltpu.SemaphoreType.DMA((n,)),
            pltpu.SemaphoreType.DMA((ff // width, n)),
            pltpu.SemaphoreType.DMA((m,)),
        ],
        compiler_params=pltpu.CompilerParams(vmem_limit_bytes=VMEM_LIMIT),
        cost_estimate=cost(4 * rows * width * ff + 2 * rows * width * width, 4 * rows * ff),
        name="segment_feed_back",
    )(origin, dz, gp, n1, r1, vec, *pieces.arrays, *pieces_out.arrays)


class Slots:
    def __init__(self, chips, chunk, both):
        self.chips, self.chunk, self.both = chips, chunk, both

    def shapes(self, cols):
        s = jax.ShapeDtypeStruct((self.chips, self.chunk, cols), BF)
        return [s, s] if self.both else [s]

    def store(self, table, outs, source, rows_first, rows, chunk_of, col, width):
        pass


def grads_kernel(chips, cores, chunk, width, ff, *refs):
    table, g_ref, dm_ref, du_ref, hb_ref, o_ref, db_ref = refs[:7]
    outs = refs[7 : 7 + cores]
    scratch = refs[7 + cores]
    step = pl.program_id(0)
    group = ff // width
    core = table[chips]

    def spread(first_device, devices, blocks, col):
        for q in range(devices // cores):
            slot = table[first_device // cores + q]
            for c in range(cores):
                device = q * cores + (jnp.bitwise_xor(core, c) if cores > 1 else 0)
                for b in range(blocks):
                    start = pl.multiple_of((device * blocks + b) * chunk, 16)
                    outs[c][slot, :, pl.ds(col + b * width, width)] = scratch[pl.ds(start, chunk), :].astype(BF)

    per = chips * cores // group if chips * cores >= group else 1
    for j in range(group):

        @pl.when(step == j)
        def _(j=j):
            scratch[...] = dot_tn(g_ref[...], dm_ref[...])
            if chips * cores >= group:
                spread(j * per, per, group, ff)
            else:
                outs[0][0, :, pl.ds(ff + j * width, width)] = scratch[...].astype(BF)

        @pl.when(step == group + j)
        def _(j=j):
            scratch[...] = dot_tn(hb_ref[...], du_ref[...])
            spread(0, chips * cores, 1, j * width)

    @pl.when(step == 2 * group)
    def _():
        scratch[...] = dot_tn(o_ref[...], db_ref[...])
        spread(0, chips * cores, 1, 2 * ff)


def grads_call(table, g, dm, du, hb, o, db, chips, cores, chunk):
    rows, ff = g.shape
    width = dm.shape[1]
    group = ff // width
    cols = 2 * ff + width
    return pl.pallas_call(
        partial(grads_kernel, chips, cores, chunk, width, ff),
        grid=(2 * group + 1,),
        in_specs=[
            SMEM,
            pl.BlockSpec((rows, width), lambda i: (0, jnp.minimum(i, group - 1))),
            whole((rows, width)),
            pl.BlockSpec((rows, width), lambda i: (0, jnp.clip(i - group, 0, group - 1))),
            whole((rows, width)),
            whole((rows, width)),
            whole((rows, width)),
        ],
        out_specs=[pl.BlockSpec((chips, chunk, cols), lambda i: (0, 0, 0), pipeline_mode=pl.Buffered(1))] * cores,
        out_shape=[jax.ShapeDtypeStruct((chips, chunk, cols), BF)] * cores,
        scratch_shapes=[pltpu.VMEM((width, width), F32)],
        compiler_params=pltpu.CompilerParams(vmem_limit_bytes=VMEM_LIMIT),
        cost_estimate=cost(2 * rows * width * cols, 4 * rows * ff + 4 * width * cols),
        name="segment_grads",
    )(table, g, dm, du, hb, o, db)


def attention_back_kernel(pieces, chips, cores, chunk, width, *refs):
    n = len(pieces.arrays)
    origin, table, qkv_ref, a_ref, do_ref, dz_ref, x_ref, do_first, dz_first = refs[:9]
    srcs = refs[9 : 9 + n]
    dx_ref = refs[9 + n]
    sums_ref = refs[10 + n]
    outs = refs[11 + n : 11 + n + cores]
    wqkv, total, dqkv, d_o, d_z, sem = refs[11 + n + cores :]
    step = pl.program_id(0)

    @pl.when(step == 0)
    def _():
        copies = pieces.copies(srcs, origin, sem, 0, 3 * width, wqkv)
        start_all(copies)
        wait_all(copies)
        total[...] = jnp.zeros_like(total)
        sums_ref[...] = jnp.zeros_like(sums_ref)

    d_o[...] = do_ref[...].astype(F32)
    d_z[...] = dz_ref[...]
    for s in range(TILE // SEG):
        at = pl.ds(table[chips + 1] + step * (TILE // SEG) + s, 1)
        d_o[s * SEG : s * SEG + 1, :] = do_first[at, :]
        d_z[s * SEG : s * SEG + 1, :] = dz_first[at, :]
    for s in range(TILE // SEG):
        rows = pl.ds(s * SEG, SEG)
        for p in range(width // 128):
            q = qkv_ref[rows, pl.ds(p * 128, 128)]
            k = qkv_ref[rows, pl.ds(width + p * 128, 128)]
            v = qkv_ref[rows, pl.ds(2 * width + p * 128, 128)]
            d_out = d_o[rows, pl.ds(p * 128, 128)].astype(BF)
            d_q, d_k, d_v = pair_backward(q, k, v, a_ref[s, p], d_out)
            dqkv[rows, pl.ds(p * 128, 128)] = d_q
            dqkv[rows, pl.ds(width + p * 128, 128)] = d_k
            dqkv[rows, pl.ds(2 * width + p * 128, 128)] = d_v
    sums_ref[0:1, :] += col_sum(dqkv[:, 2 * width :])
    dx_ref[...] = (d_z[...] + dot_nt(dqkv[...], wqkv[...])).astype(BF)
    total[...] += dot_tn(x_ref[...], dqkv[...])

    @pl.when(step == pl.num_programs(0) - 1)
    def _():
        core = table[chips]
        for q in range(chips):
            slot = table[q]
            for c in range(cores):
                device = q * cores + (jnp.bitwise_xor(core, c) if cores > 1 else 0)
                start = pl.multiple_of(device * chunk, 16)
                outs[c][slot] = total[pl.ds(start, chunk), :].astype(BF)


def attention_back_call(origin, table, qkv, a, do, dz, x, do_first, dz_first, pieces, chips, cores, chunk):
    rows, width = x.shape
    n = len(pieces.arrays)
    pairs = width // 128
    return pl.pallas_call(
        partial(attention_back_kernel, pieces, chips, cores, chunk, width),
        grid=(rows // TILE,),
        in_specs=[
            SMEM,
            SMEM,
            tile(TILE, 3 * width),
            tile(TILE // SEG, pairs, 2 * SEG, SEG),
            tile(TILE, width),
            tile(TILE, width),
            tile(TILE, width),
            whole(do_first.shape),
            whole(dz_first.shape),
        ]
        + [ANY] * n,
        out_specs=[tile(TILE, width), whole_out((8, width))]
        + [pl.BlockSpec((chips, chunk, 3 * width), lambda i: (0, 0, 0), pipeline_mode=pl.Buffered(1))] * cores,
        out_shape=[jax.ShapeDtypeStruct((rows, width), BF), jax.ShapeDtypeStruct((8, width), F32)]
        + [jax.ShapeDtypeStruct((chips, chunk, 3 * width), BF)] * cores,
        scratch_shapes=[
            pltpu.VMEM((width, 3 * width), BF),
            pltpu.VMEM((width, 3 * width), F32),
            pltpu.VMEM((TILE, 3 * width), BF),
            pltpu.VMEM((TILE, width), F32),
            pltpu.VMEM((TILE, width), F32),
            pltpu.SemaphoreType.DMA((n,)),
        ],
        compiler_params=pltpu.CompilerParams(vmem_limit_bytes=VMEM_LIMIT),
        cost_estimate=cost(2 * rows * width * 8 * width, 20 * rows * width),
        name="segment_attention_back",
    )(origin, table, qkv, a, do, dz, x, do_first, dz_first, *pieces.arrays)


def one_hot(rows, cols, base):
    r = lax.broadcasted_iota(jnp.int32, (rows, cols), 0)
    c = lax.broadcasted_iota(jnp.int32, (rows, cols), 1)
    return (r == c + base).astype(F32).astype(BF)


def own_cols(values, base, cols):
    return dot_nn(values.astype(BF), one_hot(values.shape[1], cols, base)).astype(BF)


def few_feed_forward(hb, h, vec, upb, wup, wdown, g_ref, gp_ref, ff):
    block = 512
    total = jnp.zeros(h.shape, F32)
    for j in range(ff // block):
        cols = slice(j * block, (j + 1) * block)
        active, slope = gelu_both(dot_nn(hb, wup[:, cols]) + upb[:, cols])
        active = active.astype(BF)
        g_ref[:, cols] = active
        gp_ref[:, cols] = slope.astype(BF)
        total = total + dot_nn(active, wdown[cols, :])
    return norm_rows(h + total + vec[BIAS_D : BIAS_D + 1, :])


def few_feed_backward(dy, n2, r2, n1, r1, hb, o, vec, wup, wdown, wout, g_ref, gp_ref, me, chunk, ff, outs):
    gup_ref, gdown_ref, gout_ref, sums_ref, upsum_ref = outs
    block = 512
    group = ff // hb.shape[1]
    base = me * chunk
    dz = norm_back(dy * vec[GAIN2 : GAIN2 + 1, :], n2, r2)
    dm = dz.astype(BF)
    total = dz
    own_h = own_cols(hb, base, chunk)
    own_g = jnp.zeros((hb.shape[0], group * chunk), F32)
    own_up = jnp.zeros((8, group * chunk), F32)
    for j in range(ff // block):
        cols = slice(j * block, (j + 1) * block)
        du = (dot_nt(dm, wdown[cols, :]) * gp_ref[:, cols].astype(F32)).astype(BF)
        total = total + dot_nt(du, wup[:, cols])
        gup_ref[:, cols] = dot_tn(own_h, du).astype(BF)
        chosen = one_hot(block, group * chunk, base * group - j * block)
        own_g = own_g + dot_nn(g_ref[:, cols], chosen)
        own_up = own_up + dot_nn(jnp.broadcast_to(col_sum(du), (8, block)).astype(BF), chosen)
    gdown_ref[...] = dot_tn(own_g.astype(BF), dm).astype(BF)
    upsum_ref[...] = own_up
    dz1 = norm_back(total * vec[GAIN1 : GAIN1 + 1, :], n1, r1)
    db = dz1.astype(BF)
    gout_ref[...] = dot_tn(own_cols(o, base, chunk), db).astype(BF)
    do = dot_nt(db, wout[...])
    sums = [col_sum(total * n1), col_sum(dy * n2), None, col_sum(db), col_sum(dm), col_sum(total), col_sum(dy)]
    sums[2] = jnp.zeros_like(sums[0])
    stacked = jnp.concatenate(sums + [jnp.zeros_like(sums[0])], axis=0)
    sums_ref[...] = dot_nn(stacked.astype(BF), one_hot(hb.shape[1], chunk, base))
    return dz1, do


def cross_kernel(pa, pb, width, ff, chunk, places_n, *refs):
    na, nb = len(pa.arrays), len(pb.arrays)
    origin, table, heads_ref, grad_ref, doc_col, doc_row, tab_ref, vec, upb = refs[:9]
    srca = refs[9 : 9 + na]
    srcb = refs[9 + na : 9 + na + nb]
    base_o = 9 + na + nb
    out_ref, dx_ref, gqkv_ref, gout_ref, gup_ref, gdown_ref, sums_ref, upsum_ref, gtab_ref = refs[base_o : base_o + 9]
    wqkv, wout, wup, wdown, qkv, a_ref, o_s, d_s, g_ref, gp_ref, sem_a, sem_o, sem_up, sem_down = refs[base_o + 9 :]
    rows = heads_ref.shape[0]
    me = table[0]
    ca = pa.copies(srca, origin, sem_a, 0, 3 * width, wqkv)
    co = pa.copies(srca, origin, sem_o, 3 * width, width, wout)
    ups, downs = up_down_copies(pb, srcb, origin, sem_up, sem_down, width, ff, wup, wdown)
    start_all(ca)
    start_all(co)
    start_all(ups)
    start_all(downs)
    same = doc_col[...] == doc_row[...]
    earlier = lax.broadcasted_iota(jnp.int32, (rows, rows), 0) > lax.broadcasted_iota(jnp.int32, (rows, rows), 1)
    position = jnp.sum(jnp.where(same & earlier, 1.0, 0.0), axis=1, keepdims=True)
    slot = lax.broadcasted_iota(jnp.int32, (rows, places_n), 1).astype(F32)
    lookup = (slot == position).astype(F32).astype(BF)
    entry = heads_ref[...].astype(F32) + dot_nn(lookup, tab_ref[...].astype(BF))
    low = entry.astype(BF)
    allowed = jnp.concatenate([same, same], axis=0)
    wait_all(ca)
    proj = dot_nn(low, wqkv[...])
    qkv[:, : 2 * width] = proj[:, : 2 * width].astype(BF)
    qkv[:, 2 * width :] = (proj[:, 2 * width :] + vec[BIAS_V : BIAS_V + 1, :]).astype(BF)
    for p in range(width // 128):
        q = qkv[:, p * 128 : (p + 1) * 128]
        k = qkv[:, width + p * 128 : width + (p + 1) * 128]
        v = qkv[:, 2 * width + p * 128 : 2 * width + (p + 1) * 128]
        weights, out = pair_forward(q, k, v, allowed)
        a_ref[p] = weights
        o_s[:, p * 128 : (p + 1) * 128] = out
    wait_all(co)
    o = o_s[...]
    n1, r1 = norm_rows(entry + dot_nn(o, wout[...]) + vec[BIAS_O : BIAS_O + 1, :])
    h = n1 * vec[GAIN1 : GAIN1 + 1, :] + vec[SHIFT1 : SHIFT1 + 1, :]
    hb = h.astype(BF)
    wait_all(ups)
    wait_all(downs)
    n2, r2 = few_feed_forward(hb, h, vec, upb, wup, wdown, g_ref, gp_ref, ff)
    out_ref[...] = n2 * vec[GAIN2 : GAIN2 + 1, :] + vec[SHIFT2 : SHIFT2 + 1, :]
    dy = grad_ref[...].astype(F32)
    outs = (gup_ref, gdown_ref, gout_ref, sums_ref, upsum_ref)
    dz1, do = few_feed_backward(dy, n2, r2, n1, r1, hb, o, vec, wup, wdown, wout, g_ref, gp_ref, me, chunk, ff, outs)
    do = do.astype(BF)
    for p in range(width // 128):
        q = qkv[:, p * 128 : (p + 1) * 128]
        k = qkv[:, width + p * 128 : width + (p + 1) * 128]
        v = qkv[:, 2 * width + p * 128 : 2 * width + (p + 1) * 128]
        d_q, d_k, d_v = pair_backward(q, k, v, a_ref[p], do[:, p * 128 : (p + 1) * 128])
        d_s[:, p * 128 : (p + 1) * 128] = d_q
        d_s[:, width + p * 128 : width + (p + 1) * 128] = d_k
        d_s[:, 2 * width + p * 128 : 2 * width + (p + 1) * 128] = d_v
    d_all = d_s[...]
    gqkv_ref[...] = dot_tn(own_cols(low, me * chunk, chunk), d_all).astype(BF)
    d_in = dz1 + dot_nt(d_all, wqkv[...])
    dx_ref[...] = d_in
    high = d_in.astype(BF)
    rest = (d_in - high.astype(F32)).astype(BF)
    gtab = dot_tn(lookup, high) + dot_tn(lookup, rest)
    pick = one_hot(width, chunk, me * chunk)
    gtab_ref[...] = dot_nn(gtab.astype(BF), pick)
    dv = jnp.broadcast_to(col_sum(d_all[:, 2 * width :]), (8, width)).astype(BF)
    row = lax.broadcasted_iota(jnp.int32, (8, chunk), 0)
    sums_ref[...] += jnp.where(row == 2, dot_nn(dv, pick), 0.0)


def cross_call(origin, table, heads, grad, docs, tab, vec, upb, pa, pb, ff, chunk):
    rows, width = heads.shape
    na, nb = len(pa.arrays), len(pb.arrays)
    group = ff // width
    pairs = width // 128
    full = pl.BlockSpec(memory_space=pltpu.VMEM)
    return pl.pallas_call(
        partial(cross_kernel, pa, pb, width, ff, chunk, tab.shape[0]),
        in_specs=[SMEM, SMEM] + [full] * 7 + [ANY] * (na + nb),
        out_specs=[full] * 9,
        out_shape=[
            jax.ShapeDtypeStruct((rows, width), F32),
            jax.ShapeDtypeStruct((rows, width), F32),
            jax.ShapeDtypeStruct((chunk, 3 * width), BF),
            jax.ShapeDtypeStruct((chunk, width), BF),
            jax.ShapeDtypeStruct((chunk, ff), BF),
            jax.ShapeDtypeStruct((group * chunk, width), BF),
            jax.ShapeDtypeStruct((8, chunk), F32),
            jax.ShapeDtypeStruct((8, group * chunk), F32),
            jax.ShapeDtypeStruct((tab.shape[0], chunk), F32),
        ],
        scratch_shapes=[
            pltpu.VMEM((width, 3 * width), BF),
            pltpu.VMEM((width, width), BF),
            pltpu.VMEM((width, ff), BF),
            pltpu.VMEM((ff, width), BF),
            pltpu.VMEM((rows, 3 * width), BF),
            pltpu.VMEM((pairs, 2 * rows, rows), BF),
            pltpu.VMEM((rows, width), BF),
            pltpu.VMEM((rows, 3 * width), BF),
            pltpu.VMEM((rows, ff), BF),
            pltpu.VMEM((rows, ff), BF),
            pltpu.SemaphoreType.DMA((na,)),
            pltpu.SemaphoreType.DMA((na,)),
            pltpu.SemaphoreType.DMA((nb,)),
            pltpu.SemaphoreType.DMA((group, nb)),
        ],
        compiler_params=pltpu.CompilerParams(vmem_limit_bytes=VMEM_LIMIT),
        cost_estimate=cost(16 * rows * width * ff, 20 * width * width),
        name="cross_block",
    )(origin, table, heads, grad, docs.reshape(rows, 1), docs.reshape(1, rows), tab, vec, upb, *pa.arrays, *pb.arrays)


def first_kernel(pa, pb, width, ff, chunk, *refs):
    na, nb = len(pa.arrays), len(pb.arrays)
    origin, table, pay_ref, dy_ref, vec, upb = refs[:6]
    srca = refs[6 : 6 + na]
    srcb = refs[6 + na : 6 + na + nb]
    base_o = 6 + na + nb
    dz1_ref, do_ref, gout_ref, gup_ref, gdown_ref, sums_ref, upsum_ref = refs[base_o : base_o + 7]
    wout, wup, wdown, g_ref, gp_ref, sem_o, sem_up, sem_down = refs[base_o + 7 :]
    me = table[0]
    co = pa.copies(srca, origin, sem_o, 3 * width, width, wout)
    ups, downs = up_down_copies(pb, srcb, origin, sem_up, sem_down, width, ff, wup, wdown)
    start_all(ups)
    start_all(downs)
    start_all(co)
    hb = pay_ref[:, width : 2 * width]
    o = pay_ref[:, 2 * width : 3 * width]
    n1 = pay_ref[:, 3 * width : 4 * width].astype(F32)
    r1 = jnp.sum(pay_ref[:, 4 * width :].astype(F32), axis=1, keepdims=True)
    wait_all(ups)
    wait_all(downs)
    wait_all(co)
    n2, r2 = few_feed_forward(hb, hb.astype(F32), vec, upb, wup, wdown, g_ref, gp_ref, ff)
    outs = (gup_ref, gdown_ref, gout_ref, sums_ref, upsum_ref)
    dz1, do = few_feed_backward(
        dy_ref[...], n2, r2, n1, r1, hb, o, vec, wup, wdown, wout, g_ref, gp_ref, me, chunk, ff, outs
    )
    dz1_ref[...] = dz1
    do_ref[...] = do


def first_call(origin, table, pay, dy, vec, upb, pa, pb, ff, chunk):
    rows, width = dy.shape
    na, nb = len(pa.arrays), len(pb.arrays)
    group = ff // width
    full = pl.BlockSpec(memory_space=pltpu.VMEM)
    return pl.pallas_call(
        partial(first_kernel, pa, pb, width, ff, chunk),
        in_specs=[SMEM, SMEM] + [full] * 4 + [ANY] * (na + nb),
        out_specs=[full] * 7,
        out_shape=[
            jax.ShapeDtypeStruct((rows, width), F32),
            jax.ShapeDtypeStruct((rows, width), F32),
            jax.ShapeDtypeStruct((chunk, width), BF),
            jax.ShapeDtypeStruct((chunk, ff), BF),
            jax.ShapeDtypeStruct((group * chunk, width), BF),
            jax.ShapeDtypeStruct((8, chunk), F32),
            jax.ShapeDtypeStruct((8, group * chunk), F32),
        ],
        scratch_shapes=[
            pltpu.VMEM((width, width), BF),
            pltpu.VMEM((width, ff), BF),
            pltpu.VMEM((ff, width), BF),
            pltpu.VMEM((rows, ff), BF),
            pltpu.VMEM((rows, ff), BF),
            pltpu.SemaphoreType.DMA((na,)),
            pltpu.SemaphoreType.DMA((nb,)),
            pltpu.SemaphoreType.DMA((group, nb)),
        ],
        compiler_params=pltpu.CompilerParams(vmem_limit_bytes=VMEM_LIMIT),
        cost_estimate=cost(14 * rows * width * ff, 15 * width * width),
        name="first_rows",
    )(origin, table, pay, dy, vec, upb, *pa.arrays, *pb.arrays)


class Ring:
    def __init__(self, shards):
        chips = shards // 2
        self.shards, self.chips = shards, chips
        self.order = list(range(0, chips, 2)) + list(range(chips - 1, 0, -2))
        self.place = {chip: i for i, chip in enumerate(self.order)}

    def shift(self, by):
        pairs = []
        for i, chip in enumerate(self.order):
            to = self.order[(i + by) % self.chips]
            pairs += [(2 * chip, 2 * to), (2 * chip + 1, 2 * to + 1)]
        return pairs

    def forward(self, x):
        return lax.ppermute(x, "shard", self.shift(1))

    def backward(self, x):
        return lax.ppermute(x, "shard", self.shift(-1))

    def sibling(self, x):
        return lax.ppermute(x, "shard", [(i, i ^ 1) for i in range(self.shards)])

    def origin_table(self):
        rows = []
        for d in range(self.shards):
            chip, core = d // 2, d % 2
            row = []
            for k in range(self.chips):
                other = self.order[(self.place[chip] - k) % self.chips]
                row += [2 * other + core, 2 * other + 1 - core]
            rows.append(row)
        return rows

    def slot_table(self):
        rows = []
        for d in range(self.shards):
            chip = d // 2
            rows.append([(self.place[q] - self.place[chip]) % self.chips for q in range(self.chips)] + [d % 2])
        return rows

    def gather(self, x):
        rows = x.shape[0]
        half = (rows // 32) * 16 or rows
        entries = [(x, 0, 0), (self.sibling(x), 1, 0)]
        ahead, behind = x, x
        for step in range(1, self.chips // 2):
            ahead, behind = self.forward(ahead), self.backward(behind)
            entries += [(ahead, 2 * step, 0), (self.sibling(ahead), 2 * step + 1, 0)]
            back = self.chips - step
            entries += [(behind, 2 * back, 0), (self.sibling(behind), 2 * back + 1, 0)]
        far = self.chips // 2
        last_a = self.forward(ahead[:half])
        entries += [(last_a, 2 * far, 0), (self.sibling(last_a), 2 * far + 1, 0)]
        if half < rows:
            last_b = self.backward(behind[half:])
            entries += [(last_b, 2 * far, half), (self.sibling(last_b), 2 * far + 1, half)]
        return Pieces(entries, rows)

    def reduce(self, own, other):
        mine = self.sibling(other)

        def local(k):
            return own[k % self.chips] + mine[k % self.chips]

        far = self.chips // 2
        half = (own.shape[1] // 32) * 16 or own.shape[1]
        start = local(far)
        ahead = self.forward(start[:half])
        behind = self.backward(start[half:]) if half < own.shape[1] else None
        edge = local(far - 1)
        ahead = jnp.concatenate([ahead + edge[:half], edge[half:]], axis=0) if behind is not None else ahead + edge
        edge = local(-(far - 1))
        behind = jnp.concatenate([edge[:half], behind + edge[half:]], axis=0) if behind is not None else edge
        for step in range(far - 1, 1, -1):
            ahead = self.forward(ahead) + local(step - 1)
            behind = self.backward(behind) + local(-(step - 1))
        return local(0) + self.forward(ahead) + self.backward(behind)


def swap_seq(x):
    return lax.ppermute(x, "seq", [(0, 1), (1, 0)])


def over_seq(x):
    low = x.astype(BF)
    return low.astype(F32) + swap_seq(low).astype(F32)


def sum_everywhere(x, shards):
    low = x.astype(BF)
    bit = 1
    while bit < shards:
        low = low + lax.ppermute(low, "shard", [(i, i ^ bit) for i in range(shards)])
        bit *= 2
    return low.astype(F32) + swap_seq(low).astype(F32)


def pack(qkv, out, up, down):
    chunk = qkv.shape[0]
    parts = [down[j * chunk : (j + 1) * chunk] for j in range(down.shape[0] // chunk)]
    return jnp.concatenate([qkv, out], axis=1), jnp.concatenate([up] + parts, axis=1)


def body(
    tokens,
    qkv_weight,
    out_weight,
    up_weight,
    down_weight,
    norm_gains,
    biases,
    up_bias,
    position_table,
    segment_docs,
    cotangent,
):
    shards = lax.axis_size("shard")
    me = lax.axis_index("shard")
    rows, width = tokens.shape
    segs = rows // SEG
    ff = up_weight.shape[2]
    group = ff // width
    own = width // shards
    docs = segment_docs[0]
    ringed = own % 16 == 0
    ring = Ring(shards)

    def vec_rows(b):
        return [norm_gains[b], biases[b], jnp.zeros((VEC_ROWS - 7, own), BF)]

    small = jnp.concatenate(vec_rows(0) + vec_rows(1) + [position_table], axis=0)
    packs = [pack(qkv_weight[b], out_weight[b], up_weight[b], down_weight[b]) for b in range(2)]
    small_all = lax.all_gather(small, "shard", axis=1, tiled=True).astype(F32)
    upb_all = lax.all_gather(up_bias, "shard", axis=1, tiled=True).astype(F32)
    if ringed:
        chips, cores, chunk = ring.chips, 2, own
        origin = jnp.asarray(ring.origin_table(), jnp.int32)[me]
        table = jnp.concatenate([jnp.asarray(ring.slot_table(), jnp.int32)[me], (me * segs)[None]])
        pieces = [[ring.gather(x) for x in packs[b]] for b in range(2)]
    else:
        chips, cores, chunk = 1, 1, width
        origin = jnp.zeros((1,), jnp.int32)
        table = jnp.stack([jnp.int32(0), jnp.int32(0), me * segs])
        pieces = []
        for b in range(2):
            full = [lax.all_gather(w[b], "shard", axis=0, tiled=True) for w in (qkv_weight, out_weight, up_weight, down_weight)]
            pieces.append([Pieces([(x, 0, 0)], width) for x in pack(*full)])
    place = me[None]
    vec0, vec1, tab = small_all[:VEC_ROWS], small_all[VEC_ROWS : 2 * VEC_ROWS], small_all[2 * VEC_ROWS :]

    qkv, a, o, h, hb, n1, r1 = attention_call(origin, tokens, vec0, pieces[0][0])
    y, g, gp, dz, pay, sums2 = feed_call(origin, h, cotangent, o, n1, r1, vec0, upb_all[:1], pieces[0][1], ff)

    grad_first = cotangent.reshape(segs, SEG, width)[:, 0, :]
    pay = jnp.concatenate([pay.reshape(segs, -1).astype(BF), grad_first], axis=1)
    pay_all = lax.all_gather(pay, "shard", axis=0, tiled=True)
    heads = pay_all[:, :width]
    grad_heads = pay_all[:, 4 * width + 128 :]
    cross_out, d_cross, cq, co, cu, cd, c_sums, c_up, c_tab = cross_call(
        origin, place, heads, grad_heads, docs, tab, vec1, upb_all[1:], pieces[1][0], pieces[1][1], ff, own
    )
    own_rows = lax.dynamic_slice_in_dim(cross_out, me * segs, segs, 0)
    merged = y.reshape(segs, SEG, width).at[:, 0, :].set(own_rows.astype(BF)).reshape(rows, width)

    dm, du, dz1, db, do, sums1, up_sums = feed_back_call(origin, dz, gp, n1, r1, vec0, pieces[0][1], pieces[0][0])
    main = grads_call(table, g, dm, du, hb, o, db, chips, cores, chunk)

    dz1_first, do_first, fo, fu, fd, f_sums, f_up = first_call(
        origin, place, pay_all[:, : 4 * width + 128], d_cross, vec0, upb_all[:1], pieces[0][0], pieces[0][1], ff, own
    )
    d_tokens, sums_v, *tail = attention_back_call(
        origin, table, qkv, a, do, dz1, tokens, do_first, dz1_first, pieces[0][0], chips, cores, chunk
    )

    if ringed:
        main_own = ring.reduce(*main)
        tail_own = ring.reduce(*tail)
        main_up, main_out = main_own[:, :ff], main_own[:, 2 * ff :]
        main_down = jnp.concatenate([main_own[:, ff + j * width : ff + (j + 1) * width] for j in range(group)], axis=0)
    else:
        full = main[0][0]
        down_full = jnp.concatenate([full[:, ff + j * width : ff + (j + 1) * width] for j in range(group)], axis=0)
        main_up = lax.psum_scatter(full[:, :ff], "shard", scatter_dimension=0, tiled=True)
        main_out = lax.psum_scatter(full[:, 2 * ff :], "shard", scatter_dimension=0, tiled=True)
        main_down = lax.psum_scatter(down_full, "shard", scatter_dimension=0, tiled=True)
        tail_own = lax.psum_scatter(tail[0][0], "shard", scatter_dimension=0, tiled=True)
    main_up = main_up.astype(F32) + fu.astype(F32)
    main_out = main_out.astype(F32) + fo.astype(F32)
    main_down = main_down.astype(F32) + fd.astype(F32)

    vec_sums = jnp.concatenate(
        [sums1[0:1], sums2[0:1], sums_v[0:1], sums1[2:3], sums2[2:3], sums1[1:2], sums2[1:2], jnp.zeros((1, width), F32)]
        + [up_sums[0].reshape(group, width), jnp.zeros((4, width), F32)],
        axis=0,
    )
    vec_all = sum_everywhere(vec_sums, shards)
    seg_vec = lax.dynamic_slice_in_dim(vec_all[:8], me * own, own, 1)
    seg_up = lax.dynamic_slice_in_dim(vec_all[8 : 8 + group].reshape(ff), me * own * group, own * group, 0)
    few_vec = over_seq(jnp.concatenate([f_sums, c_sums, c_tab], axis=0))
    few_up = over_seq(jnp.concatenate([f_up, c_up], axis=0))
    seg_vec = seg_vec + few_vec[:8]
    cross_vec = few_vec[8:16]
    grad_up_bias = jnp.stack([seg_up + few_up[0], few_up[8]])
    return (
        merged,
        d_tokens,
        jnp.stack([over_seq(tail_own), over_seq(cq)]),
        jnp.stack([over_seq(main_out), over_seq(co)]),
        jnp.stack([over_seq(main_up), over_seq(cu)]),
        jnp.stack([over_seq(main_down), over_seq(cd)]),
        jnp.stack([seg_vec[:2], cross_vec[:2]]),
        jnp.stack([seg_vec[2:7], cross_vec[2:7]]),
        grad_up_bias,
        few_vec[16:],
    )


def solution(mesh):
    in_specs = (
        P(("seq", "shard"), None),
        P(None, "shard", None),
        P(None, "shard", None),
        P(None, "shard", None),
        P(None, "shard", None),
        P(None, None, "shard"),
        P(None, None, "shard"),
        P(None, "shard"),
        P(None, "shard"),
        P("seq", None),
        P(("seq", "shard"), None),
    )
    out_specs = (
        P(("seq", "shard"), None),
        P(("seq", "shard"), None),
        P(None, "shard", None),
        P(None, "shard", None),
        P(None, "shard", None),
        P(None, "shard", None),
        P(None, None, "shard"),
        P(None, None, "shard"),
        P(None, "shard"),
        P(None, "shard"),
    )
    return jax.shard_map(body, mesh=mesh, in_specs=in_specs, out_specs=out_specs, check_vma=False)
```

```python
from functools import partial

import jax
import jax.numpy as jnp
from jax import lax
from jax.experimental import pallas as pl
from jax.experimental.pallas import tpu as pltpu
from jax.sharding import PartitionSpec as P

HEAD = 64
SEG = 128
EPSILON = 1e-05
MASKED = -1e30
BF = jnp.bfloat16
F32 = jnp.float32
TILE = 256
VMEM_LIMIT = 60 * 1024 * 1024

GAIN1, GAIN2, BIAS_V, BIAS_O, BIAS_D, SHIFT1, SHIFT2, UP0 = 0, 1, 2, 3, 4, 5, 6, 7
VEC_ROWS = 16


def dot_nn(a, b):
    return lax.dot_general(a, b, (((1,), (0,)), ((), ())), preferred_element_type=F32)


def dot_nt(a, b):
    return lax.dot_general(a, b, (((1,), (1,)), ((), ())), preferred_element_type=F32)


def dot_tn(a, b):
    return lax.dot_general(a, b, (((0,), (0,)), ((), ())), preferred_element_type=F32)


def row_mean(x):
    return jnp.mean(x, axis=-1, keepdims=True)


def col_sum(x):
    return jnp.sum(x.astype(F32), axis=0, keepdims=True)


def norm_rows(z):
    centred = z - row_mean(z)
    inverse = lax.rsqrt(row_mean(centred * centred) + EPSILON)
    return centred * inverse, inverse


def norm_back(scaled, normed, inverse):
    return inverse * (scaled - row_mean(scaled) - normed * row_mean(scaled * normed))


def gelu_both(u):
    phi = 0.5 + 0.5 * lax.erf(u * (2.0**-0.5))
    return u * phi, phi + u * jnp.exp(-0.5 * u * u) * 0.3989422804014327


def halves(pair):
    lane = lax.broadcasted_iota(jnp.int32, pair.shape, 1)
    zero = jnp.zeros_like(pair)
    return jnp.concatenate([jnp.where(lane < HEAD, pair, zero), jnp.where(lane < HEAD, zero, pair)], axis=0)


def side_by_side(stacked):
    rows = stacked.shape[0] // 2
    return jnp.concatenate([stacked[:rows], stacked[rows:]], axis=1)


def pairs_forward(q, k, v, allowed):
    scores = [dot_nt(halves(a), b) * (HEAD**-0.5) for a, b in zip(q, k)]
    if allowed is not None:
        scores = [jnp.where(allowed, x, MASKED) for x in scores]
    powers = [jnp.exp(x - jnp.max(x, axis=-1, keepdims=True)) for x in scores]
    weights = [(x / jnp.sum(x, axis=-1, keepdims=True)).astype(BF) for x in powers]
    return [(w, dot_nn(side_by_side(w), halves(x)).astype(BF)) for w, x in zip(weights, v)]


def pairs_backward(q, k, v, weights, d_out):
    d_stacks = [halves(x) for x in d_out]
    d_weights = [dot_nt(x, y) for x, y in zip(d_stacks, v)]
    wide = [w.astype(F32) for w in weights]
    inner = [jnp.sum(w * x, axis=-1, keepdims=True) for w, x in zip(wide, d_weights)]
    d_scores = [(w * (x - y)).astype(BF) for w, x, y in zip(wide, d_weights, inner)]
    scale = HEAD**-0.5
    d_q = [(dot_nn(side_by_side(x), halves(y)) * scale).astype(BF) for x, y in zip(d_scores, k)]
    d_k = [(dot_tn(x, halves(y)) * scale).astype(BF) for x, y in zip(d_scores, q)]
    d_v = [dot_tn(w, x).astype(BF) for w, x in zip(weights, d_stacks)]
    return zip(d_q, d_k, d_v)


class Copies:
    def __init__(self, copies):
        self.all = copies

    def start(self):
        start_all(self.all)

    def wait(self):
        wait_all(self.all)


class Pieces:
    def __init__(self, entries, chunk, origins):
        self.entries = list(entries)
        self.chunk, self.origins = chunk, origins
        self.rows = chunk * origins
        self.count = len(self.entries)
        self.arrays, self.which = [], []
        for x, *_ in self.entries:
            at = [i for i, y in enumerate(self.arrays) if y is x]
            if not at:
                self.arrays.append(x)
            self.which.append(at[0] if at else len(self.arrays) - 1)

    def copies(self, refs, origin, sems, col, width, dst, by_origin=False, blocks=1):
        def build(refs, entries, sem0):
            out = []
            for n, (ref, (x, entry, first, top, rows)) in enumerate(zip(refs, entries)):
                for j in range(blocks):
                    if by_origin:
                        to = dst.at[origin[entry], pl.ds(first, rows), :]
                    else:
                        start = (origin[entry] * blocks + j) * self.chunk + first
                        to = dst.at[pl.ds(pl.multiple_of(start, 16 if rows % 16 == 0 else 8), rows), :]
                    source = ref.at[pl.ds(top, rows), pl.ds(col + j * width, width)]
                    out.append(pltpu.make_async_copy(source, to, sems.at[(sem0 + n) * blocks + j]))
            return out

        return Copies(build([refs[i] for i in self.which], self.entries, 0))


class Loader:
    def __init__(self, *items):
        self.items = [(*item, 1)[:4] for item in items]
        self.groups = []
        for pieces, *_ in items:
            if pieces not in self.groups:
                self.groups.append(pieces)
        self.arrays = [x for g in self.groups for x in g.arrays]
        self.count = len(self.arrays)

    def scratch(self):
        buffers = [pltpu.VMEM((p.rows * blocks, width), BF) for p, _, width, blocks in self.items]
        return buffers + [pltpu.SemaphoreType.DMA((p.count * blocks,)) for p, _, _, blocks in self.items]

    def start(self, srcs, origin, scratch):
        at, where = 0, {}
        for g in self.groups:
            where[id(g)] = srcs[at : at + len(g.arrays)]
            at += len(g.arrays)
        m = len(self.items)
        sets = [
            p.copies(where[id(p)], origin, scratch[m + i], col, width, scratch[i], blocks=blocks)
            for i, (p, col, width, blocks) in enumerate(self.items)
        ]
        for copies in sets:
            copies.start()
        return [copies.wait for copies in sets]


def start_all(copies):
    for c in copies:
        c.start()


def wait_all(copies):
    for c in copies:
        c.wait()


ANY = pl.BlockSpec(memory_space=pl.ANY)
SMEM = pl.BlockSpec(memory_space=pltpu.SMEM)


def whole(shape):
    return pl.BlockSpec(shape, lambda *i: (0,) * len(shape), pipeline_mode=pl.Buffered(1))


def whole_out(shape):
    return pl.BlockSpec(shape, lambda *i: (0,) * len(shape))


def tile(*shape):
    return pl.BlockSpec(shape, lambda i: (i,) + (0,) * (len(shape) - 1))


def cost(flops, nbytes):
    return pl.CostEstimate(flops=int(flops * 0.01), bytes_accessed=int(nbytes * 0.01), transcendentals=0)


def project_kernel(load, width, *refs):
    n = load.count
    origin, x_ref, vec = refs[0], refs[1], refs[2]
    srcs = refs[3 : 3 + n]
    qkv_ref = refs[3 + n]
    scratch = refs[4 + n :]
    wqkv = scratch[0]

    @pl.when(pl.program_id(0) == 0)
    def _():
        for wait in load.start(srcs, origin, scratch):
            wait()

    qkv = dot_nn(x_ref[...], wqkv[...])
    qkv_ref[:, : 2 * width] = qkv[:, : 2 * width].astype(BF)
    qkv_ref[:, 2 * width :] = (qkv[:, 2 * width :] + vec[BIAS_V : BIAS_V + 1, :]).astype(BF)


def project_call(origin, x, vec, load):
    rows, width = x.shape
    return pl.pallas_call(
        partial(project_kernel, load, width),
        grid=(rows // TILE,),
        in_specs=[SMEM, tile(TILE, width), whole(vec.shape)] + [ANY] * load.count,
        out_specs=tile(TILE, 3 * width),
        out_shape=jax.ShapeDtypeStruct((rows, 3 * width), BF),
        scratch_shapes=load.scratch(),
        compiler_params=pltpu.CompilerParams(vmem_limit_bytes=VMEM_LIMIT),
        cost_estimate=cost(2 * rows * width * 3 * width, 10 * rows * width),
        name="segment_project",
    )(origin, x, vec, *load.arrays)


def attention_kernel(load, width, *refs):
    n = load.count
    origin, x_ref, qkv_ref, vec = refs[:4]
    srcs = refs[4 : 4 + n]
    a_ref, o_ref, h_ref, hb_ref, n_ref, r_ref = refs[4 + n : 10 + n]
    scratch = refs[10 + n :]
    wout = scratch[0]

    @pl.when(pl.program_id(0) == 0)
    def _():
        for wait in load.start(srcs, origin, scratch):
            wait()

    for s in range(TILE // SEG):
        rows = pl.ds(s * SEG, SEG)
        pairs = range(width // 128)
        q = [qkv_ref[rows, pl.ds(p * 128, 128)] for p in pairs]
        k = [qkv_ref[rows, pl.ds(width + p * 128, 128)] for p in pairs]
        v = [qkv_ref[rows, pl.ds(2 * width + p * 128, 128)] for p in pairs]
        for p, (weights, out) in enumerate(pairs_forward(q, k, v, None)):
            a_ref[s, p] = weights
            o_ref[rows, pl.ds(p * 128, 128)] = out
    z = x_ref[...].astype(F32) + dot_nn(o_ref[...], wout[...]) + vec[BIAS_O : BIAS_O + 1, :]
    normed, inverse = norm_rows(z)
    h = normed * vec[GAIN1 : GAIN1 + 1, :] + vec[SHIFT1 : SHIFT1 + 1, :]
    h_ref[...] = h
    hb_ref[...] = h.astype(BF)
    n_ref[...] = normed.astype(BF)
    r_ref[...] = inverse


def attention_call(origin, x, qkv, vec, load):
    rows, width = x.shape
    n = load.count
    segs = rows // SEG
    pairs = width // 128
    return pl.pallas_call(
        partial(attention_kernel, load, width),
        grid=(rows // TILE,),
        in_specs=[SMEM, tile(TILE, width), tile(TILE, 3 * width), whole(vec.shape)] + [ANY] * n,
        out_specs=[
            tile(TILE // SEG, pairs, 2 * SEG, SEG),
            tile(TILE, width),
            tile(TILE, width),
            tile(TILE, width),
            tile(TILE, width),
            tile(TILE, 1),
        ],
        out_shape=[
            jax.ShapeDtypeStruct((segs, pairs, 2 * SEG, SEG), BF),
            jax.ShapeDtypeStruct((rows, width), BF),
            jax.ShapeDtypeStruct((rows, width), F32),
            jax.ShapeDtypeStruct((rows, width), BF),
            jax.ShapeDtypeStruct((rows, width), BF),
            jax.ShapeDtypeStruct((rows, 1), F32),
        ],
        scratch_shapes=load.scratch(),
        compiler_params=pltpu.CompilerParams(vmem_limit_bytes=VMEM_LIMIT),
        cost_estimate=cost(2 * rows * width * 2 * width, 16 * rows * width),
        name="segment_attention",
    )(origin, x, qkv, vec, *load.arrays)


def feed_kernel(load, width, ff, *refs):
    n = load.count
    origin, h_ref, c_ref, o_ref, n_ref, r_ref, vec, upb = refs[:8]
    srcs = refs[8 : 8 + n]
    y_ref, g_ref, gp_ref, dz_ref, dm_ref, pay_ref, sums_ref = refs[8 + n : 15 + n]
    scratch = refs[15 + n :]
    wup, wdown = scratch[:2]

    @pl.when(pl.program_id(0) == 0)
    def _():
        for wait in load.start(srcs, origin, scratch):
            wait()
        sums_ref[...] = jnp.zeros_like(sums_ref)

    h = h_ref[...]
    hb = h.astype(BF)
    block = 512
    total = jnp.zeros((TILE, width), F32)
    u = dot_nn(hb, wup[:, :block]) + upb[0:1, :block]
    for j in range(ff // block):
        cols = slice(j * block, (j + 1) * block)
        if (j + 1) * block < ff:
            later = slice((j + 1) * block, (j + 2) * block)
            u_next = dot_nn(hb, wup[:, later]) + upb[0:1, later]
        active, slope = gelu_both(u)
        active = active.astype(BF)
        g_ref[:, cols] = active
        gp_ref[:, cols] = slope.astype(BF)
        total = total + dot_nn(active, wdown[cols, :])
        u = u_next
    normed, inverse = norm_rows(h + total + vec[BIAS_D : BIAS_D + 1, :])
    gain = vec[GAIN2 : GAIN2 + 1, :]
    y = normed * gain + vec[SHIFT2 : SHIFT2 + 1, :]
    y_ref[...] = y.astype(BF)
    row = lax.broadcasted_iota(jnp.int32, (TILE, 1), 0)
    dy = jnp.where(row % SEG == 0, 0.0, c_ref[...].astype(F32))
    dz = norm_back(dy * gain, normed, inverse)
    dz_ref[...] = dz
    dm = dz.astype(BF)
    dm_ref[...] = dm
    sums_ref[0:1, :] += col_sum(dy * normed)
    sums_ref[1:2, :] += col_sum(dy)
    sums_ref[2:3, :] += col_sum(dm)
    for i in range(pay_ref.shape[0] // (TILE // SEG)):

        @pl.when(pl.program_id(0) == i)
        def _(i=i):
            for s in range(TILE // SEG):
                here = slice(s * SEG, s * SEG + 1)
                few = slice(s * SEG, s * SEG + 16)
                at = slice(i * (TILE // SEG) + s, i * (TILE // SEG) + s + 1)
                pay_ref[at, 0:width] = y[here].astype(BF).astype(F32)
                pay_ref[at, width : 2 * width] = c_ref[few, :].astype(F32)[:1]
                pay_ref[at, 2 * width : 3 * width] = h[here].astype(BF).astype(F32)
                pay_ref[at, 3 * width : 4 * width] = o_ref[few, :].astype(F32)[:1]
                pay_ref[at, 4 * width : 5 * width] = n_ref[few, :].astype(F32)[:1]
                pay_ref[at, 5 * width :] = jnp.broadcast_to(r_ref[here], (1, 128))


def feed_call(origin, h, cot, o, n1, r1, vec, upb, load, ff):
    rows, width = h.shape
    n = load.count
    pay = 5 * width + 128
    return pl.pallas_call(
        partial(feed_kernel, load, width, ff),
        grid=(rows // TILE,),
        in_specs=[
            SMEM,
            tile(TILE, width),
            tile(TILE, width),
            tile(TILE, width),
            tile(TILE, width),
            tile(TILE, 1),
            whole(vec.shape),
            whole(upb.shape),
        ]
        + [ANY] * n,
        out_specs=[
            tile(TILE, width),
            tile(TILE, ff),
            tile(TILE, ff),
            tile(TILE, width),
            tile(TILE, width),
            whole_out((rows // SEG, pay)),
            whole_out((8, width)),
        ],
        out_shape=[
            jax.ShapeDtypeStruct((rows, width), BF),
            jax.ShapeDtypeStruct((rows, ff), BF),
            jax.ShapeDtypeStruct((rows, ff), BF),
            jax.ShapeDtypeStruct((rows, width), F32),
            jax.ShapeDtypeStruct((rows, width), BF),
            jax.ShapeDtypeStruct((rows // SEG, pay), F32),
            jax.ShapeDtypeStruct((8, width), F32),
        ],
        scratch_shapes=load.scratch(),
        compiler_params=pltpu.CompilerParams(vmem_limit_bytes=VMEM_LIMIT),
        cost_estimate=cost(4 * rows * width * ff, 4 * rows * ff),
        name="segment_feed",
    )(origin, h, cot, o, n1, r1, vec, upb, *load.arrays)


def feed_back_kernel(load, width, ff, *refs):
    n = load.count
    origin, dz_ref, gp_ref, n_ref, r_ref, vec = refs[:6]
    srcs = refs[6 : 6 + n]
    du_ref, dz1_ref, db_ref, do_ref, sums_ref, upsum_ref = refs[6 + n : 12 + n]
    scratch = refs[12 + n :]
    wdown, wup, wout = scratch[:3]

    @pl.when(pl.program_id(0) == 0)
    def _():
        for wait in load.start(srcs, origin, scratch):
            wait()
        sums_ref[...] = jnp.zeros_like(sums_ref)
        upsum_ref[...] = jnp.zeros_like(upsum_ref)

    dz = dz_ref[...]
    dm = dz.astype(BF)
    block = 512
    total = dz
    dg = dot_nt(dm, wdown[:block, :])
    for j in range(ff // block):
        cols = slice(j * block, (j + 1) * block)
        if (j + 1) * block < ff:
            dg_next = dot_nt(dm, wdown[(j + 1) * block : (j + 2) * block, :])
        du = (dg * gp_ref[:, cols].astype(F32)).astype(BF)
        du_ref[:, cols] = du
        upsum_ref[0:1, cols] += col_sum(du)
        total = total + dot_nt(du, wup[:, cols])
        dg = dg_next
    normed = n_ref[...].astype(F32)
    dz1 = norm_back(total * vec[GAIN1 : GAIN1 + 1, :], normed, r_ref[...])
    dz1_ref[...] = dz1
    db = dz1.astype(BF)
    db_ref[...] = db
    do_ref[...] = dot_nt(db, wout[...]).astype(BF)
    sums_ref[0:1, :] += col_sum(total * normed)
    sums_ref[1:2, :] += col_sum(total)
    sums_ref[2:3, :] += col_sum(db)


def feed_back_call(origin, dz, gp, n1, r1, vec, load):
    rows, width = dz.shape
    ff = gp.shape[1]
    n = load.count
    return pl.pallas_call(
        partial(feed_back_kernel, load, width, ff),
        grid=(rows // TILE,),
        in_specs=[SMEM, tile(TILE, width), tile(TILE, ff), tile(TILE, width), tile(TILE, 1), whole(vec.shape)] + [ANY] * n,
        out_specs=[
            tile(TILE, ff),
            tile(TILE, width),
            tile(TILE, width),
            tile(TILE, width),
            whole_out((8, width)),
            whole_out((8, ff)),
        ],
        out_shape=[
            jax.ShapeDtypeStruct((rows, ff), BF),
            jax.ShapeDtypeStruct((rows, width), F32),
            jax.ShapeDtypeStruct((rows, width), BF),
            jax.ShapeDtypeStruct((rows, width), BF),
            jax.ShapeDtypeStruct((8, width), F32),
            jax.ShapeDtypeStruct((8, ff), F32),
        ],
        scratch_shapes=load.scratch(),
        compiler_params=pltpu.CompilerParams(vmem_limit_bytes=VMEM_LIMIT),
        cost_estimate=cost(4 * rows * width * ff + 2 * rows * width * width, 4 * rows * ff),
        name="segment_feed_back",
    )(origin, dz, gp, n1, r1, vec, *load.arrays)


def spread(table, chips, cores, chunk, first_chip, count, source, outs, put):
    core = table[chips]
    for q in range(count):
        slot = table[first_chip + q]
        for c in range(cores):
            device = q * cores + (jnp.bitwise_xor(core, c) if cores > 1 else 0)
            start = pl.multiple_of(device * chunk, 16)
            put(outs[c], slot, source[pl.ds(start, chunk), :].astype(BF))


def grads_down_kernel(chips, cores, chunk, width, *refs):
    table, g_ref, dm_ref = refs[:3]
    outs = refs[3 : 3 + cores]
    scratch = refs[3 + cores]
    step = pl.program_id(0)
    scratch[...] = dot_tn(g_ref[...], dm_ref[...])
    if chips > 1:
        group = outs[0].shape[2] // width
        per = width // (chunk * group * cores)
        core = table[chips]
        for q in range(per):
            slot = table[step * per + q]
            for c in range(cores):
                device = q * cores + jnp.bitwise_xor(core, c)
                for j in range(group):
                    start = pl.multiple_of((device * group + j) * chunk, 16)
                    outs[c][slot, :, j * width : (j + 1) * width] = scratch[pl.ds(start, chunk), :].astype(BF)
    else:
        outs[0][0, :, pl.ds(pl.multiple_of(step * width, width), width)] = scratch[...].astype(BF)


def once(shape):
    return pl.BlockSpec(shape, lambda i: (0,) * len(shape), pipeline_mode=pl.Buffered(1))


def grads_down_call(table, g, dm, chips, cores, chunk):
    rows, ff = g.shape
    width = dm.shape[1]
    return pl.pallas_call(
        partial(grads_down_kernel, chips, cores, chunk, width),
        grid=(ff // width,),
        in_specs=[SMEM, pl.BlockSpec((rows, width), lambda i: (0, i)), whole((rows, width))],
        out_specs=[once((chips, chunk, ff))] * cores,
        out_shape=[jax.ShapeDtypeStruct((chips, chunk, ff), BF)] * cores,
        scratch_shapes=[pltpu.VMEM((width, width), F32)],
        compiler_params=pltpu.CompilerParams(vmem_limit_bytes=VMEM_LIMIT),
        cost_estimate=cost(2 * rows * width * ff, 2 * rows * ff + 2 * width * ff),
        name="grads_down",
    )(table, g, dm)


def grads_up_kernel(chips, cores, chunk, width, *refs):
    table, du_ref, hb_ref, o_ref, db_ref = refs[:5]
    outs = refs[5 : 5 + cores]
    scratch = refs[5 + cores]
    step = pl.program_id(0)
    last = pl.num_programs(0) - 1

    @pl.when(step < last)
    def _():
        scratch[...] = dot_tn(hb_ref[...], du_ref[...])

    @pl.when(step == last)
    def _():
        scratch[...] = dot_tn(o_ref[...], db_ref[...])

    cols = pl.ds(pl.multiple_of(step * width, width), width)

    def put(out, slot, values):
        out[slot, :, cols] = values

    spread(table, chips, cores, chunk, 0, chips, scratch, outs, put)


def grads_up_call(table, du, hb, o, db, chips, cores, chunk):
    rows, ff = du.shape
    width = hb.shape[1]
    group = ff // width
    cols = ff + width
    return pl.pallas_call(
        partial(grads_up_kernel, chips, cores, chunk, width),
        grid=(group + 1,),
        in_specs=[SMEM, pl.BlockSpec((rows, width), lambda i: (0, jnp.minimum(i, group - 1)))] + [whole((rows, width))] * 3,
        out_specs=[once((chips, chunk, cols))] * cores,
        out_shape=[jax.ShapeDtypeStruct((chips, chunk, cols), BF)] * cores,
        scratch_shapes=[pltpu.VMEM((width, width), F32)],
        compiler_params=pltpu.CompilerParams(vmem_limit_bytes=VMEM_LIMIT),
        cost_estimate=cost(2 * rows * width * cols, 2 * rows * ff + 2 * width * cols),
        name="grads_up",
    )(table, du, hb, o, db)


def attention_back_kernel(chips, cores, chunk, width, group, *refs):
    table, qkv_ref, a_ref, do_ref, x_ref, do_first, sums1, sums2, up_sums = refs[:9]
    dqkv, sums_ref = refs[9:11]
    outs = refs[11 : 11 + cores]
    total, d_o = refs[11 + cores :]
    step = pl.program_id(0)

    @pl.when(step == 0)
    def _():
        total[...] = jnp.zeros_like(total)
        sums_ref[...] = jnp.zeros_like(sums_ref)

    d_o[...] = do_ref[...].astype(F32)
    for s in range(TILE // SEG):
        at = pl.ds(table[chips + 1] + step * (TILE // SEG) + s, 1)
        d_o[s * SEG : s * SEG + 1, :] = do_first[at, :]
    for s in range(TILE // SEG):
        rows = pl.ds(s * SEG, SEG)
        pairs = range(width // 128)
        q = [qkv_ref[rows, pl.ds(p * 128, 128)] for p in pairs]
        k = [qkv_ref[rows, pl.ds(width + p * 128, 128)] for p in pairs]
        v = [qkv_ref[rows, pl.ds(2 * width + p * 128, 128)] for p in pairs]
        w = [a_ref[s, p] for p in pairs]
        d_out = [d_o[rows, pl.ds(p * 128, 128)].astype(BF) for p in pairs]
        for p, (d_q, d_k, d_v) in enumerate(pairs_backward(q, k, v, w, d_out)):
            dqkv[rows, pl.ds(p * 128, 128)] = d_q
            dqkv[rows, pl.ds(width + p * 128, 128)] = d_k
            dqkv[rows, pl.ds(2 * width + p * 128, 128)] = d_v
    sums_ref[0:1, :] += col_sum(dqkv[:, 2 * width :])
    total[...] += dot_tn(x_ref[...], dqkv[...])

    @pl.when(step == pl.num_programs(0) - 1)
    def _():
        def put(out, slot, values):
            out[slot, :, : 3 * width] = values

        spread(table, chips, cores, chunk, 0, chips, total, outs, put)
        if cores > 1:
            vec = [sums1[0:1], sums2[0:1], sums_ref[0:1], sums1[2:3], sums2[2:3], sums1[1:2], sums2[1:2]]
            vec = jnp.concatenate(vec + [jnp.zeros((1, width), F32)], axis=0)
            pad = jnp.zeros((chunk - UP0 - group, chunk), F32)
            for q in range(chips):
                blocks = []
                for device in (2 * q, 2 * q + 1):
                    own = slice(device * chunk, (device + 1) * chunk)
                    ups = [up_sums[0:1, group * chunk * device + chunk * j : group * chunk * device + chunk * (j + 1)] for j in range(group)]
                    block = jnp.concatenate([vec[:UP0, own]] + ups + [pad], axis=0)
                    blocks.append(jnp.concatenate([block, jnp.zeros((chunk, 128 - chunk), F32)], axis=1))
                for c in range(2):
                    picked = jnp.where(table[chips] == c, blocks[0], blocks[1]).astype(BF)
                    outs[c][table[q], :, 3 * width :] = picked


def attention_back_call(table, qkv, a, do, x, do_first, sums1, sums2, up_sums, chips, cores, chunk):
    rows, width = x.shape
    pairs = width // 128
    cols = 3 * width + (128 if cores > 1 else 0)
    group = up_sums.shape[1] // width
    return pl.pallas_call(
        partial(attention_back_kernel, chips, cores, chunk, width, group),
        grid=(rows // TILE,),
        in_specs=[
            SMEM,
            tile(TILE, 3 * width),
            tile(TILE // SEG, pairs, 2 * SEG, SEG),
            tile(TILE, width),
            tile(TILE, width),
            whole(do_first.shape),
            whole(sums1.shape),
            whole(sums2.shape),
            whole(up_sums.shape),
        ],
        out_specs=[tile(TILE, 3 * width), whole_out((8, width))] + [once((chips, chunk, cols))] * cores,
        out_shape=[jax.ShapeDtypeStruct((rows, 3 * width), BF), jax.ShapeDtypeStruct((8, width), F32)]
        + [jax.ShapeDtypeStruct((chips, chunk, cols), BF)] * cores,
        scratch_shapes=[pltpu.VMEM((width, 3 * width), F32), pltpu.VMEM((TILE, width), F32)],
        compiler_params=pltpu.CompilerParams(vmem_limit_bytes=VMEM_LIMIT),
        cost_estimate=cost(2 * rows * width * 5 * width, 20 * rows * width),
        name="segment_attention_back",
    )(table, qkv, a, do, x, do_first, sums1, sums2, up_sums)


def input_grad_kernel(load, width, *refs):
    n = load.count
    origin, table, dqkv_ref, dz_ref, dz_first = refs[:5]
    srcs = refs[5 : 5 + n]
    dx_ref, d_z = refs[5 + n : 7 + n]
    scratch = refs[7 + n :]
    step = pl.program_id(0)

    @pl.when(step == 0)
    def _():
        for wait in load.start(srcs, origin, scratch):
            wait()

    d_z[...] = dz_ref[...]
    for s in range(TILE // SEG):
        at = pl.ds(table[0] + step * (TILE // SEG) + s, 1)
        d_z[s * SEG : s * SEG + 1, :] = dz_first[at, :]
    dx_ref[...] = (d_z[...] + dot_nt(dqkv_ref[...], scratch[0][...])).astype(BF)


def input_grad_call(origin, first_row, dqkv, dz, dz_first, load):
    rows, width = dz.shape
    n = load.count
    return pl.pallas_call(
        partial(input_grad_kernel, load, width),
        grid=(rows // TILE,),
        in_specs=[SMEM, SMEM, tile(TILE, 3 * width), tile(TILE, width), whole(dz_first.shape)] + [ANY] * n,
        out_specs=tile(TILE, width),
        out_shape=jax.ShapeDtypeStruct((rows, width), BF),
        scratch_shapes=[pltpu.VMEM((TILE, width), F32)] + load.scratch(),
        compiler_params=pltpu.CompilerParams(vmem_limit_bytes=VMEM_LIMIT),
        cost_estimate=cost(2 * rows * width * 3 * width, 12 * rows * width),
        name="input_grad",
    )(origin, first_row, dqkv, dz, dz_first, *load.arrays)


def one_hot(rows, cols, base):
    r = lax.broadcasted_iota(jnp.int32, (rows, cols), 0)
    c = lax.broadcasted_iota(jnp.int32, (rows, cols), 1)
    return (r == c + base).astype(F32).astype(BF)


def own_cols(values, base, cols):
    return dot_nn(values.astype(BF), one_hot(values.shape[1], cols, base)).astype(BF)


def few_feed_forward(hb, h, vec, up_row, wup, wdown, g_ref, gp_ref, ff):
    block = 512
    total = jnp.zeros(h.shape, F32)
    for j in range(ff // block):
        cols = slice(j * block, (j + 1) * block)
        active, slope = gelu_both(dot_nn(hb, wup[:, cols]) + up_row[:, cols])
        active = active.astype(BF)
        g_ref[:, cols] = active
        gp_ref[:, cols] = slope.astype(BF)
        total = total + dot_nn(active, wdown[cols, :])
    return norm_rows(h + total + vec[BIAS_D : BIAS_D + 1, :])


def few_feed_backward(dy, n2, r2, n1, r1, hb, o, vec, wup, wdown, wout, g_ref, gp_ref, me, chunk, ff, grads):
    block = 512
    group = ff // hb.shape[1]
    base = me * chunk
    dz = norm_back(dy * vec[GAIN2 : GAIN2 + 1, :], n2, r2)
    dm = dz.astype(BF)
    total = dz
    own_h = own_cols(hb, base, chunk)
    own_g = jnp.zeros((hb.shape[0], group * chunk), F32)
    own_up = jnp.zeros((8, group * chunk), F32)
    for j in range(ff // block):
        cols = slice(j * block, (j + 1) * block)
        du = (dot_nt(dm, wdown[cols, :]) * gp_ref[:, cols].astype(F32)).astype(BF)
        total = total + dot_nt(du, wup[:, cols])
        grads[:, ff + j * block : ff + (j + 1) * block] = dot_tn(own_h, du).astype(BF)
        chosen = one_hot(block, group * chunk, base * group - j * block)
        own_g = own_g + dot_nn(g_ref[:, cols], chosen)
        own_up = own_up + dot_nn(jnp.broadcast_to(col_sum(du), (8, block)).astype(BF), chosen)
    down = dot_tn(own_g.astype(BF), dm).astype(BF)
    width = hb.shape[1]
    for j in range(group):
        grads[:, j * width : (j + 1) * width] = down[j * chunk : (j + 1) * chunk]
    dz1 = norm_back(total * vec[GAIN1 : GAIN1 + 1, :], n1, r1)
    db = dz1.astype(BF)
    grads[:, 2 * ff : 2 * ff + width] = dot_tn(own_cols(o, base, chunk), db).astype(BF)
    do = dot_nt(db, wout[...])
    zero = jnp.zeros((1, hb.shape[1]), F32)
    sums = [col_sum(total * n1), col_sum(dy * n2), zero, col_sum(db), col_sum(dm), col_sum(total), col_sum(dy), zero]
    sums = dot_nn(jnp.concatenate(sums, axis=0).astype(BF), one_hot(hb.shape[1], chunk, base))
    ups = [own_up[0:1, j * chunk : (j + 1) * chunk] for j in range(group)]
    sums = jnp.concatenate([sums[:UP0]] + ups + [jnp.zeros((VEC_ROWS - UP0 - group, chunk), F32)], axis=0)
    return dz1, do, sums


def cross_kernel(load, width, ff, chunk, places_n, *refs):
    n = load.count
    origin, table, pay_ref, doc_col, doc_row, tab_ref, vec, upb = refs[:8]
    srcs = refs[8 : 8 + n]
    out_ref, dx_ref, grads, sums_ref, gtab_ref = refs[8 + n : 13 + n]
    qkv, a_ref, o_s, d_s, g_ref, gp_ref = refs[13 + n : 19 + n]
    scratch = refs[19 + n :]
    wqkv, wout, wup, wdown = scratch[:4]
    rows = pay_ref.shape[0]
    me = table[0]
    wait_qkv, wait_out, wait_up, wait_down = load.start(srcs, origin, scratch)
    same = doc_col[...] == doc_row[...]
    earlier = lax.broadcasted_iota(jnp.int32, (rows, rows), 0) > lax.broadcasted_iota(jnp.int32, (rows, rows), 1)
    position = jnp.sum(jnp.where(same & earlier, 1.0, 0.0), axis=1, keepdims=True)
    slot = lax.broadcasted_iota(jnp.int32, (rows, places_n), 1).astype(F32)
    lookup = (slot == position).astype(F32).astype(BF)
    entry = pay_ref[:, :width] + dot_nn(lookup, tab_ref[...].astype(BF))
    low = entry.astype(BF)
    allowed = jnp.concatenate([same, same], axis=0)
    wait_qkv()
    proj = dot_nn(low, wqkv[...])
    qkv[:, : 2 * width] = proj[:, : 2 * width].astype(BF)
    qkv[:, 2 * width :] = (proj[:, 2 * width :] + vec[BIAS_V : BIAS_V + 1, :]).astype(BF)
    pairs = range(width // 128)

    def lanes(ref, p, first=0):
        return ref[:, first + p * 128 : first + (p + 1) * 128]

    together = len(pairs) if rows <= 128 else 1
    for at in range(0, len(pairs), together):
        some = range(at, at + together)
        q = [lanes(qkv, p) for p in some]
        k = [lanes(qkv, p, width) for p in some]
        v = [lanes(qkv, p, 2 * width) for p in some]
        for p, (weights, out) in zip(some, pairs_forward(q, k, v, allowed)):
            a_ref[p] = weights
            o_s[:, p * 128 : (p + 1) * 128] = out
    wait_out()
    o = o_s[...]
    n1, r1 = norm_rows(entry + dot_nn(o, wout[...]) + vec[BIAS_O : BIAS_O + 1, :])
    h = n1 * vec[GAIN1 : GAIN1 + 1, :] + vec[SHIFT1 : SHIFT1 + 1, :]
    hb = h.astype(BF)
    wait_up()
    wait_down()
    n2, r2 = few_feed_forward(hb, h, vec, upb.at[1:2, :], wup, wdown, g_ref, gp_ref, ff)
    out_ref[...] = n2 * vec[GAIN2 : GAIN2 + 1, :] + vec[SHIFT2 : SHIFT2 + 1, :]
    dy = pay_ref[:, width:]
    dz1, do, sums = few_feed_backward(dy, n2, r2, n1, r1, hb, o, vec, wup, wdown, wout, g_ref, gp_ref, me, chunk, ff, grads)
    do = do.astype(BF)
    for at in range(0, len(pairs), together):
        some = range(at, at + together)
        q = [lanes(qkv, p) for p in some]
        k = [lanes(qkv, p, width) for p in some]
        v = [lanes(qkv, p, 2 * width) for p in some]
        w = [a_ref[p] for p in some]
        d_out = [do[:, p * 128 : (p + 1) * 128] for p in some]
        for p, (d_q, d_k, d_v) in zip(some, pairs_backward(q, k, v, w, d_out)):
            d_s[:, p * 128 : (p + 1) * 128] = d_q
            d_s[:, width + p * 128 : width + (p + 1) * 128] = d_k
            d_s[:, 2 * width + p * 128 : 2 * width + (p + 1) * 128] = d_v
    d_all = d_s[...]
    base = 2 * ff + width
    grads[:, base : base + 3 * width] = dot_tn(own_cols(low, me * chunk, chunk), d_all).astype(BF)
    d_in = dz1 + dot_nt(d_all, wqkv[...])
    dx_ref[...] = d_in
    high = d_in.astype(BF)
    rest = (d_in - high.astype(F32)).astype(BF)
    gtab = dot_tn(lookup, high) + dot_tn(lookup, rest)
    pick = one_hot(width, chunk, me * chunk)
    own_tab = dot_nn(gtab.astype(BF), pick)
    dv = jnp.broadcast_to(col_sum(d_all[:, 2 * width :]), (VEC_ROWS, width)).astype(BF)
    row = lax.broadcasted_iota(jnp.int32, (VEC_ROWS, chunk), 0)
    sums = sums + jnp.where(row == BIAS_V, dot_nn(dv, pick), 0.0)
    sums_ref[...] = sums
    gtab_ref[...] = own_tab
    if grads.shape[1] > base + 3 * width:
        high = 2 * VEC_ROWS
        gap = jnp.zeros((chunk, 64 - chunk), F32)
        left = jnp.concatenate([sums, jnp.zeros((VEC_ROWS, chunk), F32), own_tab[: chunk - high]], axis=0)
        grads[:, base + 3 * width :] = jnp.concatenate([left, gap, own_tab[chunk - high :], gap], axis=1).astype(BF)


def cross_call(origin, table, pay, docs, tab, vec, upb, load, ff, chunk, extra):
    rows, width = pay.shape[0], vec.shape[1]
    n = load.count
    group = ff // width
    pairs = width // 128
    full = pl.BlockSpec(memory_space=pltpu.VMEM)
    return pl.pallas_call(
        partial(cross_kernel, load, width, ff, chunk, tab.shape[0]),
        in_specs=[SMEM, SMEM] + [full] * 6 + [ANY] * n,
        out_specs=[full] * 5,
        out_shape=[
            jax.ShapeDtypeStruct((rows, width), F32),
            jax.ShapeDtypeStruct((rows, width), F32),
            jax.ShapeDtypeStruct((chunk, 2 * ff + 4 * width + extra), BF),
            jax.ShapeDtypeStruct((VEC_ROWS, chunk), F32),
            jax.ShapeDtypeStruct((tab.shape[0], chunk), F32),
        ],
        scratch_shapes=[
            pltpu.VMEM((rows, 3 * width), BF),
            pltpu.VMEM((pairs, 2 * rows, rows), BF),
            pltpu.VMEM((rows, width), BF),
            pltpu.VMEM((rows, 3 * width), BF),
            pltpu.VMEM((rows, ff), BF),
            pltpu.VMEM((rows, ff), BF),
        ]
        + load.scratch(),
        compiler_params=pltpu.CompilerParams(vmem_limit_bytes=VMEM_LIMIT),
        cost_estimate=cost(16 * rows * width * ff, 20 * width * width),
        name="cross_block",
    )(origin, table, pay, docs.reshape(rows, 1), docs.reshape(1, rows), tab, vec, upb, *load.arrays)


def first_forward_kernel(load, pay_pieces, width, ff, *refs):
    n, m = load.count, len(pay_pieces.arrays)
    origin, pay_origin, vec, upb = refs[:4]
    srcs = refs[4 : 4 + n]
    pay_srcs = refs[4 + n : 4 + n + m]
    cross_ref, pay_ref, g_ref, gp_ref, n_ref, r_ref = refs[4 + n + m : 10 + n + m]
    sem, sem_cross = refs[10 + n + m : 12 + n + m]
    scratch = refs[12 + n + m :]
    wup, wdown = scratch[:2]
    copies = pay_pieces.copies(pay_srcs, pay_origin, sem, 2 * width, pay_ref.shape[1], pay_ref)
    others = pay_pieces.copies(pay_srcs, pay_origin, sem_cross, 0, 2 * width, cross_ref)
    copies.start()
    others.start()
    waits = load.start(srcs, origin, scratch)
    copies.wait()
    others.wait()
    for wait in waits:
        wait()
    hb = pay_ref[:, :width].astype(BF)
    normed, inverse = few_feed_forward(hb, hb.astype(F32), vec, upb.at[0:1, :], wup, wdown, g_ref, gp_ref, ff)
    n_ref[...] = normed
    r_ref[...] = inverse


def first_forward_call(origin, pay_origin, pay_pieces, vec, upb, load, ff):
    width = vec.shape[1]
    rows = pay_pieces.rows
    n, m = load.count, len(pay_pieces.arrays)
    full = pl.BlockSpec(memory_space=pltpu.VMEM)
    return pl.pallas_call(
        partial(first_forward_kernel, load, pay_pieces, width, ff),
        in_specs=[SMEM, SMEM] + [full] * 2 + [ANY] * (n + m),
        out_specs=[full] * 6,
        out_shape=[
            jax.ShapeDtypeStruct((rows, 2 * width), F32),
            jax.ShapeDtypeStruct((rows, pay_pieces.arrays[0].shape[1] - 2 * width), F32),
            jax.ShapeDtypeStruct((rows, ff), BF),
            jax.ShapeDtypeStruct((rows, ff), BF),
            jax.ShapeDtypeStruct((rows, width), F32),
            jax.ShapeDtypeStruct((rows, 1), F32),
        ],
        scratch_shapes=[pltpu.SemaphoreType.DMA((pay_pieces.count,))] * 2 + load.scratch(),
        compiler_params=pltpu.CompilerParams(vmem_limit_bytes=VMEM_LIMIT),
        cost_estimate=cost(6 * rows * width * ff, 4 * width * ff),
        name="first_rows_forward",
    )(origin, pay_origin, vec, upb, *load.arrays, *pay_pieces.arrays)


def first_kernel(load, width, ff, chunk, *refs):
    n = load.count
    origin, table, pay_ref, dy_ref, g_ref, gp_ref, n2_ref, r2_ref, vec = refs[:9]
    srcs = refs[9 : 9 + n]
    dz1_ref, do_ref, grads, sums_ref = refs[9 + n : 13 + n]
    scratch = refs[13 + n :]
    wdown, wup, wout = scratch[:3]
    waits = load.start(srcs, origin, scratch)
    hb = pay_ref[:, :width].astype(BF)
    o = pay_ref[:, width : 2 * width].astype(BF)
    n1 = pay_ref[:, 2 * width : 3 * width]
    r1 = pay_ref[:, 3 * width : 3 * width + 1]
    for wait in waits:
        wait()
    dz1, do, sums = few_feed_backward(
        dy_ref[...],
        n2_ref[...],
        r2_ref[...],
        n1,
        r1,
        hb,
        o,
        vec,
        wup,
        wdown,
        wout,
        g_ref,
        gp_ref,
        table[0],
        chunk,
        ff,
        grads,
    )
    dz1_ref[...] = dz1
    do_ref[...] = do
    if sums_ref.shape[1] > chunk:
        sums = jnp.concatenate([sums, jnp.zeros((sums_ref.shape[0] - VEC_ROWS, chunk), F32)], axis=0)
        sums = jnp.concatenate([sums, jnp.zeros((sums_ref.shape[0], sums_ref.shape[1] - chunk), F32)], axis=1)
    sums_ref[...] = sums.astype(sums_ref.dtype)


def first_call(origin, table, pay, dy, g, gp, n2, r2, vec, load, chunk, sums_shape):
    rows, width = dy.shape
    ff = g.shape[1]
    n = load.count
    group = ff // width
    full = pl.BlockSpec(memory_space=pltpu.VMEM)
    return pl.pallas_call(
        partial(first_kernel, load, width, ff, chunk),
        in_specs=[SMEM, SMEM] + [full] * 7 + [ANY] * n,
        out_specs=[full] * 4,
        out_shape=[
            jax.ShapeDtypeStruct((rows, width), F32),
            jax.ShapeDtypeStruct((rows, width), F32),
            jax.ShapeDtypeStruct((chunk, 2 * ff + width), BF),
            sums_shape,
        ],
        scratch_shapes=load.scratch(),
        compiler_params=pltpu.CompilerParams(vmem_limit_bytes=VMEM_LIMIT),
        cost_estimate=cost(8 * rows * width * ff, 4 * width * ff),
        name="first_rows_back",
    )(origin, table, pay, dy, g, gp, n2, r2, vec, *load.arrays)


def vector_kernel(pieces, col, own, width, ff, *refs):
    n = len(pieces.arrays)
    origin = refs[0]
    srcs = refs[1 : 1 + n]
    vec0, vec1, tab, upb = refs[1 + n : 5 + n]
    held, sem = refs[5 + n :]
    copies = pieces.copies(srcs, origin, sem, col, 128, held, by_origin=True)
    copies.start()
    upb[...] = jnp.zeros_like(upb)
    copies.wait()
    high = 2 * VEC_ROWS
    group = ff // width
    for i in range(pieces.origins):
        block = held[i].astype(F32)
        cols = slice(own * i, own * (i + 1))
        vec0[:, cols] = block[:VEC_ROWS, :own]
        vec1[:, cols] = block[VEC_ROWS:high, :own]
        tab[: own - high, cols] = block[high:own, :own]
        tab[own - high :, cols] = block[:, 64 : 64 + own]
        for b in range(2):
            for j in range(group):
                at = group * own * i + own * j
                upb[b : b + 1, at : at + own] = block[b * VEC_ROWS + UP0 + j : b * VEC_ROWS + UP0 + j + 1, :own]


def vector_call(origin, pieces, col, own, width, ff, places_n):
    n = len(pieces.arrays)
    full = pl.BlockSpec(memory_space=pltpu.VMEM)
    return pl.pallas_call(
        partial(vector_kernel, pieces, col, own, width, ff),
        in_specs=[SMEM] + [ANY] * n,
        out_specs=[full] * 4,
        out_shape=[
            jax.ShapeDtypeStruct((VEC_ROWS, width), F32),
            jax.ShapeDtypeStruct((VEC_ROWS, width), F32),
            jax.ShapeDtypeStruct((places_n, width), F32),
            jax.ShapeDtypeStruct((8, ff), F32),
        ],
        scratch_shapes=[pltpu.VMEM((pieces.origins, own, 128), BF), pltpu.SemaphoreType.DMA((pieces.count,))],
        compiler_params=pltpu.CompilerParams(vmem_limit_bytes=VMEM_LIMIT),
        cost_estimate=cost(1000, 128 * width * 8),
        name="vectors",
    )(origin, *pieces.arrays)


def pack_kernel(own, width, ff, places_n, *refs):
    qkv, out, up, down, gains, biases, upb, table, first, feed, other, side = refs
    group = ff // width
    first[:, : 3 * width] = qkv[0]
    first[:, 3 * width : 4 * width] = out[0]
    other[:, : 3 * width] = qkv[1]
    other[:, 3 * width : 4 * width] = out[1]
    for b, (pack, at) in enumerate(((feed, 0), (other, 4 * width))):
        pack[:, at : at + ff] = up[b]
        for j in range(group):
            pack[:, at + ff + j * width : at + ff + (j + 1) * width] = down[b, j * own : (j + 1) * own, :]
    side[...] = jnp.zeros_like(side)
    for b in range(2):
        at = b * VEC_ROWS
        side[at : at + 2, :own] = gains[b].astype(F32)
        side[at + 2 : at + 7, :own] = biases[b].astype(F32)
        row = upb[...].astype(F32)[b : b + 1]
        for j in range(group):
            side[at + UP0 + j : at + UP0 + j + 1, :own] = row[:, j * own : (j + 1) * own]
    places = table[...].astype(F32)
    high = 2 * VEC_ROWS
    side[high:own, :own] = places[: own - high]
    side[:, 64 : 64 + own] = places[own - high :]
    first[:, 4 * width :] = side[...].astype(BF)


def pack_call(own, width, ff, qkv, out, up, down, gains, biases, upb, table):
    full = pl.BlockSpec(memory_space=pltpu.VMEM)
    return pl.pallas_call(
        partial(pack_kernel, own, width, ff, table.shape[0]),
        in_specs=[full] * 8,
        out_specs=[full] * 3,
        out_shape=[
            jax.ShapeDtypeStruct((own, 4 * width + 128), BF),
            jax.ShapeDtypeStruct((own, 2 * ff), BF),
            jax.ShapeDtypeStruct((own, 4 * width + 2 * ff), BF),
        ],
        scratch_shapes=[pltpu.VMEM((own, 128), F32)],
        compiler_params=pltpu.CompilerParams(vmem_limit_bytes=VMEM_LIMIT),
        cost_estimate=cost(1000, 8 * own * 8 * width),
        name="pack_weights",
    )(qkv, out, up, down, gains, biases, upb, table)


def sum_kernel(plan, widths, *refs):
    groups = len(widths)
    count = sum(2 * groups + len(more) for _, more in plan)
    at = 0
    for out, (shift, more) in zip(refs[count:], plan):
        slots = refs[at : at + 2 * groups]
        at += 2 * groups
        extra = [(ref, first) for ref, first in zip(refs[at : at + len(more)], more)]
        at += len(more)
        rows = out.shape[0]
        edges = sorted({0, rows} | {e for ref, first in extra for e in (first, first + ref.shape[0])})
        for low, high in zip(edges, edges[1:]):
            col = 0
            for g, width in enumerate(widths):
                value = slots[2 * g][0, shift + low : shift + high, :].astype(F32)
                value = value + slots[2 * g + 1][0, shift + low : shift + high, :].astype(F32)
                for ref, first in extra:
                    if first <= low and high <= first + ref.shape[0]:
                        value = value + ref[low - first : high - first, col : col + width].astype(F32)
                out[low:high, col : col + width] = value.astype(BF)
                col += width


def sum_call(groups, outputs):
    args, specs, plan, shapes = [], [], [], []
    widths = [x.shape[2] for x, _ in groups]
    for slot, shift, rows, more in outputs:
        for pair in groups:
            for x in pair:
                args.append(x)
                specs.append(pl.BlockSpec((1,) + x.shape[1:], lambda i, k=slot: (k, 0, 0)))
        for x, _ in more:
            args.append(x)
            specs.append(pl.BlockSpec(x.shape, lambda i: (0, 0)))
        plan.append((shift, [first for _, first in more]))
        shapes.append(jax.ShapeDtypeStruct((rows, sum(widths)), BF))
    return pl.pallas_call(
        partial(sum_kernel, plan, widths),
        grid=(1,),
        in_specs=specs,
        out_specs=[pl.BlockSpec(x.shape, lambda i: (0, 0)) for x in shapes],
        out_shape=shapes,
        compiler_params=pltpu.CompilerParams(vmem_limit_bytes=VMEM_LIMIT),
        cost_estimate=cost(1000, sum(8 * x.shape[0] * x.shape[1] for x in shapes)),
        name="add_pieces",
    )(*args)


def finish_kernel(ff, width, *refs):
    x0, y0, x1, y1, grad_up, grad_out, grad_down = refs
    own = x0.shape[0]
    for b, (x, y) in enumerate(((x0, y0), (x1, y1))):
        for j in range(ff // width):
            cols = slice(j * width, (j + 1) * width)
            grad_down[b, j * own : (j + 1) * own, :] = x[:, cols].astype(F32) + y[:, cols].astype(F32)
        grad_up[b] = x[:, ff : 2 * ff].astype(F32) + y[:, ff : 2 * ff].astype(F32)
        grad_out[b] = x[:, 2 * ff : 2 * ff + width].astype(F32) + y[:, 2 * ff : 2 * ff + width].astype(F32)


def finish_call(ff, width, *args):
    own = args[0].shape[0]
    full = pl.BlockSpec(memory_space=pltpu.VMEM)
    return pl.pallas_call(
        partial(finish_kernel, ff, width),
        in_specs=[full] * 4,
        out_specs=[full] * 3,
        out_shape=[
            jax.ShapeDtypeStruct((2, own, ff), F32),
            jax.ShapeDtypeStruct((2, own, width), F32),
            jax.ShapeDtypeStruct((2, own * ff // width, width), F32),
        ],
        compiler_params=pltpu.CompilerParams(vmem_limit_bytes=VMEM_LIMIT),
        cost_estimate=cost(1000, 16 * own * (2 * ff + width)),
        name="finish_feed",
    )(*args)


def finish_last_kernel(own, width, group, places_n, *refs):
    q0, q0s, q1, q1s, grad_qkv, grad_gains, grad_biases, grad_up_bias, grad_table = refs
    blocks = []
    for b, (x, y) in enumerate(((q0, q0s), (q1, q1s))):
        at = x.shape[1] - 3 * width - 128
        cols = slice(at, at + 3 * width)
        grad_qkv[b] = x[:, cols].astype(F32) + y[:, cols].astype(F32)
        blocks.append(x[:, at + 3 * width :].astype(F32) + y[:, at + 3 * width :].astype(F32))
    for b, block in enumerate(blocks):
        grad_gains[b] = block[:2, :own]
        grad_biases[b] = block[2:7, :own]
        for j in range(group):
            grad_up_bias[b : b + 1, j * own : (j + 1) * own] = block[UP0 + j : UP0 + j + 1, :own]
    high = 2 * VEC_ROWS
    grad_table[: own - high, :] = blocks[1][high:own, :own]
    grad_table[own - high :, :] = blocks[1][:, 64 : 64 + own]


def finish_last_call(own, width, group, places_n, *args):
    full = pl.BlockSpec(memory_space=pltpu.VMEM)
    return pl.pallas_call(
        partial(finish_last_kernel, own, width, group, places_n),
        in_specs=[full] * 4,
        out_specs=[full] * 5,
        out_shape=[
            jax.ShapeDtypeStruct((2, own, 3 * width), F32),
            jax.ShapeDtypeStruct((2, 2, own), F32),
            jax.ShapeDtypeStruct((2, 5, own), F32),
            jax.ShapeDtypeStruct((2, group * own), F32),
            jax.ShapeDtypeStruct((places_n, own), F32),
        ],
        compiler_params=pltpu.CompilerParams(vmem_limit_bytes=VMEM_LIMIT),
        cost_estimate=cost(1000, 48 * own * width),
        name="finish_qkv",
    )(*args)


def tie(x, *others):
    return lax.optimization_barrier((x, others))[0] if others else x


class Ring:
    def __init__(self, shards):
        chips = shards // 2
        self.shards, self.chips = shards, chips
        self.order = list(range(0, chips, 2)) + list(range(chips - 1, 0, -2))
        self.place = {chip: i for i, chip in enumerate(self.order)}

    def shift(self, by):
        pairs = []
        for i, chip in enumerate(self.order):
            to = self.order[(i + by) % self.chips]
            pairs += [(2 * chip, 2 * to), (2 * chip + 1, 2 * to + 1)]
        return pairs

    def forward(self, x):
        return lax.ppermute(x, "shard", self.shift(1))

    def backward(self, x):
        return lax.ppermute(x, "shard", self.shift(-1))

    def sibling(self, x):
        return lax.ppermute(x, "shard", [(i, i ^ 1) for i in range(self.shards)])

    def behind_table(self):
        return [
            [self.order[(self.place[d // 2] - k) % self.chips] for k in range(self.chips)] for d in range(self.shards)
        ]

    def slot_table(self):
        rows = []
        for d in range(self.shards):
            chip = d // 2
            rows.append([(self.place[q] - self.place[chip]) % self.chips for q in range(self.chips)] + [d % 2])
        return rows


def half_of(rows):
    return (rows // 32) * 16 if rows >= 32 else rows


class Gather:
    def __init__(self, ring, x):
        self.ring, self.steps = ring, 0
        self.ahead = self.behind = x
        self.rows = x.shape[0]
        self.entries, self.pending = [], []

    def take(self, *others):
        values = (self.ahead, self.behind, [e[0] for e in self.pending])
        ahead, behind, shared = tie(values, *others)
        for e, x in zip(self.pending, shared):
            self.entries.append((x,) + e[1:])
        self.sent = (ahead, behind)
        far = self.ring.chips // 2
        if self.steps == 0:
            fresh = [(ahead, 0, 0)]
        elif self.steps < far:
            fresh = [(ahead, self.steps, 0), (behind, self.ring.chips - self.steps, 0)]
        else:
            fresh = [(ahead, far, 0), (behind, far, half_of(self.rows))]
        self.entries += [(x, 2 * back, first, 0, x.shape[0]) for x, back, first in fresh]
        return ahead, behind, fresh

    def share(self, fresh):
        self.pending = [(self.ring.sibling(x), 2 * back + 1, first, 0, x.shape[0]) for x, back, first in fresh]

    def step(self, *others):
        ahead, behind, fresh = self.take(*others)
        half = half_of(self.rows)
        last = self.steps == self.ring.chips // 2 - 1
        self.ahead = self.ring.forward(ahead[:half] if last else ahead)
        self.behind = self.ring.backward(behind[half:] if last else behind)
        self.share(fresh)
        self.steps += 1

    def finish(self, *others):
        self.share(self.take(*others)[2])
        return Pieces(self.entries + self.pending, self.rows, self.ring.shards)


class Exchange:
    def __init__(self, ring, x, bits):
        self.ring, self.rows, self.bits = ring, x.shape[0], bits
        self.held, self.new, self.masks, self.shared = x, None, [0], []

    def gather(self, *others):
        if self.new is None:
            self.held = tie(self.held, *others)
            return
        held, new = tie((self.held, self.new), *others)
        self.held, self.new = held, new

    def step(self, *others):
        self.gather(*others)
        if self.new is not None:
            self.held = jnp.concatenate([self.held, self.new], axis=0)
        self.sent = (self.held,)
        bit = self.bits[len(self.masks).bit_length() - 1]
        pairs = [(d, d ^ (2 * bit)) for d in range(self.ring.shards)]
        self.new = lax.ppermute(self.held, "shard", pairs)
        self.masks += [m ^ bit for m in self.masks]
        if len(self.masks) == 2 ** len(self.bits):
            self.shared.append(self.ring.sibling(self.held))

    def finish(self, *others):
        self.gather(*others)
        self.shared.append(self.ring.sibling(self.new))
        entries, at = [], 0
        for own, other in zip((self.held, self.new), self.shared):
            for i in range(own.shape[0] // self.rows):
                entries.append((own, at, 0, i * self.rows, self.rows))
                entries.append((other, len(self.masks) + at, 0, i * self.rows, self.rows))
                at += 1
        return Pieces(entries, self.rows, self.ring.shards)

    def origin_table(self, me):
        core = me % 2
        own = jnp.bitwise_xor(me // 2, jnp.asarray(self.masks, jnp.int32))
        return jnp.concatenate([2 * own + core, 2 * own + 1 - core])


class Reduce:
    def __init__(self, ring, *groups):
        self.ring, self.steps = ring, 0
        self.groups = list(groups)

    def step(self, *others):
        ring, far = self.ring, self.ring.chips // 2
        rows = self.groups[0][0].shape[1]
        half = half_of(rows)
        self.steps += 1
        k = far - self.steps + 1
        if self.steps == 1:
            groups = tie(self.groups, *others)
            outputs = [(far, 0, half, []), (far, half, rows - half, [])]
        else:
            groups, ahead, behind = tie((self.groups, self.ahead, self.behind), *others)
            first = half if self.steps == 2 else 0
            outputs = [(k, 0, rows, [(ahead, 0)]), (ring.chips - k, 0, rows, [(behind, first)])]
        self.sent = tuple(sum_call(groups, outputs))
        self.ahead = ring.forward(self.sent[0])
        self.behind = ring.backward(self.sent[1])

    def ahead_behind(self):
        return self.ahead, self.behind

    def result(self, more, *others):
        groups, ahead, behind = tie((self.groups, self.ahead, self.behind), *others)
        rows = groups[0][0].shape[1]
        return sum_call(groups, [(0, 0, rows, [(ahead, 0), (behind, 0), (more, 0)])])[0]


def swap_seq(x):
    return lax.ppermute(x, "seq", [(0, 1), (1, 0)])


def over_seq(x):
    low = x.astype(BF)
    return low.astype(F32) + swap_seq(low).astype(F32)


def body(
    tokens,
    qkv_weight,
    out_weight,
    up_weight,
    down_weight,
    norm_gains,
    biases,
    up_bias,
    position_table,
    segment_docs,
    cotangent,
):
    shards = lax.axis_size("shard")
    me = lax.axis_index("shard")
    rows, width = tokens.shape
    segs = rows // SEG
    ff = up_weight.shape[2]
    group = ff // width
    own = width // shards
    places_n = position_table.shape[0]
    docs = segment_docs[0]
    ringed = own == 48 and places_n == 64 and shards % 4 == 0
    ring = Ring(shards)
    place = me[None]

    if ringed:
        chips, cores, chunk = ring.chips, 2, own
        behind = jnp.asarray(ring.behind_table(), jnp.int32)[me]
        core = me % 2
        origin = jnp.stack([2 * behind + core, 2 * behind + 1 - core], axis=1).reshape(-1)
        table = jnp.concatenate([jnp.asarray(ring.slot_table(), jnp.int32)[me], (me * segs)[None]])
        first, feed, other = pack_call(
            own, width, ff, qkv_weight, out_weight, up_weight, down_weight, norm_gains, biases, up_bias, position_table
        )
        g_a, g_f, x_w = Gather(ring, first), Gather(ring, feed), Gather(ring, other)
        g_a.step()
        g_a.step()
        g_f.step(*g_a.sent)
        g_a.step()
        g_a.step()
        g_f.step(*g_a.sent)
        p_a = g_a.finish()
        vec0, vec1, tab, upb = vector_call(origin, p_a, 4 * width, own, width, ff, places_n)
        l_qkv, l_out = (p_a, 0, 3 * width), (p_a, 3 * width, width)
    else:
        chips, cores, chunk = 1, 1, width
        origin = jnp.zeros((1,), jnp.int32)
        table = jnp.stack([jnp.int32(0), jnp.int32(0), me * segs])
        full = [
            [lax.all_gather(w[b], "shard", axis=0, tiled=True) for w in (qkv_weight, out_weight, up_weight, down_weight)]
            for b in range(2)
        ]
        small = []
        for b in range(2):
            small += [norm_gains[b], biases[b], up_bias[b].reshape(group, own), jnp.zeros((VEC_ROWS - UP0 - group, own), BF)]
        small = jnp.concatenate(small + [position_table], axis=0)
        small_all = lax.all_gather(small, "shard", axis=1, tiled=True).astype(F32)
        vec0, vec1, tab = small_all[:VEC_ROWS], small_all[VEC_ROWS : 2 * VEC_ROWS], small_all[2 * VEC_ROWS :]
        upb = [
            v[UP0 : UP0 + group].reshape(group, shards, own).transpose(1, 0, 2).reshape(1, ff) for v in (vec0, vec1)
        ]
        upb = jnp.concatenate(upb + [jnp.zeros((6, ff), F32)], axis=0)

        def single(x):
            return Pieces([(x, 0, 0, 0, x.shape[0])], x.shape[0], 1)

        w0, w1 = [[(single(x), 0, x.shape[1]) for x in full[b]] for b in range(2)]
        l_qkv, l_out, l_up, l_down = w0

    def gated(x, *sent):
        return tie(x, *[y for z in sent for y in z]) if ringed else x

    gate = gated(origin, g_f.sent) if ringed else origin
    qkv = project_call(gate, tokens, vec0, Loader(l_qkv))
    if ringed:
        g_f.step(qkv)
        gate = gated(origin, g_f.sent)
    a, o, h, hb, n1, r1 = attention_call(gate, tokens, qkv, vec0, Loader(l_out))
    if ringed:
        g_f.step(o)
        x_w.step(*g_f.sent)
        p_f = g_f.finish()
        l_up, l_down = (p_f, 0, ff), (p_f, ff, width, group)
        gate = gated(origin, x_w.sent)
    y, g, gp, dz, dm, pay, sums2 = feed_call(gate, h, cotangent, o, n1, r1, vec0, upb, Loader(l_up, l_down), ff)

    gate = origin
    if ringed:
        exchange = Exchange(ring, pay, (1, 4, 2))
        exchange.step()
        x_w.step(dm)
        gate = gated(origin, exchange.sent, x_w.sent)
    du, dz1, db, do, sums1, up_sums = feed_back_call(gate, dz, gp, n1, r1, vec0, Loader(l_down, l_up, l_out))
    gate = table
    if ringed:
        exchange.step(du)
        x_w.step(du)
        gate = gated(table, exchange.sent, x_w.sent)
    main_d = list(grads_down_call(tie(gate, du), g, dm, chips, cores, chunk))
    gate = table
    if ringed:
        exchange.step(main_d[0])
        main_d[1] = ring.sibling(tie(main_d[1], *exchange.sent))
        gate = gated(table, exchange.sent)
    main_u = list(grads_up_call(tie(gate, main_d[0]), du, hb, o, db, chips, cores, chunk))
    gate = origin
    if ringed:
        p_p = exchange.finish(main_u[0])
        x_w.step(main_u[0], exchange.new)
        main_u[1] = ring.sibling(tie(main_u[1], *x_w.sent))
        pay_origin = exchange.origin_table(me)
        gate = gated(origin, x_w.sent)
    else:
        p_p = single(lax.all_gather(pay, "shard", axis=0, tiled=True))
        pay_origin = origin

    pay_cross, pay_all, g_f, gp_f, n2_f, r2_f = first_forward_call(
        tie(gate, main_u[0]), pay_origin, p_p, vec0, upb, Loader(l_up, l_down), ff
    )
    gate = origin
    if ringed:
        r_m = Reduce(ring, tuple(main_d), tuple(main_u))
        r_m.step(g_f)
        p_x = x_w.finish(g_f)
        at = 4 * width
        w1 = (p_x, 0, 3 * width), (p_x, 3 * width, width), (p_x, at, ff), (p_x, at + ff, width, group)
        gate = gated(origin, r_m.sent)
    cross_out, d_cross, c_all, c_sums, c_tab = cross_call(
        tie(gate, g_f), place, pay_cross, docs, tab, vec1, upb, Loader(*w1), ff, own, 128 if ringed else 0
    )
    gate = origin
    if ringed:
        r_m.step(d_cross)
        c_swap = swap_seq(c_all)
        gate = gated(origin, r_m.sent)
    sums_shape = jax.ShapeDtypeStruct((own, 128), BF) if ringed else jax.ShapeDtypeStruct((VEC_ROWS, own), F32)
    dz1_first, do_first, f_all, f_sums = first_call(
        gate, place, pay_all, d_cross, g_f, gp_f, n2_f, r2_f, vec0, Loader(l_down, l_up, l_out), own, sums_shape
    )
    gate = table
    if ringed:
        r_m.step(do_first)
        gate = gated(table, r_m.sent)
    dqkv, sums_v, *tail = attention_back_call(
        gate, qkv, a, do, tokens, do_first, sums1, sums2, up_sums, chips, cores, chunk
    )
    gate = origin
    if ringed:
        tail[1] = ring.sibling(tie(tail[1], *r_m.ahead_behind()))
        r_m.step(tail[0])
        r_q = Reduce(ring, tuple(tail))
        r_q.step(*r_m.sent)
        gate = gated(origin, r_q.sent)
    d_tokens = input_grad_call(gate, table[-1:], dqkv, dz1, dz1_first, Loader(l_qkv))
    own_rows = lax.dynamic_slice_in_dim(cross_out, me * segs, segs, 0)
    merged = y.reshape(segs, SEG, width).at[:, 0, :].set(own_rows.astype(BF)).reshape(rows, width)

    if ringed:
        r_q.step(d_tokens)
        m_all = r_m.result(f_all, *r_q.sent)
        m_swap = swap_seq(m_all)
        r_q.step()
        grad_up, grad_out, grad_down = finish_call(ff, width, m_all, m_swap, c_all, c_swap)
        r_q.step()
        q_all = r_q.result(jnp.concatenate([jnp.zeros((own, 3 * width), BF), f_sums], axis=1))
        grad_qkv, grad_gains, grad_biases, grad_up_bias, grad_table = finish_last_call(
            own, width, group, places_n, q_all, swap_seq(q_all), c_all, c_swap
        )
    else:

        def scattered(x):
            return lax.psum_scatter(x, "shard", scatter_dimension=0, tiled=True)

        def blocks(x):
            return jnp.concatenate([x[:, j * width : (j + 1) * width] for j in range(group)], axis=0)

        main_d, main_u, q_sum = scattered(blocks(main_d[0][0])), scattered(main_u[0][0]), scattered(tail[0][0])
        c_down, c_feed, c_qkv = blocks(c_all[:, :ff]), c_all[:, ff : 2 * ff + width], c_all[:, 2 * ff + width :]
        grad_down = jnp.stack([over_seq(main_d.astype(F32) + blocks(f_all[:, :ff]).astype(F32)), over_seq(c_down)])
        both = jnp.stack([over_seq(main_u.astype(F32) + f_all[:, ff:].astype(F32)), over_seq(c_feed)])
        grad_up, grad_out = both[:, :, :ff], both[:, :, ff:]
        grad_qkv = jnp.stack([over_seq(q_sum), over_seq(c_qkv)])
        vec_sums = jnp.concatenate(
            [sums1[0:1], sums2[0:1], sums_v[0:1], sums1[2:3], sums2[2:3], sums1[1:2], sums2[1:2], jnp.zeros((1, width), F32)]
            + [up_sums[0].reshape(group, width)],
            axis=0,
        )
        vec_sums = lax.psum(vec_sums, ("seq", "shard"))
        seg_vec = lax.dynamic_slice_in_dim(vec_sums[:8], me * own, own, 1)
        seg_up = lax.dynamic_slice_in_dim(vec_sums[8:].reshape(ff), me * own * group, own * group, 0)
        few = over_seq(jnp.concatenate([f_sums, c_sums, c_tab], axis=0))
        first_vec, cross_vec, grad_table = few[:VEC_ROWS], few[VEC_ROWS : 2 * VEC_ROWS], few[2 * VEC_ROWS :]
        seg_vec = seg_vec + first_vec[:8]
        grad_gains = jnp.stack([seg_vec[:2], cross_vec[:2]])
        grad_biases = jnp.stack([seg_vec[2:7], cross_vec[2:7]])
        seg_up = seg_up + first_vec[UP0 : UP0 + group].reshape(-1)
        grad_up_bias = jnp.stack([seg_up, cross_vec[UP0 : UP0 + group].reshape(-1)])
    return (
        merged,
        d_tokens,
        grad_qkv,
        grad_out,
        grad_up,
        grad_down,
        grad_gains,
        grad_biases,
        grad_up_bias,
        grad_table,
    )


def solution(mesh):
    in_specs = (
        P(("seq", "shard"), None),
        P(None, "shard", None),
        P(None, "shard", None),
        P(None, "shard", None),
        P(None, "shard", None),
        P(None, None, "shard"),
        P(None, None, "shard"),
        P(None, "shard"),
        P(None, "shard"),
        P("seq", None),
        P(("seq", "shard"), None),
    )
    out_specs = (
        P(("seq", "shard"), None),
        P(("seq", "shard"), None),
        P(None, "shard", None),
        P(None, "shard", None),
        P(None, "shard", None),
        P(None, "shard", None),
        P(None, None, "shard"),
        P(None, None, "shard"),
        P(None, "shard"),
        P(None, "shard"),
    )
    return jax.shard_map(body, mesh=mesh, in_specs=in_specs, out_specs=out_specs, check_vma=False)
```

```python
from functools import partial

import jax
import jax.numpy as jnp
from jax import lax
from jax.experimental import pallas as pl
from jax.experimental.pallas import tpu as pltpu
from jax.sharding import PartitionSpec as P

HEAD = 64
SEG = 128
EPSILON = 1e-05
MASKED = -1e30
BF = jnp.bfloat16
F32 = jnp.float32
TILE = 256
VMEM_LIMIT = 67043328

GAIN1, GAIN2, BIAS_V, BIAS_O, BIAS_D, SHIFT1, SHIFT2, UP0 = 0, 1, 2, 3, 4, 5, 6, 7
VEC_ROWS = 16


def dot_nn(a, b):
    return lax.dot_general(a, b, (((1,), (0,)), ((), ())), preferred_element_type=F32)


def dot_nt(a, b):
    return lax.dot_general(a, b, (((1,), (1,)), ((), ())), preferred_element_type=F32)


def dot_tn(a, b):
    return lax.dot_general(a, b, (((0,), (0,)), ((), ())), preferred_element_type=F32)


def row_mean(x):
    return jnp.mean(x, axis=-1, keepdims=True)


def col_sum(x):
    return jnp.sum(x.astype(F32), axis=0, keepdims=True)


def norm_rows(z):
    centred = z - row_mean(z)
    inverse = lax.rsqrt(row_mean(centred * centred) + EPSILON)
    return centred * inverse, inverse


def norm_back(scaled, normed, inverse):
    return inverse * (scaled - row_mean(scaled) - normed * row_mean(scaled * normed))


def gelu_both(u):
    phi = 0.5 + 0.5 * lax.erf(u * (2.0**-0.5))
    return u * phi, phi + u * jnp.exp(-0.5 * u * u) * 0.3989422804014327


def halves(pair):
    lane = lax.broadcasted_iota(jnp.int32, pair.shape, 1)
    zero = jnp.zeros_like(pair)
    return jnp.concatenate([jnp.where(lane < HEAD, pair, zero), jnp.where(lane < HEAD, zero, pair)], axis=0)


def side_by_side(stacked):
    rows = stacked.shape[0] // 2
    return jnp.concatenate([stacked[:rows], stacked[rows:]], axis=1)


def pairs_forward(q, k, v, allowed):
    scores = [dot_nt(halves(a), b) * (HEAD**-0.5) for a, b in zip(q, k)]
    if allowed is not None:
        scores = [jnp.where(allowed, x, MASKED) for x in scores]
    powers = [jnp.exp(x - jnp.max(x, axis=-1, keepdims=True)) for x in scores]
    weights = [(x / jnp.sum(x, axis=-1, keepdims=True)).astype(BF) for x in powers]
    return [(w, dot_nn(side_by_side(w), halves(x)).astype(BF)) for w, x in zip(weights, v)]


def pairs_backward(q, k, v, weights, d_out):
    d_stacks = [halves(x) for x in d_out]
    d_weights = [dot_nt(x, y) for x, y in zip(d_stacks, v)]
    wide = [w.astype(F32) for w in weights]
    inner = [jnp.sum(w * x, axis=-1, keepdims=True) for w, x in zip(wide, d_weights)]
    d_scores = [(w * (x - y)).astype(BF) for w, x, y in zip(wide, d_weights, inner)]
    scale = HEAD**-0.5
    d_q = [(dot_nn(side_by_side(x), halves(y)) * scale).astype(BF) for x, y in zip(d_scores, k)]
    d_k = [(dot_tn(x, halves(y)) * scale).astype(BF) for x, y in zip(d_scores, q)]
    d_v = [dot_tn(w, x).astype(BF) for w, x in zip(weights, d_stacks)]
    return zip(d_q, d_k, d_v)


class Copies:
    def __init__(self, copies):
        self.all = copies

    def start(self):
        start_all(self.all)

    def wait(self):
        wait_all(self.all)


class Pieces:
    def __init__(self, entries, chunk, origins):
        self.entries = list(entries)
        self.chunk, self.origins = chunk, origins
        self.rows = chunk * origins
        self.count = len(self.entries)
        self.arrays, self.which = [], []
        for x, *_ in self.entries:
            at = [i for i, y in enumerate(self.arrays) if y is x]
            if not at:
                self.arrays.append(x)
            self.which.append(at[0] if at else len(self.arrays) - 1)

    def copies(self, refs, origin, sems, col, width, dst, by_origin=False, blocks=1):
        def build(refs, entries, sem0):
            out = []
            for n, (ref, (x, entry, first, top, rows)) in enumerate(zip(refs, entries)):
                for j in range(blocks):
                    if by_origin:
                        to = dst.at[origin[entry], pl.ds(first, rows), :]
                    else:
                        start = (origin[entry] * blocks + j) * self.chunk + first
                        to = dst.at[pl.ds(pl.multiple_of(start, 16 if rows % 16 == 0 else 8), rows), :]
                    source = ref.at[pl.ds(top, rows), pl.ds(col + j * width, width)]
                    out.append(pltpu.make_async_copy(source, to, sems.at[(sem0 + n) * blocks + j]))
            return out

        return Copies(build([refs[i] for i in self.which], self.entries, 0))


class Loader:
    def __init__(self, *items):
        self.items = [(*item, 1)[:4] for item in items]
        self.groups = []
        for pieces, *_ in items:
            if pieces not in self.groups:
                self.groups.append(pieces)
        self.arrays = [x for g in self.groups for x in g.arrays]
        self.count = len(self.arrays)

    def scratch(self):
        buffers = [pltpu.VMEM((p.rows * blocks, width), BF) for p, _, width, blocks in self.items]
        return buffers + [pltpu.SemaphoreType.DMA((p.count * blocks,)) for p, _, _, blocks in self.items]

    def start(self, srcs, origin, scratch):
        at, where = 0, {}
        for g in self.groups:
            where[id(g)] = srcs[at : at + len(g.arrays)]
            at += len(g.arrays)
        m = len(self.items)
        sets = [
            p.copies(where[id(p)], origin, scratch[m + i], col, width, scratch[i], blocks=blocks)
            for i, (p, col, width, blocks) in enumerate(self.items)
        ]
        for copies in sets:
            copies.start()
        return [copies.wait for copies in sets]


def start_all(copies):
    for c in copies:
        c.start()


def wait_all(copies):
    for c in copies:
        c.wait()


ANY = pl.BlockSpec(memory_space=pl.ANY)
SMEM = pl.BlockSpec(memory_space=pltpu.SMEM)


def whole(shape):
    return pl.BlockSpec(shape, lambda *i: (0,) * len(shape), pipeline_mode=pl.Buffered(1))


def whole_out(shape):
    return pl.BlockSpec(shape, lambda *i: (0,) * len(shape))


def tile(*shape):
    return pl.BlockSpec(shape, lambda i: (i,) + (0,) * (len(shape) - 1))


def cost(flops, nbytes):
    return pl.CostEstimate(flops=int(flops * 0.01), bytes_accessed=int(nbytes * 0.01), transcendentals=0)


def project_kernel(load, width, *refs):
    n = load.count
    origin, x_ref, vec = refs[0], refs[1], refs[2]
    srcs = refs[3 : 3 + n]
    qkv_ref = refs[3 + n]
    scratch = refs[4 + n :]
    wqkv = scratch[0]

    @pl.when(pl.program_id(0) == 0)
    def _():
        for wait in load.start(srcs, origin, scratch):
            wait()

    qkv = dot_nn(x_ref[...], wqkv[...])
    qkv_ref[:, : 2 * width] = qkv[:, : 2 * width].astype(BF)
    qkv_ref[:, 2 * width :] = (qkv[:, 2 * width :] + vec[BIAS_V : BIAS_V + 1, :]).astype(BF)


def project_call(origin, x, vec, load):
    rows, width = x.shape
    return pl.pallas_call(
        partial(project_kernel, load, width),
        grid=(rows // TILE,),
        in_specs=[SMEM, tile(TILE, width), whole(vec.shape)] + [ANY] * load.count,
        out_specs=tile(TILE, 3 * width),
        out_shape=jax.ShapeDtypeStruct((rows, 3 * width), BF),
        scratch_shapes=load.scratch(),
        compiler_params=pltpu.CompilerParams(vmem_limit_bytes=VMEM_LIMIT),
        cost_estimate=cost(2 * rows * width * 3 * width, 10 * rows * width),
        name="segment_project",
    )(origin, x, vec, *load.arrays)


def attention_kernel(load, width, *refs):
    n = load.count
    origin, x_ref, qkv_ref, vec = refs[:4]
    srcs = refs[4 : 4 + n]
    a_ref, o_ref, h_ref, hb_ref, n_ref, r_ref = refs[4 + n : 10 + n]
    scratch = refs[10 + n :]
    wout = scratch[0]

    @pl.when(pl.program_id(0) == 0)
    def _():
        for wait in load.start(srcs, origin, scratch):
            wait()

    for s in range(TILE // SEG):
        rows = pl.ds(s * SEG, SEG)
        pairs = range(width // 128)
        q = [qkv_ref[rows, pl.ds(p * 128, 128)] for p in pairs]
        k = [qkv_ref[rows, pl.ds(width + p * 128, 128)] for p in pairs]
        v = [qkv_ref[rows, pl.ds(2 * width + p * 128, 128)] for p in pairs]
        for p, (weights, out) in enumerate(pairs_forward(q, k, v, None)):
            a_ref[s, p] = weights
            o_ref[rows, pl.ds(p * 128, 128)] = out
    z = x_ref[...].astype(F32) + dot_nn(o_ref[...], wout[...]) + vec[BIAS_O : BIAS_O + 1, :]
    normed, inverse = norm_rows(z)
    h = normed * vec[GAIN1 : GAIN1 + 1, :] + vec[SHIFT1 : SHIFT1 + 1, :]
    h_ref[...] = h
    hb_ref[...] = h.astype(BF)
    n_ref[...] = normed.astype(BF)
    r_ref[...] = inverse


def attention_call(origin, x, qkv, vec, load):
    rows, width = x.shape
    n = load.count
    segs = rows // SEG
    pairs = width // 128
    return pl.pallas_call(
        partial(attention_kernel, load, width),
        grid=(rows // TILE,),
        in_specs=[SMEM, tile(TILE, width), tile(TILE, 3 * width), whole(vec.shape)] + [ANY] * n,
        out_specs=[
            tile(TILE // SEG, pairs, 2 * SEG, SEG),
            tile(TILE, width),
            tile(TILE, width),
            tile(TILE, width),
            tile(TILE, width),
            tile(TILE, 1),
        ],
        out_shape=[
            jax.ShapeDtypeStruct((segs, pairs, 2 * SEG, SEG), BF),
            jax.ShapeDtypeStruct((rows, width), BF),
            jax.ShapeDtypeStruct((rows, width), F32),
            jax.ShapeDtypeStruct((rows, width), BF),
            jax.ShapeDtypeStruct((rows, width), BF),
            jax.ShapeDtypeStruct((rows, 1), F32),
        ],
        scratch_shapes=load.scratch(),
        compiler_params=pltpu.CompilerParams(vmem_limit_bytes=VMEM_LIMIT),
        cost_estimate=cost(2 * rows * width * 2 * width, 16 * rows * width),
        name="segment_attention",
    )(origin, x, qkv, vec, *load.arrays)


def feed_kernel(load, width, ff, *refs):
    n = load.count
    origin, h_ref, c_ref, o_ref, n_ref, r_ref, vec, upb = refs[:8]
    srcs = refs[8 : 8 + n]
    y_ref, g_ref, gp_ref, dz_ref, dm_ref, pay_ref, sums_ref = refs[8 + n : 15 + n]
    scratch = refs[15 + n :]
    wup, wdown = scratch[:2]

    @pl.when(pl.program_id(0) == 0)
    def _():
        for wait in load.start(srcs, origin, scratch):
            wait()
        sums_ref[...] = jnp.zeros_like(sums_ref)

    h = h_ref[...]
    hb = h.astype(BF)
    block = 512
    total = jnp.zeros((TILE, width), F32)
    u = dot_nn(hb, wup[:, :block]) + upb[0:1, :block]
    for j in range(ff // block):
        cols = slice(j * block, (j + 1) * block)
        if (j + 1) * block < ff:
            later = slice((j + 1) * block, (j + 2) * block)
            u_next = dot_nn(hb, wup[:, later]) + upb[0:1, later]
        active, slope = gelu_both(u)
        active = active.astype(BF)
        g_ref[:, cols] = active
        gp_ref[:, cols] = slope.astype(BF)
        total = total + dot_nn(active, wdown[cols, :])
        u = u_next
    normed, inverse = norm_rows(h + total + vec[BIAS_D : BIAS_D + 1, :])
    gain = vec[GAIN2 : GAIN2 + 1, :]
    y = normed * gain + vec[SHIFT2 : SHIFT2 + 1, :]
    y_ref[...] = y.astype(BF)
    row = lax.broadcasted_iota(jnp.int32, (TILE, 1), 0)
    dy = jnp.where(row % SEG == 0, 0.0, c_ref[...].astype(F32))
    dz = norm_back(dy * gain, normed, inverse)
    dz_ref[...] = dz
    dm = dz.astype(BF)
    dm_ref[...] = dm
    sums_ref[0:1, :] += col_sum(dy * normed)
    sums_ref[1:2, :] += col_sum(dy)
    sums_ref[2:3, :] += col_sum(dm)
    lane = lax.broadcasted_iota(jnp.int32, (1, 128), 1)
    for i in range(pay_ref.shape[0] // (TILE // SEG)):

        @pl.when(pl.program_id(0) == i)
        def _(i=i):
            for s in range(TILE // SEG):
                here = slice(s * SEG, s * SEG + 1)
                few = slice(s * SEG, s * SEG + 16)
                at = slice(i * (TILE // SEG) + s, i * (TILE // SEG) + s + 1)
                pay_ref[at, 0:width] = y[here].astype(BF).astype(F32)
                pay_ref[at, width : 2 * width] = c_ref[few, :].astype(F32)[:1]
                pay_ref[at, 2 * width : 3 * width] = h[here].astype(BF).astype(F32)
                pay_ref[at, 3 * width : 4 * width] = o_ref[few, :].astype(F32)[:1]
                pay_ref[at, 4 * width : 5 * width] = n_ref[few, :].astype(F32)[:1]
                high = r_ref[here].astype(BF).astype(F32)
                pay_ref[at, 5 * width :] = jnp.where(lane == 0, high, jnp.where(lane == 1, r_ref[here] - high, 0.0))


def feed_call(origin, h, cot, o, n1, r1, vec, upb, load, ff):
    rows, width = h.shape
    n = load.count
    pay = 5 * width + 128
    return pl.pallas_call(
        partial(feed_kernel, load, width, ff),
        grid=(rows // TILE,),
        in_specs=[
            SMEM,
            tile(TILE, width),
            tile(TILE, width),
            tile(TILE, width),
            tile(TILE, width),
            tile(TILE, 1),
            whole(vec.shape),
            whole(upb.shape),
        ]
        + [ANY] * n,
        out_specs=[
            tile(TILE, width),
            tile(TILE, ff),
            tile(TILE, ff),
            tile(TILE, width),
            tile(TILE, width),
            whole_out((rows // SEG, pay)),
            whole_out((8, width)),
        ],
        out_shape=[
            jax.ShapeDtypeStruct((rows, width), BF),
            jax.ShapeDtypeStruct((rows, ff), BF),
            jax.ShapeDtypeStruct((rows, ff), BF),
            jax.ShapeDtypeStruct((rows, width), F32),
            jax.ShapeDtypeStruct((rows, width), BF),
            jax.ShapeDtypeStruct((rows // SEG, pay), F32),
            jax.ShapeDtypeStruct((8, width), F32),
        ],
        scratch_shapes=load.scratch(),
        compiler_params=pltpu.CompilerParams(vmem_limit_bytes=VMEM_LIMIT),
        cost_estimate=cost(4 * rows * width * ff, 4 * rows * ff),
        name="segment_feed",
    )(origin, h, cot, o, n1, r1, vec, upb, *load.arrays)


def feed_back_kernel(load, width, ff, *refs):
    n = load.count
    origin, dz_ref, gp_ref, n_ref, r_ref, vec = refs[:6]
    srcs = refs[6 : 6 + n]
    du_ref, dz1_ref, db_ref, do_ref, sums_ref, upsum_ref = refs[6 + n : 12 + n]
    scratch = refs[12 + n :]
    wdown, wup, wout = scratch[:3]

    @pl.when(pl.program_id(0) == 0)
    def _():
        for wait in load.start(srcs, origin, scratch):
            wait()
        sums_ref[...] = jnp.zeros_like(sums_ref)
        upsum_ref[...] = jnp.zeros_like(upsum_ref)

    dz = dz_ref[...]
    dm = dz.astype(BF)
    block = 512
    total = dz
    dg = dot_nt(dm, wdown[:block, :])
    for j in range(ff // block):
        cols = slice(j * block, (j + 1) * block)
        if (j + 1) * block < ff:
            dg_next = dot_nt(dm, wdown[(j + 1) * block : (j + 2) * block, :])
        du = (dg * gp_ref[:, cols].astype(F32)).astype(BF)
        du_ref[:, cols] = du
        upsum_ref[0:1, cols] += col_sum(du)
        total = total + dot_nt(du, wup[:, cols])
        dg = dg_next
    normed = n_ref[...].astype(F32)
    dz1 = norm_back(total * vec[GAIN1 : GAIN1 + 1, :], normed, r_ref[...])
    dz1_ref[...] = dz1
    db = dz1.astype(BF)
    db_ref[...] = db
    do_ref[...] = dot_nt(db, wout[...]).astype(BF)
    sums_ref[0:1, :] += col_sum(total * normed)
    sums_ref[1:2, :] += col_sum(total)
    sums_ref[2:3, :] += col_sum(db)


def feed_back_call(origin, dz, gp, n1, r1, vec, load):
    rows, width = dz.shape
    ff = gp.shape[1]
    n = load.count
    return pl.pallas_call(
        partial(feed_back_kernel, load, width, ff),
        grid=(rows // TILE,),
        in_specs=[SMEM, tile(TILE, width), tile(TILE, ff), tile(TILE, width), tile(TILE, 1), whole(vec.shape)] + [ANY] * n,
        out_specs=[
            tile(TILE, ff),
            tile(TILE, width),
            tile(TILE, width),
            tile(TILE, width),
            whole_out((8, width)),
            whole_out((8, ff)),
        ],
        out_shape=[
            jax.ShapeDtypeStruct((rows, ff), BF),
            jax.ShapeDtypeStruct((rows, width), F32),
            jax.ShapeDtypeStruct((rows, width), BF),
            jax.ShapeDtypeStruct((rows, width), BF),
            jax.ShapeDtypeStruct((8, width), F32),
            jax.ShapeDtypeStruct((8, ff), F32),
        ],
        scratch_shapes=load.scratch(),
        compiler_params=pltpu.CompilerParams(vmem_limit_bytes=VMEM_LIMIT),
        cost_estimate=cost(4 * rows * width * ff + 2 * rows * width * width, 4 * rows * ff),
        name="segment_feed_back",
    )(origin, dz, gp, n1, r1, vec, *load.arrays)


def spread(table, chips, cores, chunk, first_chip, count, source, outs, put):
    core = table[chips]
    for q in range(count):
        slot = table[first_chip + q]
        for c in range(cores):
            device = q * cores + (jnp.bitwise_xor(core, c) if cores > 1 else 0)
            start = pl.multiple_of(device * chunk, 16)
            put(outs[c], slot, source[pl.ds(start, chunk), :].astype(BF))


def once(shape):
    return pl.BlockSpec(shape, lambda i: (0,) * len(shape), pipeline_mode=pl.Buffered(1))


def grads_feed_kernel(chips, cores, chunk, width, group, *refs):
    table, g_ref, dm_ref, hb_ref, du_ref = refs[:5]
    outs = refs[5 : 5 + cores]
    scratch = refs[5 + cores]
    step = pl.program_id(0)

    @pl.when(step < group)
    def _():
        scratch[...] = dot_tn(g_ref[...], dm_ref[...])
        if chips > 1:
            per = width // (chunk * group * cores)
            core = table[chips]
            for q in range(per):
                slot = table[step * per + q]
                for c in range(cores):
                    device = q * cores + jnp.bitwise_xor(core, c)
                    for j in range(group):
                        start = pl.multiple_of((device * group + j) * chunk, 16)
                        outs[c][slot, :, j * width : (j + 1) * width] = scratch[pl.ds(start, chunk), :].astype(BF)
        else:
            outs[0][0, :, pl.ds(pl.multiple_of(step * width, width), width)] = scratch[...].astype(BF)

    @pl.when(step >= group)
    def _():
        scratch[...] = dot_tn(hb_ref[...], du_ref[...])
        cols = pl.ds(pl.multiple_of(step * width, width), width)

        def put(out, slot, values):
            out[slot, :, cols] = values

        spread(table, chips, cores, chunk, 0, chips, scratch, outs, put)


def grads_feed_call(table, g, dm, hb, du, chips, cores, chunk):
    rows, ff = g.shape
    width = dm.shape[1]
    group = ff // width
    return pl.pallas_call(
        partial(grads_feed_kernel, chips, cores, chunk, width, group),
        grid=(2 * group,),
        in_specs=[
            SMEM,
            pl.BlockSpec((rows, width), lambda i: (0, jnp.minimum(i, group - 1))),
            whole((rows, width)),
            whole((rows, width)),
            pl.BlockSpec((rows, width), lambda i: (0, jnp.maximum(i - group, 0))),
        ],
        out_specs=[once((chips, chunk, 2 * ff))] * cores,
        out_shape=[jax.ShapeDtypeStruct((chips, chunk, 2 * ff), BF)] * cores,
        scratch_shapes=[pltpu.VMEM((width, width), F32)],
        compiler_params=pltpu.CompilerParams(vmem_limit_bytes=VMEM_LIMIT),
        cost_estimate=cost(4 * rows * width * ff, 4 * rows * ff + 4 * width * ff),
        name="grads_feed",
    )(table, g, dm, hb, du)


def grads_out_kernel(chips, cores, chunk, *refs):
    table, o_ref, db_ref = refs[:3]
    outs = refs[3 : 3 + cores]
    scratch = refs[3 + cores]
    scratch[...] = dot_tn(o_ref[...], db_ref[...])

    def put(out, slot, values):
        out[slot] = values

    spread(table, chips, cores, chunk, 0, chips, scratch, outs, put)


def grads_out_call(table, o, db, chips, cores, chunk):
    width = o.shape[1]
    full = pl.BlockSpec(memory_space=pltpu.VMEM)
    return pl.pallas_call(
        partial(grads_out_kernel, chips, cores, chunk),
        in_specs=[SMEM, full, full],
        out_specs=[full] * cores,
        out_shape=[jax.ShapeDtypeStruct((chips, chunk, width), BF)] * cores,
        scratch_shapes=[pltpu.VMEM((width, width), F32)],
        compiler_params=pltpu.CompilerParams(vmem_limit_bytes=VMEM_LIMIT),
        cost_estimate=cost(2 * o.shape[0] * width * width, 8 * width * width),
        name="grads_out",
    )(table, o, db)


def attention_back_kernel(chips, cores, chunk, width, group, *refs):
    table, qkv_ref, a_ref, do_ref, x_ref, do_first, sums1, sums2, up_sums = refs[:9]
    dqkv, sums_ref = refs[9:11]
    outs = refs[11 : 11 + cores]
    total, d_o = refs[11 + cores :]
    step = pl.program_id(0)

    @pl.when(step == 0)
    def _():
        total[...] = jnp.zeros_like(total)
        sums_ref[...] = jnp.zeros_like(sums_ref)

    d_o[...] = do_ref[...].astype(F32)
    for s in range(TILE // SEG):
        at = pl.ds(table[chips + 1] + step * (TILE // SEG) + s, 1)
        d_o[s * SEG : s * SEG + 1, :] = do_first[at, :]
    for s in range(TILE // SEG):
        rows = pl.ds(s * SEG, SEG)
        pairs = range(width // 128)
        q = [qkv_ref[rows, pl.ds(p * 128, 128)] for p in pairs]
        k = [qkv_ref[rows, pl.ds(width + p * 128, 128)] for p in pairs]
        v = [qkv_ref[rows, pl.ds(2 * width + p * 128, 128)] for p in pairs]
        w = [a_ref[s, p] for p in pairs]
        d_out = [d_o[rows, pl.ds(p * 128, 128)].astype(BF) for p in pairs]
        for p, (d_q, d_k, d_v) in enumerate(pairs_backward(q, k, v, w, d_out)):
            dqkv[rows, pl.ds(p * 128, 128)] = d_q
            dqkv[rows, pl.ds(width + p * 128, 128)] = d_k
            dqkv[rows, pl.ds(2 * width + p * 128, 128)] = d_v
    sums_ref[0:1, :] += col_sum(dqkv[:, 2 * width :])
    total[...] += dot_tn(x_ref[...], dqkv[...])

    @pl.when(step == pl.num_programs(0) - 1)
    def _():
        def put(out, slot, values):
            out[slot, :, : 3 * width] = values

        spread(table, chips, cores, chunk, 0, chips, total, outs, put)
        if cores > 1:
            vec = [sums1[0:1], sums2[0:1], sums_ref[0:1], sums1[2:3], sums2[2:3], sums1[1:2], sums2[1:2]]
            vec = jnp.concatenate(vec + [jnp.zeros((1, width), F32)], axis=0)
            pad = jnp.zeros((chunk - UP0 - group, chunk), F32)
            for q in range(chips):
                blocks = []
                for device in (2 * q, 2 * q + 1):
                    own = slice(device * chunk, (device + 1) * chunk)
                    ups = [up_sums[0:1, group * chunk * device + chunk * j : group * chunk * device + chunk * (j + 1)] for j in range(group)]
                    block = jnp.concatenate([vec[:UP0, own]] + ups + [pad], axis=0)
                    blocks.append(jnp.concatenate([block, jnp.zeros((chunk, 128 - chunk), F32)], axis=1))
                for c in range(2):
                    picked = jnp.where(table[chips] == c, blocks[0], blocks[1]).astype(BF)
                    outs[c][table[q], :, 3 * width :] = picked


def attention_back_call(table, qkv, a, do, x, do_first, sums1, sums2, up_sums, chips, cores, chunk):
    rows, width = x.shape
    pairs = width // 128
    cols = 3 * width + (128 if cores > 1 else 0)
    group = up_sums.shape[1] // width
    return pl.pallas_call(
        partial(attention_back_kernel, chips, cores, chunk, width, group),
        grid=(rows // TILE,),
        in_specs=[
            SMEM,
            tile(TILE, 3 * width),
            tile(TILE // SEG, pairs, 2 * SEG, SEG),
            tile(TILE, width),
            tile(TILE, width),
            whole(do_first.shape),
            whole(sums1.shape),
            whole(sums2.shape),
            whole(up_sums.shape),
        ],
        out_specs=[tile(TILE, 3 * width), whole_out((8, width))] + [once((chips, chunk, cols))] * cores,
        out_shape=[jax.ShapeDtypeStruct((rows, 3 * width), BF), jax.ShapeDtypeStruct((8, width), F32)]
        + [jax.ShapeDtypeStruct((chips, chunk, cols), BF)] * cores,
        scratch_shapes=[pltpu.VMEM((width, 3 * width), F32), pltpu.VMEM((TILE, width), F32)],
        compiler_params=pltpu.CompilerParams(vmem_limit_bytes=VMEM_LIMIT),
        cost_estimate=cost(2 * rows * width * 5 * width, 20 * rows * width),
        name="segment_attention_back",
    )(table, qkv, a, do, x, do_first, sums1, sums2, up_sums)


def input_grad_kernel(load, width, *refs):
    n = load.count
    origin, table, dqkv_ref, dz_ref, dz_first = refs[:5]
    srcs = refs[5 : 5 + n]
    dx_ref, d_z = refs[5 + n : 7 + n]
    scratch = refs[7 + n :]
    step = pl.program_id(0)

    @pl.when(step == 0)
    def _():
        for wait in load.start(srcs, origin, scratch):
            wait()

    d_z[...] = dz_ref[...]
    for s in range(TILE // SEG):
        at = pl.ds(table[0] + step * (TILE // SEG) + s, 1)
        d_z[s * SEG : s * SEG + 1, :] = dz_first[at, :]
    dx_ref[...] = (d_z[...] + dot_nt(dqkv_ref[...], scratch[0][...])).astype(BF)


def input_grad_call(origin, first_row, dqkv, dz, dz_first, load):
    rows, width = dz.shape
    n = load.count
    return pl.pallas_call(
        partial(input_grad_kernel, load, width),
        grid=(rows // TILE,),
        in_specs=[SMEM, SMEM, tile(TILE, 3 * width), tile(TILE, width), whole(dz_first.shape)] + [ANY] * n,
        out_specs=tile(TILE, width),
        out_shape=jax.ShapeDtypeStruct((rows, width), BF),
        scratch_shapes=[pltpu.VMEM((TILE, width), F32)] + load.scratch(),
        compiler_params=pltpu.CompilerParams(vmem_limit_bytes=VMEM_LIMIT),
        cost_estimate=cost(2 * rows * width * 3 * width, 12 * rows * width),
        name="input_grad",
    )(origin, first_row, dqkv, dz, dz_first, *load.arrays)


def one_hot(rows, cols, base):
    r = lax.broadcasted_iota(jnp.int32, (rows, cols), 0)
    c = lax.broadcasted_iota(jnp.int32, (rows, cols), 1)
    return (r == c + base).astype(F32).astype(BF)


def window(ref, first, width, base, count):
    size = min(256, width)
    start = jnp.minimum((base // 128) * 128, width - size)
    values = ref[:, pl.ds(pl.multiple_of(start + first, 128), size)]
    return dot_nn(values.astype(BF), one_hot(size, count, base - start))


def few_feed_forward(hb, h, vec, up_row, wup, wdown, g_ref, gp_ref, ff, wait_up, wait_down):
    block = 512
    total = jnp.zeros(h.shape, F32)
    wait_up()
    for j in range(ff // block):
        cols = slice(j * block, (j + 1) * block)
        active, slope = gelu_both(dot_nn(hb, wup[:, cols]) + up_row[:, cols])
        g_ref[:, cols] = active.astype(BF)
        gp_ref[:, cols] = slope.astype(BF)
    wait_down()
    for j in range(ff // block):
        cols = slice(j * block, (j + 1) * block)
        total = total + dot_nn(g_ref[:, cols], wdown[cols, :])
    return norm_rows(h + total + vec[BIAS_D : BIAS_D + 1, :])


def few_backward(dy, n2, r2, n1, r1, vec, wup, wdown, wout, gp_ref, du_ref, ff, wait_down, wait_up, wait_out):
    block = 512
    dz = norm_back(dy * vec[GAIN2 : GAIN2 + 1, :], n2, r2)
    dm = dz.astype(BF)
    total = dz
    wait_down()
    for j in range(ff // block):
        cols = slice(j * block, (j + 1) * block)
        du_ref[:, cols] = (dot_nt(dm, wdown[cols, :]) * gp_ref[:, cols].astype(F32)).astype(BF)
    wait_up()
    for j in range(ff // block):
        cols = slice(j * block, (j + 1) * block)
        total = total + dot_nt(du_ref[:, cols], wup[:, cols])
    dz1 = norm_back(total * vec[GAIN1 : GAIN1 + 1, :], n1, r1)
    db = dz1.astype(BF)
    wait_out()
    return dm, total, dz1, db, dot_nt(db, wout[...])


def few_grads(me, chunk, ff, hb, o, g_ref, du_ref, dm, db, sums, wide, grads):
    block = 512
    width = dm.shape[1]
    group = ff // width
    base = me * chunk
    own_h = window(*hb, width, base, chunk).astype(BF)
    own_o = window(*o, width, base, chunk).astype(BF)
    own_g = window(g_ref, 0, ff, base * group, group * chunk).astype(BF)
    down = dot_tn(own_g, dm).astype(BF)
    for j in range(group):
        grads[:, j * width : (j + 1) * width] = down[j * chunk : (j + 1) * chunk]
    for j in range(ff // block):
        cols = slice(j * block, (j + 1) * block)
        grads[:, ff + j * block : ff + (j + 1) * block] = dot_tn(own_h, du_ref[:, cols]).astype(BF)
    grads[:, 2 * ff : 2 * ff + width] = dot_tn(own_o, db).astype(BF)
    wide[...] = jnp.zeros_like(wide)
    for i, x in enumerate(sums):
        if x is not None:
            wide[i : i + 1, :width] = x
    wide[8:9, :] = col_sum(du_ref[...])
    own_sums = window(wide, 0, width, base, chunk)
    own_up = window(wide, 0, ff, base * group, group * chunk)
    ups = [own_up[8:9, j * chunk : (j + 1) * chunk] for j in range(group)]
    return jnp.concatenate([own_sums[:UP0]] + ups + [jnp.zeros((VEC_ROWS - UP0 - group, chunk), F32)], axis=0)


def cross_kernel(load, width, ff, chunk, places_n, *refs):
    n = load.count
    origin, table, pay_ref, doc_col, doc_row, tab_ref, vec, upb = refs[:8]
    srcs = refs[8 : 8 + n]
    out_ref, dx_ref, grads, sums_ref, gtab_ref = refs[8 + n : 13 + n]
    qkv, a_ref, o_s, d_s, g_ref, gp_ref, du_ref, low_ref, hb_ref, wide, tab_own = refs[13 + n : 24 + n]
    scratch = refs[24 + n :]
    wqkv, wout, wup, wdown = scratch[:4]
    rows = pay_ref.shape[0]
    me = table[0]
    wait_qkv, wait_out, wait_up, wait_down = load.start(srcs, origin, scratch)
    same = doc_col[...] == doc_row[...]
    earlier = lax.broadcasted_iota(jnp.int32, (rows, rows), 0) > lax.broadcasted_iota(jnp.int32, (rows, rows), 1)
    position = jnp.sum(jnp.where(same & earlier, 1.0, 0.0), axis=1, keepdims=True)
    slot = lax.broadcasted_iota(jnp.int32, (rows, places_n), 1).astype(F32)
    lookup = (slot == position).astype(F32).astype(BF)
    entry = pay_ref[:, :width] + dot_nn(lookup, tab_ref[...].astype(BF))
    low = entry.astype(BF)
    low_ref[...] = low
    allowed = jnp.concatenate([same, same], axis=0)
    wait_qkv()
    proj = dot_nn(low, wqkv[...])
    qkv[:, : 2 * width] = proj[:, : 2 * width].astype(BF)
    qkv[:, 2 * width :] = (proj[:, 2 * width :] + vec[BIAS_V : BIAS_V + 1, :]).astype(BF)
    pairs = range(width // 128)

    def lanes(ref, p, first=0):
        return ref[:, first + p * 128 : first + (p + 1) * 128]

    together = len(pairs) if rows <= 128 else 1
    for at in range(0, len(pairs), together):
        some = range(at, at + together)
        q = [lanes(qkv, p) for p in some]
        k = [lanes(qkv, p, width) for p in some]
        v = [lanes(qkv, p, 2 * width) for p in some]
        for p, (weights, out) in zip(some, pairs_forward(q, k, v, allowed)):
            a_ref[p] = weights
            o_s[:, p * 128 : (p + 1) * 128] = out
    wait_out()
    o = o_s[...]
    n1, r1 = norm_rows(entry + dot_nn(o, wout[...]) + vec[BIAS_O : BIAS_O + 1, :])
    h = n1 * vec[GAIN1 : GAIN1 + 1, :] + vec[SHIFT1 : SHIFT1 + 1, :]
    hb = h.astype(BF)
    n2, r2 = few_feed_forward(hb, h, vec, upb.at[1:2, :], wup, wdown, g_ref, gp_ref, ff, wait_up, wait_down)
    out_ref[...] = n2 * vec[GAIN2 : GAIN2 + 1, :] + vec[SHIFT2 : SHIFT2 + 1, :]
    dy = pay_ref[:, width:]

    def ready():
        return None

    hb_ref[...] = hb
    dm, total, dz1, db, do = few_backward(
        dy, n2, r2, n1, r1, vec, wup, wdown, wout, gp_ref, du_ref, ff, ready, ready, ready
    )
    do = do.astype(BF)
    for at in range(0, len(pairs), together):
        some = range(at, at + together)
        q = [lanes(qkv, p) for p in some]
        k = [lanes(qkv, p, width) for p in some]
        v = [lanes(qkv, p, 2 * width) for p in some]
        w = [a_ref[p] for p in some]
        d_out = [do[:, p * 128 : (p + 1) * 128] for p in some]
        for p, (d_q, d_k, d_v) in zip(some, pairs_backward(q, k, v, w, d_out)):
            d_s[:, p * 128 : (p + 1) * 128] = d_q
            d_s[:, width + p * 128 : width + (p + 1) * 128] = d_k
            d_s[:, 2 * width + p * 128 : 2 * width + (p + 1) * 128] = d_v
    d_all = d_s[...]
    d_in = dz1 + dot_nt(d_all, wqkv[...])
    dx_ref[...] = d_in
    dv = col_sum(d_all[:, 2 * width :])
    sums = [col_sum(total * n1), col_sum(dy * n2), dv, col_sum(db), col_sum(dm), col_sum(total), col_sum(dy)]
    sums = few_grads(me, chunk, ff, (hb_ref, 0), (o_s, 0), g_ref, du_ref, dm, db, sums, wide, grads)
    base = 2 * ff + width
    own_low = window(low_ref, 0, width, me * chunk, chunk).astype(BF)
    grads[:, base : base + 3 * width] = dot_tn(own_low, d_all).astype(BF)
    high = d_in.astype(BF)
    rest = (d_in - high.astype(F32)).astype(BF)
    tab_own[...] = dot_tn(lookup, high) + dot_tn(lookup, rest)
    own_tab = window(tab_own, 0, width, me * chunk, chunk)
    sums_ref[...] = sums
    gtab_ref[...] = own_tab
    if grads.shape[1] > base + 3 * width:
        high = 2 * VEC_ROWS
        gap = jnp.zeros((chunk, 64 - chunk), F32)
        left = jnp.concatenate([sums, jnp.zeros((VEC_ROWS, chunk), F32), own_tab[: chunk - high]], axis=0)
        grads[:, base + 3 * width :] = jnp.concatenate([left, gap, own_tab[chunk - high :], gap], axis=1).astype(BF)


def cross_call(origin, table, pay, docs, tab, vec, upb, load, ff, chunk, extra):
    rows, width = pay.shape[0], vec.shape[1]
    n = load.count
    group = ff // width
    pairs = width // 128
    full = pl.BlockSpec(memory_space=pltpu.VMEM)
    return pl.pallas_call(
        partial(cross_kernel, load, width, ff, chunk, tab.shape[0]),
        in_specs=[SMEM, SMEM] + [full] * 6 + [ANY] * n,
        out_specs=[full] * 5,
        out_shape=[
            jax.ShapeDtypeStruct((rows, width), F32),
            jax.ShapeDtypeStruct((rows, width), F32),
            jax.ShapeDtypeStruct((chunk, 2 * ff + 4 * width + extra), BF),
            jax.ShapeDtypeStruct((VEC_ROWS, chunk), F32),
            jax.ShapeDtypeStruct((tab.shape[0], chunk), F32),
        ],
        scratch_shapes=[
            pltpu.VMEM((rows, 3 * width), BF),
            pltpu.VMEM((pairs, 2 * rows, rows), BF),
            pltpu.VMEM((rows, width), BF),
            pltpu.VMEM((rows, 3 * width), BF),
            pltpu.VMEM((rows, ff), BF),
            pltpu.VMEM((rows, ff), BF),
            pltpu.VMEM((rows, ff), BF),
            pltpu.VMEM((rows, width), BF),
            pltpu.VMEM((rows, width), BF),
            pltpu.VMEM((VEC_ROWS, ff), F32),
            pltpu.VMEM((tab.shape[0], width), F32),
        ]
        + load.scratch(),
        compiler_params=pltpu.CompilerParams(vmem_limit_bytes=VMEM_LIMIT),
        cost_estimate=cost(16 * rows * width * ff, 20 * width * width),
        name="cross_block",
    )(origin, table, pay, docs.reshape(rows, 1), docs.reshape(1, rows), tab, vec, upb, *load.arrays)


def first_forward_kernel(load, pay_pieces, width, ff, *refs):
    n, m = load.count, len(pay_pieces.arrays)
    origin, pay_origin, vec, upb = refs[:4]
    srcs = refs[4 : 4 + n]
    pay_srcs = refs[4 + n : 4 + n + m]
    cross_ref, pay_ref, g_ref, gp_ref, n_ref, r_ref = refs[4 + n + m : 10 + n + m]
    held, sem = refs[10 + n + m : 12 + n + m]
    scratch = refs[12 + n + m :]
    wup, wdown = scratch[:2]
    copies = pay_pieces.copies(pay_srcs, pay_origin, sem, 0, held.shape[2], held, by_origin=True)
    copies.start()
    wait_up, wait_down = load.start(srcs, origin, scratch)
    copies.wait()
    pay = held[...].astype(F32).reshape(pay_ref.shape[0], held.shape[2])
    cross_ref[...] = pay[:, : 2 * width]
    pay_ref[...] = pay[:, 2 * width :]
    hb = pay_ref[:, :width].astype(BF)
    normed, inverse = few_feed_forward(
        hb, hb.astype(F32), vec, upb.at[0:1, :], wup, wdown, g_ref, gp_ref, ff, wait_up, wait_down
    )
    n_ref[...] = normed
    r_ref[...] = inverse


def first_forward_call(origin, pay_origin, pay_pieces, vec, upb, load, ff):
    width = vec.shape[1]
    rows = pay_pieces.rows
    n, m = load.count, len(pay_pieces.arrays)
    full = pl.BlockSpec(memory_space=pltpu.VMEM)
    return pl.pallas_call(
        partial(first_forward_kernel, load, pay_pieces, width, ff),
        in_specs=[SMEM, SMEM] + [full] * 2 + [ANY] * (n + m),
        out_specs=[full] * 6,
        out_shape=[
            jax.ShapeDtypeStruct((rows, 2 * width), F32),
            jax.ShapeDtypeStruct((rows, pay_pieces.arrays[0].shape[1] - 2 * width), F32),
            jax.ShapeDtypeStruct((rows, ff), BF),
            jax.ShapeDtypeStruct((rows, ff), BF),
            jax.ShapeDtypeStruct((rows, width), F32),
            jax.ShapeDtypeStruct((rows, 1), F32),
        ],
        scratch_shapes=[
            pltpu.VMEM((pay_pieces.origins, pay_pieces.chunk, pay_pieces.arrays[0].shape[1]), BF),
            pltpu.SemaphoreType.DMA((pay_pieces.count,)),
        ]
        + load.scratch(),
        compiler_params=pltpu.CompilerParams(vmem_limit_bytes=VMEM_LIMIT),
        cost_estimate=cost(6 * rows * width * ff, 4 * width * ff),
        name="first_rows_forward",
    )(origin, pay_origin, vec, upb, *load.arrays, *pay_pieces.arrays)


def first_kernel(load, width, ff, *refs):
    n = load.count
    origin, pay_ref, dy_ref, gp_ref, n2_ref, r2_ref, vec = refs[:7]
    srcs = refs[7 : 7 + n]
    dz1_ref, do_ref, du_ref, dm_ref, db_ref, total_ref = refs[7 + n : 13 + n]
    scratch = refs[13 + n :]
    wdown, wup, wout = scratch[:3]
    waits = load.start(srcs, origin, scratch)
    n1 = pay_ref[:, 2 * width : 3 * width]
    r1 = jnp.sum(pay_ref[:, 3 * width :], axis=1, keepdims=True)
    dm, total, dz1, db, do = few_backward(
        dy_ref[...], n2_ref[...], r2_ref[...], n1, r1, vec, wup, wdown, wout, gp_ref, du_ref, ff, *waits
    )
    dm_ref[...] = dm
    db_ref[...] = db
    total_ref[...] = total
    dz1_ref[...] = dz1
    do_ref[...] = do


def first_call(origin, pay, dy, gp, n2, r2, vec, load):
    rows, width = dy.shape
    ff = gp.shape[1]
    n = load.count
    full = pl.BlockSpec(memory_space=pltpu.VMEM)
    return pl.pallas_call(
        partial(first_kernel, load, width, ff),
        in_specs=[SMEM] + [full] * 6 + [ANY] * n,
        out_specs=[full] * 6,
        out_shape=[
            jax.ShapeDtypeStruct((rows, width), F32),
            jax.ShapeDtypeStruct((rows, width), F32),
            jax.ShapeDtypeStruct((rows, ff), BF),
            jax.ShapeDtypeStruct((rows, width), BF),
            jax.ShapeDtypeStruct((rows, width), BF),
            jax.ShapeDtypeStruct((rows, width), F32),
        ],
        scratch_shapes=load.scratch(),
        compiler_params=pltpu.CompilerParams(vmem_limit_bytes=VMEM_LIMIT),
        cost_estimate=cost(8 * rows * width * ff, 4 * width * ff),
        name="first_rows_back",
    )(origin, pay, dy, gp, n2, r2, vec, *load.arrays)


def first_grads_kernel(width, ff, chunk, *refs):
    table, pay_ref, dy_ref, g_ref, n2_ref, du_ref, dm_ref, db_ref, total_ref, grads, sums_ref, wide = refs
    dm, db, total, dy = dm_ref[...], db_ref[...], total_ref[...], dy_ref[...]
    n1 = pay_ref[:, 2 * width : 3 * width]
    sums = [col_sum(total * n1), col_sum(dy * n2_ref[...]), None, col_sum(db), col_sum(dm), col_sum(total), col_sum(dy)]
    sums = few_grads(
        table[0], chunk, ff, (pay_ref, 0), (pay_ref, width), g_ref, du_ref, dm, db, sums, wide, grads
    )
    if sums_ref.shape[1] > chunk:
        sums = jnp.concatenate([sums, jnp.zeros((sums_ref.shape[0] - VEC_ROWS, chunk), F32)], axis=0)
        sums_ref[:, : sums_ref.shape[1] - 128] = jnp.zeros((sums_ref.shape[0], sums_ref.shape[1] - 128), BF)
        sums = jnp.concatenate([sums, jnp.zeros((sums_ref.shape[0], 128 - chunk), F32)], axis=1)
        sums_ref[:, sums_ref.shape[1] - 128 :] = sums.astype(BF)
    else:
        sums_ref[...] = sums


def first_grads_call(table, pay, dy, g, n2, du, dm, db, total, chunk, sums_shape):
    rows, width = dy.shape
    ff = g.shape[1]
    full = pl.BlockSpec(memory_space=pltpu.VMEM)
    return pl.pallas_call(
        partial(first_grads_kernel, width, ff, chunk),
        in_specs=[SMEM] + [full] * 8,
        out_specs=[full] * 2,
        out_shape=[jax.ShapeDtypeStruct((chunk, 2 * ff + width), BF), sums_shape],
        scratch_shapes=[pltpu.VMEM((VEC_ROWS, ff), F32)],
        compiler_params=pltpu.CompilerParams(vmem_limit_bytes=VMEM_LIMIT),
        cost_estimate=cost(2 * rows * width * ff // 4, 8 * rows * ff),
        name="first_rows_grads",
    )(table, pay, dy, g, n2, du, dm, db, total)


def vector_kernel(pieces, col, own, width, ff, *refs):
    n = len(pieces.arrays)
    origin = refs[0]
    srcs = refs[1 : 1 + n]
    vec0, vec1, tab, upb = refs[1 + n : 5 + n]
    held, sem = refs[5 + n :]
    copies = pieces.copies(srcs, origin, sem, col, 128, held, by_origin=True)
    copies.start()
    upb[...] = jnp.zeros_like(upb)
    copies.wait()
    high = 2 * VEC_ROWS
    group = ff // width
    for i in range(pieces.origins):
        block = held[i].astype(F32)
        cols = slice(own * i, own * (i + 1))
        vec0[:, cols] = block[:VEC_ROWS, :own]
        vec1[:, cols] = block[VEC_ROWS:high, :own]
        tab[: own - high, cols] = block[high:own, :own]
        tab[own - high :, cols] = block[:, 64 : 64 + own]
        for b in range(2):
            for j in range(group):
                at = group * own * i + own * j
                upb[b : b + 1, at : at + own] = block[b * VEC_ROWS + UP0 + j : b * VEC_ROWS + UP0 + j + 1, :own]


def vector_call(origin, pieces, col, own, width, ff, places_n):
    n = len(pieces.arrays)
    full = pl.BlockSpec(memory_space=pltpu.VMEM)
    return pl.pallas_call(
        partial(vector_kernel, pieces, col, own, width, ff),
        in_specs=[SMEM] + [ANY] * n,
        out_specs=[full] * 4,
        out_shape=[
            jax.ShapeDtypeStruct((VEC_ROWS, width), F32),
            jax.ShapeDtypeStruct((VEC_ROWS, width), F32),
            jax.ShapeDtypeStruct((places_n, width), F32),
            jax.ShapeDtypeStruct((8, ff), F32),
        ],
        scratch_shapes=[pltpu.VMEM((pieces.origins, own, 128), BF), pltpu.SemaphoreType.DMA((pieces.count,))],
        compiler_params=pltpu.CompilerParams(vmem_limit_bytes=VMEM_LIMIT),
        cost_estimate=cost(1000, 128 * width * 8),
        name="vectors",
    )(origin, *pieces.arrays)


def pack_kernel(own, width, ff, places_n, *refs):
    qkv, out, up, down, gains, biases, upb, table, first, feed, other, side = refs
    group = ff // width
    first[:, : 3 * width] = qkv[0]
    first[:, 3 * width : 4 * width] = out[0]
    other[:, : 3 * width] = qkv[1]
    other[:, 3 * width : 4 * width] = out[1]
    for b, (pack, at) in enumerate(((feed, 0), (other, 4 * width))):
        pack[:, at : at + ff] = up[b]
        for j in range(group):
            pack[:, at + ff + j * width : at + ff + (j + 1) * width] = down[b, j * own : (j + 1) * own, :]
    side[...] = jnp.zeros_like(side)
    for b in range(2):
        at = b * VEC_ROWS
        side[at : at + 2, :own] = gains[b].astype(F32)
        side[at + 2 : at + 7, :own] = biases[b].astype(F32)
        row = upb[...].astype(F32)[b : b + 1]
        for j in range(group):
            side[at + UP0 + j : at + UP0 + j + 1, :own] = row[:, j * own : (j + 1) * own]
    places = table[...].astype(F32)
    high = 2 * VEC_ROWS
    side[high:own, :own] = places[: own - high]
    side[:, 64 : 64 + own] = places[own - high :]
    first[:, 4 * width :] = side[...].astype(BF)


def pack_call(own, width, ff, qkv, out, up, down, gains, biases, upb, table):
    full = pl.BlockSpec(memory_space=pltpu.VMEM)
    return pl.pallas_call(
        partial(pack_kernel, own, width, ff, table.shape[0]),
        in_specs=[full] * 8,
        out_specs=[full] * 3,
        out_shape=[
            jax.ShapeDtypeStruct((own, 4 * width + 128), BF),
            jax.ShapeDtypeStruct((own, 2 * ff), BF),
            jax.ShapeDtypeStruct((own, 4 * width + 2 * ff), BF),
        ],
        scratch_shapes=[pltpu.VMEM((own, 128), F32)],
        compiler_params=pltpu.CompilerParams(vmem_limit_bytes=VMEM_LIMIT),
        cost_estimate=cost(1000, 8 * own * 8 * width),
        name="pack_weights",
    )(qkv, out, up, down, gains, biases, upb, table)


def sum_kernel(plan, widths, *refs):
    groups = len(widths)
    count = sum(2 * groups + len(more) for _, more in plan)
    at = 0
    for out, (shift, more) in zip(refs[count:], plan):
        slots = refs[at : at + 2 * groups]
        at += 2 * groups
        extra = [(ref, first) for ref, first in zip(refs[at : at + len(more)], more)]
        at += len(more)
        rows = out.shape[0]
        edges = sorted({0, rows} | {e for ref, first in extra for e in (first, first + ref.shape[0])})
        for low, high in zip(edges, edges[1:]):
            col = 0
            for g, width in enumerate(widths):
                value = slots[2 * g][0, shift + low : shift + high, :].astype(F32)
                value = value + slots[2 * g + 1][0, shift + low : shift + high, :].astype(F32)
                for ref, first in extra:
                    if first <= low and high <= first + ref.shape[0]:
                        value = value + ref[low - first : high - first, col : col + width].astype(F32)
                out[low:high, col : col + width] = value.astype(BF)
                col += width


def sum_call(groups, outputs):
    args, specs, plan, shapes = [], [], [], []
    widths = [x.shape[2] for x, _ in groups]
    for slot, shift, rows, more in outputs:
        for pair in groups:
            for x in pair:
                args.append(x)
                specs.append(pl.BlockSpec((1,) + x.shape[1:], lambda i, k=slot: (k, 0, 0)))
        for x, _ in more:
            args.append(x)
            specs.append(pl.BlockSpec(x.shape, lambda i: (0, 0)))
        plan.append((shift, [first for _, first in more]))
        shapes.append(jax.ShapeDtypeStruct((rows, sum(widths)), BF))
    return pl.pallas_call(
        partial(sum_kernel, plan, widths),
        grid=(1,),
        in_specs=specs,
        out_specs=[pl.BlockSpec(x.shape, lambda i: (0, 0)) for x in shapes],
        out_shape=shapes,
        compiler_params=pltpu.CompilerParams(vmem_limit_bytes=VMEM_LIMIT),
        cost_estimate=cost(1000, sum(8 * x.shape[0] * x.shape[1] for x in shapes)),
        name="add_pieces",
    )(*args)


def finish_kernel(ff, width, *refs):
    x0, y0, x1, y1, grad_up, grad_out, grad_down = refs
    own = x0.shape[0]
    for b, (x, y) in enumerate(((x0, y0), (x1, y1))):
        for j in range(ff // width):
            cols = slice(j * width, (j + 1) * width)
            grad_down[b, j * own : (j + 1) * own, :] = x[:, cols].astype(F32) + y[:, cols].astype(F32)
        grad_up[b] = x[:, ff : 2 * ff].astype(F32) + y[:, ff : 2 * ff].astype(F32)
        grad_out[b] = x[:, 2 * ff : 2 * ff + width].astype(F32) + y[:, 2 * ff : 2 * ff + width].astype(F32)


def finish_call(ff, width, *args):
    own = args[0].shape[0]
    full = pl.BlockSpec(memory_space=pltpu.VMEM)
    return pl.pallas_call(
        partial(finish_kernel, ff, width),
        in_specs=[full] * 4,
        out_specs=[full] * 3,
        out_shape=[
            jax.ShapeDtypeStruct((2, own, ff), F32),
            jax.ShapeDtypeStruct((2, own, width), F32),
            jax.ShapeDtypeStruct((2, own * ff // width, width), F32),
        ],
        compiler_params=pltpu.CompilerParams(vmem_limit_bytes=VMEM_LIMIT),
        cost_estimate=cost(1000, 16 * own * (2 * ff + width)),
        name="finish_feed",
    )(*args)


def finish_last_kernel(own, width, group, places_n, *refs):
    q0, q0s, q1, q1s, grad_qkv, grad_gains, grad_biases, grad_up_bias, grad_table = refs
    blocks = []
    for b, (x, y) in enumerate(((q0, q0s), (q1, q1s))):
        at = x.shape[1] - 3 * width - 128
        cols = slice(at, at + 3 * width)
        grad_qkv[b] = x[:, cols].astype(F32) + y[:, cols].astype(F32)
        blocks.append(x[:, at + 3 * width :].astype(F32) + y[:, at + 3 * width :].astype(F32))
    for b, block in enumerate(blocks):
        grad_gains[b] = block[:2, :own]
        grad_biases[b] = block[2:7, :own]
        for j in range(group):
            grad_up_bias[b : b + 1, j * own : (j + 1) * own] = block[UP0 + j : UP0 + j + 1, :own]
    high = 2 * VEC_ROWS
    grad_table[: own - high, :] = blocks[1][high:own, :own]
    grad_table[own - high :, :] = blocks[1][:, 64 : 64 + own]


def finish_last_call(own, width, group, places_n, *args):
    full = pl.BlockSpec(memory_space=pltpu.VMEM)
    return pl.pallas_call(
        partial(finish_last_kernel, own, width, group, places_n),
        in_specs=[full] * 4,
        out_specs=[full] * 5,
        out_shape=[
            jax.ShapeDtypeStruct((2, own, 3 * width), F32),
            jax.ShapeDtypeStruct((2, 2, own), F32),
            jax.ShapeDtypeStruct((2, 5, own), F32),
            jax.ShapeDtypeStruct((2, group * own), F32),
            jax.ShapeDtypeStruct((places_n, own), F32),
        ],
        compiler_params=pltpu.CompilerParams(vmem_limit_bytes=VMEM_LIMIT),
        cost_estimate=cost(1000, 48 * own * width),
        name="finish_qkv",
    )(*args)


def tie(x, *others):
    return lax.optimization_barrier((x, others))[0] if others else x


class Ring:
    def __init__(self, shards):
        chips = shards // 2
        self.shards, self.chips = shards, chips
        self.order = list(range(0, chips, 2)) + list(range(chips - 1, 0, -2))
        self.place = {chip: i for i, chip in enumerate(self.order)}

    def shift(self, by):
        pairs = []
        for i, chip in enumerate(self.order):
            to = self.order[(i + by) % self.chips]
            pairs += [(2 * chip, 2 * to), (2 * chip + 1, 2 * to + 1)]
        return pairs

    def forward(self, x):
        return lax.ppermute(x, "shard", self.shift(1))

    def backward(self, x):
        return lax.ppermute(x, "shard", self.shift(-1))

    def sibling(self, x):
        return lax.ppermute(x, "shard", [(i, i ^ 1) for i in range(self.shards)])

    def behind_table(self):
        return [
            [self.order[(self.place[d // 2] - k) % self.chips] for k in range(self.chips)] for d in range(self.shards)
        ]

    def slot_table(self):
        rows = []
        for d in range(self.shards):
            chip = d // 2
            rows.append([(self.place[q] - self.place[chip]) % self.chips for q in range(self.chips)] + [d % 2])
        return rows


def half_of(rows):
    return (rows // 32) * 16 if rows >= 32 else rows


class Gather:
    def __init__(self, ring, x):
        self.ring, self.steps = ring, 0
        self.ahead = self.behind = x
        self.rows = x.shape[0]
        self.entries, self.pending = [], []

    def take(self, *others):
        values = (self.ahead, self.behind, [e[0] for e in self.pending])
        ahead, behind, shared = tie(values, *others)
        for e, x in zip(self.pending, shared):
            self.entries.append((x,) + e[1:])
        self.sent = (ahead, behind)
        far = self.ring.chips // 2
        if self.steps == 0:
            fresh = [(ahead, 0, 0)]
        elif self.steps < far:
            fresh = [(ahead, self.steps, 0), (behind, self.ring.chips - self.steps, 0)]
        else:
            fresh = [(ahead, far, 0), (behind, far, half_of(self.rows))]
        self.entries += [(x, 2 * back, first, 0, x.shape[0]) for x, back, first in fresh]
        return ahead, behind, fresh

    def share(self, fresh):
        self.pending = [(self.ring.sibling(x), 2 * back + 1, first, 0, x.shape[0]) for x, back, first in fresh]

    def step(self, *others):
        self.take_arrived(*others)
        self.send()
        self.share_arrived()

    def take_arrived(self, *others):
        self.ahead, self.behind, self.fresh = self.take(*others)
        self.steps += 1

    def share_arrived(self, others=()):
        self.share([(tie(x, *others), back, first) for x, back, first in self.fresh])

    def send(self, *others):
        ahead, behind = tie((self.ahead, self.behind), *others)
        self.sent = (ahead, behind)
        half = half_of(self.rows)
        last = self.steps == self.ring.chips // 2
        self.ahead = self.ring.forward(ahead[:half] if last else ahead)
        self.behind = self.ring.backward(behind[half:] if last else behind)

    def finish(self, *others):
        self.share(self.take(*others)[2])
        return Pieces(self.entries + self.pending, self.rows, self.ring.shards)


class Exchange:
    def __init__(self, ring, x, bits):
        self.ring, self.rows, self.bits = ring, x.shape[0], bits
        self.parts, self.new, self.masks = [], [x], [0]

    def take(self, *others):
        self.parts, new = tie((self.parts, self.new), *others)
        self.parts = list(self.parts) + list(new)
        if len(self.masks) == 2:
            self.parts = [jnp.stack(self.parts).reshape(2 * self.rows, -1)]

    def step(self, *others):
        bit = self.bits[len(self.masks).bit_length() - 1]
        self.take(*others)
        self.sent = tuple(self.parts)
        pairs = [(d, d ^ (2 * bit)) for d in range(self.ring.shards)]
        self.new = [lax.ppermute(x, "shard", pairs) for x in self.parts]
        self.masks += [m ^ bit for m in self.masks]

    def finish(self, *others):
        self.take(*others)
        entries, at = [], 0
        for own in self.parts:
            other = self.ring.sibling(own)
            for i in range(own.shape[0] // self.rows):
                entries.append((own, at, 0, i * self.rows, self.rows))
                entries.append((other, len(self.masks) + at, 0, i * self.rows, self.rows))
                at += 1
        return Pieces(entries, self.rows, self.ring.shards)

    def origin_table(self, me):
        core = me % 2
        own = jnp.bitwise_xor(me // 2, jnp.asarray(self.masks, jnp.int32))
        return jnp.concatenate([2 * own + core, 2 * own + 1 - core])


class Reduce:
    def __init__(self, ring, *groups):
        self.ring, self.steps = ring, 0
        self.groups = list(groups)

    def step(self, *others):
        ring, far = self.ring, self.ring.chips // 2
        rows = self.groups[0][0].shape[1]
        half = half_of(rows)
        self.steps += 1
        k = far - self.steps + 1
        if self.steps == 1:
            groups = tie(self.groups, *others)
            outputs = [(far, 0, half, []), (far, half, rows - half, [])]
        else:
            groups, ahead, behind = tie((self.groups, self.ahead, self.behind), *others)
            first = half if self.steps == 2 else 0
            outputs = [(k, 0, rows, [(ahead, 0)]), (ring.chips - k, 0, rows, [(behind, first)])]
        self.sent = tuple(sum_call(groups, outputs))
        self.ahead = ring.forward(self.sent[0])
        self.behind = ring.backward(self.sent[1])

    def ahead_behind(self):
        return self.ahead, self.behind

    def result(self, more, *others):
        groups, ahead, behind = tie((self.groups, self.ahead, self.behind), *others)
        rows = groups[0][0].shape[1]
        return sum_call(groups, [(0, 0, rows, [(ahead, 0), (behind, 0), (more, 0)])])[0]


def swap_seq(x):
    return lax.ppermute(x, "seq", [(0, 1), (1, 0)])


def over_seq(x):
    low = x.astype(BF)
    return low.astype(F32) + swap_seq(low).astype(F32)


def body(
    tokens,
    qkv_weight,
    out_weight,
    up_weight,
    down_weight,
    norm_gains,
    biases,
    up_bias,
    position_table,
    segment_docs,
    cotangent,
):
    shards = lax.axis_size("shard")
    me = lax.axis_index("shard")
    rows, width = tokens.shape
    segs = rows // SEG
    ff = up_weight.shape[2]
    group = ff // width
    own = width // shards
    places_n = position_table.shape[0]
    docs = segment_docs[0]
    ringed = own == 48 and places_n == 64 and shards % 4 == 0
    ring = Ring(shards)
    place = me[None]

    if ringed:
        chips, cores, chunk = ring.chips, 2, own
        behind = jnp.asarray(ring.behind_table(), jnp.int32)[me]
        core = me % 2
        origin = jnp.stack([2 * behind + core, 2 * behind + 1 - core], axis=1).reshape(-1)
        table = jnp.concatenate([jnp.asarray(ring.slot_table(), jnp.int32)[me], (me * segs)[None]])
        first, feed, other = pack_call(
            own, width, ff, qkv_weight, out_weight, up_weight, down_weight, norm_gains, biases, up_bias, position_table
        )
        g_a, g_f, x_w = Gather(ring, first), Gather(ring, feed), Gather(ring, other)
        g_a.step()
        g_a.step()
        g_a.step()
        g_f.step(*g_a.sent)
        g_a.step()
        p_a = g_a.finish()
        g_f.step(*g_a.sent)
        vec0, vec1, tab, upb = vector_call(origin, p_a, 4 * width, own, width, ff, places_n)
        l_qkv, l_out = (p_a, 0, 3 * width), (p_a, 3 * width, width)
    else:
        chips, cores, chunk = 1, 1, width
        origin = jnp.zeros((1,), jnp.int32)
        table = jnp.stack([jnp.int32(0), jnp.int32(0), me * segs])
        full = [
            [lax.all_gather(w[b], "shard", axis=0, tiled=True) for w in (qkv_weight, out_weight, up_weight, down_weight)]
            for b in range(2)
        ]
        small = []
        for b in range(2):
            small += [norm_gains[b], biases[b], up_bias[b].reshape(group, own), jnp.zeros((VEC_ROWS - UP0 - group, own), BF)]
        small = jnp.concatenate(small + [position_table], axis=0)
        small_all = lax.all_gather(small, "shard", axis=1, tiled=True).astype(F32)
        vec0, vec1, tab = small_all[:VEC_ROWS], small_all[VEC_ROWS : 2 * VEC_ROWS], small_all[2 * VEC_ROWS :]
        upb = [
            v[UP0 : UP0 + group].reshape(group, shards, own).transpose(1, 0, 2).reshape(1, ff) for v in (vec0, vec1)
        ]
        upb = jnp.concatenate(upb + [jnp.zeros((6, ff), F32)], axis=0)

        def single(x):
            return Pieces([(x, 0, 0, 0, x.shape[0])], x.shape[0], 1)

        w0, w1 = [[(single(x), 0, x.shape[1]) for x in full[b]] for b in range(2)]
        l_qkv, l_out, l_up, l_down = w0

    def gated(x, *sent):
        return tie(x, *[y for z in sent for y in z]) if ringed else x

    gate = gated(origin, g_f.sent) if ringed else origin
    qkv = project_call(gate, tokens, vec0, Loader(l_qkv))
    if ringed:
        g_f.step(qkv)
        gate = gated(origin, g_f.sent)
    a, o, h, hb, n1, r1 = attention_call(gate, tokens, qkv, vec0, Loader(l_out))
    if ringed:
        g_f.step(o)
        x_w.step(*g_f.sent)
        p_f = g_f.finish()
        l_up, l_down = (p_f, 0, ff), (p_f, ff, width, group)
        gate = gated(origin, x_w.sent)
    y, g, gp, dz, dm, pay, sums2 = feed_call(gate, h, cotangent, o, n1, r1, vec0, upb, Loader(l_up, l_down), ff)

    pay = pay.astype(BF)
    gate = origin
    if ringed:
        exchange = Exchange(ring, pay, (1, 4, 2))
        exchange.step()
        x_w.step(dm)
        gate = gated(origin, exchange.sent, x_w.sent)
    du, dz1, db, do, sums1, up_sums = feed_back_call(gate, dz, gp, n1, r1, vec0, Loader(l_down, l_up, l_out))
    gate = table
    if ringed:
        exchange.step(du)
        x_w.step(du, *exchange.sent)
        gate = gated(table, exchange.sent, x_w.sent)
    main = list(grads_feed_call(tie(gate, du), g, dm, hb, du, chips, cores, chunk))
    gate = table
    if ringed:
        x_w.take_arrived(main[0])
        exchange.step(main[0], *x_w.sent)
        x_w.share_arrived(exchange.sent)
        main[1] = ring.sibling(tie(main[1], *exchange.sent))
        gate = gated(table, exchange.sent)
    main_o = list(grads_out_call(tie(gate, main[0]), o, db, chips, cores, chunk))
    gate = origin
    if ringed:
        p_p = exchange.finish(main_o[0])
        x_w.send(main_o[0], *p_p.arrays, *[e[0] for e in x_w.pending])
        main_o[1] = ring.sibling(tie(main_o[1], *x_w.sent))
        pay_origin = exchange.origin_table(me)
        gate = gated(origin, x_w.sent)
    else:
        p_p = single(lax.all_gather(pay, "shard", axis=0, tiled=True))
        pay_origin = origin

    pay_cross, pay_all, g_f, gp_f, n2_f, r2_f = first_forward_call(
        tie(gate, main_o[0]), pay_origin, p_p, vec0, upb, Loader(l_up, l_down), ff
    )
    gate = origin
    if ringed:
        r_m = Reduce(ring, tuple(main), tuple(main_o))
        r_m.step(g_f)
        p_x = x_w.finish(g_f)
        at = 4 * width
        w1 = (p_x, 0, 3 * width), (p_x, 3 * width, width), (p_x, at, ff), (p_x, at + ff, width, group)
        gate = gated(origin, r_m.sent)
    cross_out, d_cross, c_all, c_sums, c_tab = cross_call(
        tie(gate, g_f), place, pay_cross, docs, tab, vec1, upb, Loader(*w1), ff, own, 128 if ringed else 0
    )
    gate = origin
    if ringed:
        r_m.step(d_cross)
        c_swap = swap_seq(tie(c_all, *r_m.sent))
        gate = gated(origin, r_m.sent)
    dz1_first, do_first, du_f, dm_f, db_f, total_f = first_call(
        gate, pay_all, d_cross, gp_f, n2_f, r2_f, vec0, Loader(l_down, l_up, l_out)
    )
    gate = table
    if ringed:
        r_m.step(do_first, c_swap)
        gate = gated(table, r_m.sent)
    dqkv, sums_v, *tail = attention_back_call(
        gate, qkv, a, do, tokens, do_first, sums1, sums2, up_sums, chips, cores, chunk
    )
    gate = origin
    if ringed:
        tail[1] = ring.sibling(tie(tail[1], *r_m.ahead_behind()))
        r_m.step(tail[0])
        r_q = Reduce(ring, tuple(tail))
        r_q.step(*r_m.sent)
        gate = gated(origin, r_q.sent)
    d_tokens = input_grad_call(gate, table[-1:], dqkv, dz1, dz1_first, Loader(l_qkv))
    sent = ()
    if ringed:
        r_q.step(d_tokens)
        sent = r_q.sent
    sums_shape = jax.ShapeDtypeStruct((own, 3 * width + 128), BF) if ringed else jax.ShapeDtypeStruct((VEC_ROWS, own), F32)
    f_all, f_sums = first_grads_call(
        gated(place, sent), pay_all, d_cross, g_f, n2_f, du_f, dm_f, db_f, total_f, own, sums_shape
    )
    if ringed:
        m_all = r_m.result(f_all)
        r_q.step(m_all)
        m_swap = swap_seq(tie(m_all, *r_q.sent))
        y, cross_out = tie((y, cross_out), *r_q.sent)
    own_rows = lax.dynamic_slice_in_dim(cross_out, me * segs, segs, 0)
    merged = y.reshape(segs, SEG, width).at[:, 0, :].set(own_rows.astype(BF)).reshape(rows, width)
    if ringed:
        r_q.step()
        grad_up, grad_out, grad_down = finish_call(ff, width, m_all, tie(m_swap, *r_q.sent), c_all, c_swap)
        q_all = r_q.result(f_sums)
        grad_qkv, grad_gains, grad_biases, grad_up_bias, grad_table = finish_last_call(
            own, width, group, places_n, q_all, swap_seq(q_all), c_all, c_swap
        )
    else:

        def scattered(x):
            return lax.psum_scatter(x, "shard", scatter_dimension=0, tiled=True)

        def blocks(x):
            return jnp.concatenate([x[:, j * width : (j + 1) * width] for j in range(group)], axis=0)

        feed_sum, main_u, q_sum = main[0][0], scattered(jnp.concatenate([main[0][0][:, ff:], main_o[0][0]], axis=1)), scattered(tail[0][0])
        main_d = scattered(blocks(feed_sum[:, :ff]))
        c_down, c_feed, c_qkv = blocks(c_all[:, :ff]), c_all[:, ff : 2 * ff + width], c_all[:, 2 * ff + width :]
        grad_down = jnp.stack([over_seq(main_d.astype(F32) + blocks(f_all[:, :ff]).astype(F32)), over_seq(c_down)])
        both = jnp.stack([over_seq(main_u.astype(F32) + f_all[:, ff:].astype(F32)), over_seq(c_feed)])
        grad_up, grad_out = both[:, :, :ff], both[:, :, ff:]
        grad_qkv = jnp.stack([over_seq(q_sum), over_seq(c_qkv)])
        vec_sums = jnp.concatenate(
            [sums1[0:1], sums2[0:1], sums_v[0:1], sums1[2:3], sums2[2:3], sums1[1:2], sums2[1:2], jnp.zeros((1, width), F32)]
            + [up_sums[0].reshape(group, width)],
            axis=0,
        )
        vec_sums = lax.psum(vec_sums, ("seq", "shard"))
        seg_vec = lax.dynamic_slice_in_dim(vec_sums[:8], me * own, own, 1)
        seg_up = lax.dynamic_slice_in_dim(vec_sums[8:].reshape(ff), me * own * group, own * group, 0)
        few = over_seq(jnp.concatenate([f_sums, c_sums, c_tab], axis=0))
        first_vec, cross_vec, grad_table = few[:VEC_ROWS], few[VEC_ROWS : 2 * VEC_ROWS], few[2 * VEC_ROWS :]
        seg_vec = seg_vec + first_vec[:8]
        grad_gains = jnp.stack([seg_vec[:2], cross_vec[:2]])
        grad_biases = jnp.stack([seg_vec[2:7], cross_vec[2:7]])
        seg_up = seg_up + first_vec[UP0 : UP0 + group].reshape(-1)
        grad_up_bias = jnp.stack([seg_up, cross_vec[UP0 : UP0 + group].reshape(-1)])
    return (
        merged,
        d_tokens,
        grad_qkv,
        grad_out,
        grad_up,
        grad_down,
        grad_gains,
        grad_biases,
        grad_up_bias,
        grad_table,
    )


def solution(mesh):
    in_specs = (
        P(("seq", "shard"), None),
        P(None, "shard", None),
        P(None, "shard", None),
        P(None, "shard", None),
        P(None, "shard", None),
        P(None, None, "shard"),
        P(None, None, "shard"),
        P(None, "shard"),
        P(None, "shard"),
        P("seq", None),
        P(("seq", "shard"), None),
    )
    out_specs = (
        P(("seq", "shard"), None),
        P(("seq", "shard"), None),
        P(None, "shard", None),
        P(None, "shard", None),
        P(None, "shard", None),
        P(None, "shard", None),
        P(None, None, "shard"),
        P(None, None, "shard"),
        P(None, "shard"),
        P(None, "shard"),
    )
    return jax.shard_map(body, mesh=mesh, in_specs=in_specs, out_specs=out_specs, check_vma=False)
```

```python
from functools import partial

import jax
import jax.numpy as jnp
from jax import lax
from jax.experimental import pallas as pl
from jax.experimental.pallas import tpu as pltpu
from jax.sharding import PartitionSpec as P

HEAD = 64
SEG = 128
EPSILON = 1e-05
MASKED = -1e30
BF = jnp.bfloat16
F32 = jnp.float32
TILE = 256
VMEM_LIMIT = 67043328

GAIN1, GAIN2, BIAS_V, BIAS_O, BIAS_D, SHIFT1, SHIFT2, UP0 = 0, 1, 2, 3, 4, 5, 6, 7
VEC_ROWS = 16


def dot_nn(a, b):
    return lax.dot_general(a, b, (((1,), (0,)), ((), ())), preferred_element_type=F32)


def dot_nt(a, b):
    return lax.dot_general(a, b, (((1,), (1,)), ((), ())), preferred_element_type=F32)


def dot_tn(a, b):
    return lax.dot_general(a, b, (((0,), (0,)), ((), ())), preferred_element_type=F32)


def row_mean(x):
    return jnp.mean(x, axis=-1, keepdims=True)


def col_sum(x):
    return jnp.sum(x.astype(F32), axis=0, keepdims=True)


def norm_rows(z):
    centred = z - row_mean(z)
    inverse = lax.rsqrt(row_mean(centred * centred) + EPSILON)
    return centred * inverse, inverse


def norm_back(scaled, normed, inverse):
    return inverse * (scaled - row_mean(scaled) - normed * row_mean(scaled * normed))


def gelu_both(u):
    phi = 0.5 + 0.5 * lax.erf(u * (2.0**-0.5))
    return u * phi, phi + u * jnp.exp(-0.5 * u * u) * 0.3989422804014327


def halves(pair):
    lane = lax.broadcasted_iota(jnp.int32, pair.shape, 1)
    zero = jnp.zeros_like(pair)
    return jnp.concatenate([jnp.where(lane < HEAD, pair, zero), jnp.where(lane < HEAD, zero, pair)], axis=0)


def side_by_side(stacked):
    rows = stacked.shape[0] // 2
    return jnp.concatenate([stacked[:rows], stacked[rows:]], axis=1)


def pairs_forward(q, k, v, allowed):
    scores = [dot_nt(halves(a), b) * (HEAD**-0.5) for a, b in zip(q, k)]
    if allowed is not None:
        scores = [jnp.where(allowed, x, MASKED) for x in scores]
    powers = [jnp.exp(x - jnp.max(x, axis=-1, keepdims=True)) for x in scores]
    weights = [(x / jnp.sum(x, axis=-1, keepdims=True)).astype(BF) for x in powers]
    return [(w, dot_nn(side_by_side(w), halves(x)).astype(BF)) for w, x in zip(weights, v)]


def pairs_backward(q, k, v, weights, d_out):
    d_stacks = [halves(x) for x in d_out]
    d_weights = [dot_nt(x, y) for x, y in zip(d_stacks, v)]
    wide = [w.astype(F32) for w in weights]
    inner = [jnp.sum(w * x, axis=-1, keepdims=True) for w, x in zip(wide, d_weights)]
    d_scores = [(w * (x - y)).astype(BF) for w, x, y in zip(wide, d_weights, inner)]
    scale = HEAD**-0.5
    d_q = [(dot_nn(side_by_side(x), halves(y)) * scale).astype(BF) for x, y in zip(d_scores, k)]
    d_k = [(dot_tn(x, halves(y)) * scale).astype(BF) for x, y in zip(d_scores, q)]
    d_v = [dot_tn(w, x).astype(BF) for w, x in zip(weights, d_stacks)]
    return zip(d_q, d_k, d_v)


class Copies:
    def __init__(self, copies):
        self.all = copies

    def start(self):
        start_all(self.all)

    def wait(self):
        wait_all(self.all)


class Pieces:
    def __init__(self, entries, chunk, origins):
        self.entries = list(entries)
        self.chunk, self.origins = chunk, origins
        self.rows = chunk * origins
        self.count = len(self.entries)
        self.arrays, self.which = [], []
        for x, *_ in self.entries:
            at = [i for i, y in enumerate(self.arrays) if y is x]
            if not at:
                self.arrays.append(x)
            self.which.append(at[0] if at else len(self.arrays) - 1)

    def copies(self, refs, origin, sems, col, width, dst, by_origin=False, blocks=1):
        def build(refs, entries, sem0):
            out = []
            for n, (ref, (x, entry, first, top, rows)) in enumerate(zip(refs, entries)):
                for j in range(blocks):
                    if by_origin:
                        to = dst.at[origin[entry], pl.ds(first, rows), :]
                    else:
                        start = (origin[entry] * blocks + j) * self.chunk + first
                        to = dst.at[pl.ds(pl.multiple_of(start, 16 if rows % 16 == 0 else 8), rows), :]
                    source = ref.at[pl.ds(top, rows), pl.ds(col + j * width, width)]
                    out.append(pltpu.make_async_copy(source, to, sems.at[(sem0 + n) * blocks + j]))
            return out

        return Copies(build([refs[i] for i in self.which], self.entries, 0))


class Loader:
    def __init__(self, *items):
        self.items = [(*item, 1)[:4] for item in items]
        self.groups = []
        for pieces, *_ in items:
            if pieces not in self.groups:
                self.groups.append(pieces)
        self.arrays = [x for g in self.groups for x in g.arrays]
        self.count = len(self.arrays)

    def scratch(self):
        buffers = [pltpu.VMEM((p.rows * blocks, width), BF) for p, _, width, blocks in self.items]
        return buffers + [pltpu.SemaphoreType.DMA((p.count * blocks,)) for p, _, _, blocks in self.items]

    def start(self, srcs, origin, scratch):
        at, where = 0, {}
        for g in self.groups:
            where[id(g)] = srcs[at : at + len(g.arrays)]
            at += len(g.arrays)
        m = len(self.items)
        sets = [
            p.copies(where[id(p)], origin, scratch[m + i], col, width, scratch[i], blocks=blocks)
            for i, (p, col, width, blocks) in enumerate(self.items)
        ]
        for copies in sets:
            copies.start()
        return [copies.wait for copies in sets]


def start_all(copies):
    for c in copies:
        c.start()


def wait_all(copies):
    for c in copies:
        c.wait()


ANY = pl.BlockSpec(memory_space=pl.ANY)
SMEM = pl.BlockSpec(memory_space=pltpu.SMEM)


def whole(shape):
    return pl.BlockSpec(shape, lambda *i: (0,) * len(shape), pipeline_mode=pl.Buffered(1))


def whole_out(shape):
    return pl.BlockSpec(shape, lambda *i: (0,) * len(shape))


def tile(*shape):
    return pl.BlockSpec(shape, lambda i: (i,) + (0,) * (len(shape) - 1))


def cost(flops, nbytes):
    return pl.CostEstimate(flops=int(flops * 0.01), bytes_accessed=int(nbytes * 0.01), transcendentals=0)


def project_kernel(load, width, *refs):
    n = load.count
    origin, x_ref, vec = refs[0], refs[1], refs[2]
    srcs = refs[3 : 3 + n]
    qkv_ref = refs[3 + n]
    scratch = refs[4 + n :]
    wqkv = scratch[0]

    @pl.when(pl.program_id(0) == 0)
    def _():
        for wait in load.start(srcs, origin, scratch):
            wait()

    qkv = dot_nn(x_ref[...], wqkv[...])
    qkv_ref[:, : 2 * width] = qkv[:, : 2 * width].astype(BF)
    qkv_ref[:, 2 * width :] = (qkv[:, 2 * width :] + vec[BIAS_V : BIAS_V + 1, :]).astype(BF)


def project_call(origin, x, vec, load):
    rows, width = x.shape
    return pl.pallas_call(
        partial(project_kernel, load, width),
        grid=(rows // TILE,),
        in_specs=[SMEM, tile(TILE, width), whole(vec.shape)] + [ANY] * load.count,
        out_specs=tile(TILE, 3 * width),
        out_shape=jax.ShapeDtypeStruct((rows, 3 * width), BF),
        scratch_shapes=load.scratch(),
        compiler_params=pltpu.CompilerParams(vmem_limit_bytes=VMEM_LIMIT),
        cost_estimate=cost(2 * rows * width * 3 * width, 10 * rows * width),
        name="segment_project",
    )(origin, x, vec, *load.arrays)


def attention_kernel(load, width, *refs):
    n = load.count
    origin, x_ref, qkv_ref, vec = refs[:4]
    srcs = refs[4 : 4 + n]
    a_ref, o_ref, h_ref, hb_ref, n_ref, r_ref = refs[4 + n : 10 + n]
    scratch = refs[10 + n :]
    wout = scratch[0]

    @pl.when(pl.program_id(0) == 0)
    def _():
        for wait in load.start(srcs, origin, scratch):
            wait()

    for s in range(TILE // SEG):
        rows = pl.ds(s * SEG, SEG)
        pairs = range(width // 128)
        q = [qkv_ref[rows, pl.ds(p * 128, 128)] for p in pairs]
        k = [qkv_ref[rows, pl.ds(width + p * 128, 128)] for p in pairs]
        v = [qkv_ref[rows, pl.ds(2 * width + p * 128, 128)] for p in pairs]
        for p, (weights, out) in enumerate(pairs_forward(q, k, v, None)):
            a_ref[s, p] = weights
            o_ref[rows, pl.ds(p * 128, 128)] = out
    z = x_ref[...].astype(F32) + dot_nn(o_ref[...], wout[...]) + vec[BIAS_O : BIAS_O + 1, :]
    normed, inverse = norm_rows(z)
    h = normed * vec[GAIN1 : GAIN1 + 1, :] + vec[SHIFT1 : SHIFT1 + 1, :]
    h_ref[...] = h
    hb_ref[...] = h.astype(BF)
    n_ref[...] = normed.astype(BF)
    r_ref[...] = inverse


def attention_call(origin, x, qkv, vec, load):
    rows, width = x.shape
    n = load.count
    segs = rows // SEG
    pairs = width // 128
    return pl.pallas_call(
        partial(attention_kernel, load, width),
        grid=(rows // TILE,),
        in_specs=[SMEM, tile(TILE, width), tile(TILE, 3 * width), whole(vec.shape)] + [ANY] * n,
        out_specs=[
            tile(TILE // SEG, pairs, 2 * SEG, SEG),
            tile(TILE, width),
            tile(TILE, width),
            tile(TILE, width),
            tile(TILE, width),
            tile(TILE, 1),
        ],
        out_shape=[
            jax.ShapeDtypeStruct((segs, pairs, 2 * SEG, SEG), BF),
            jax.ShapeDtypeStruct((rows, width), BF),
            jax.ShapeDtypeStruct((rows, width), F32),
            jax.ShapeDtypeStruct((rows, width), BF),
            jax.ShapeDtypeStruct((rows, width), BF),
            jax.ShapeDtypeStruct((rows, 1), F32),
        ],
        scratch_shapes=load.scratch(),
        compiler_params=pltpu.CompilerParams(vmem_limit_bytes=VMEM_LIMIT),
        cost_estimate=cost(2 * rows * width * 2 * width, 16 * rows * width),
        name="segment_attention",
    )(origin, x, qkv, vec, *load.arrays)


def feed_kernel(load, width, ff, *refs):
    n = load.count
    origin, h_ref, c_ref, o_ref, n_ref, r_ref, vec, upb = refs[:8]
    srcs = refs[8 : 8 + n]
    y_ref, g_ref, gp_ref, dz_ref, dm_ref, pay_ref, sums_ref = refs[8 + n : 15 + n]
    scratch = refs[15 + n :]
    wup, wdown = scratch[:2]

    @pl.when(pl.program_id(0) == 0)
    def _():
        for wait in load.start(srcs, origin, scratch):
            wait()
        sums_ref[...] = jnp.zeros_like(sums_ref)

    h = h_ref[...]
    hb = h.astype(BF)
    block = 512
    total = jnp.zeros((TILE, width), F32)
    u = dot_nn(hb, wup[:, :block]) + upb[0:1, :block]
    for j in range(ff // block):
        cols = slice(j * block, (j + 1) * block)
        if (j + 1) * block < ff:
            later = slice((j + 1) * block, (j + 2) * block)
            u_next = dot_nn(hb, wup[:, later]) + upb[0:1, later]
        active, slope = gelu_both(u)
        active = active.astype(BF)
        g_ref[:, cols] = active
        gp_ref[:, cols] = slope.astype(BF)
        total = total + dot_nn(active, wdown[cols, :])
        u = u_next
    normed, inverse = norm_rows(h + total + vec[BIAS_D : BIAS_D + 1, :])
    gain = vec[GAIN2 : GAIN2 + 1, :]
    y = normed * gain + vec[SHIFT2 : SHIFT2 + 1, :]
    y_ref[...] = y.astype(BF)
    row = lax.broadcasted_iota(jnp.int32, (TILE, 1), 0)
    dy = jnp.where(row % SEG == 0, 0.0, c_ref[...].astype(F32))
    dz = norm_back(dy * gain, normed, inverse)
    dz_ref[...] = dz
    dm = dz.astype(BF)
    dm_ref[...] = dm
    sums_ref[0:1, :] += col_sum(dy * normed)
    sums_ref[1:2, :] += col_sum(dy)
    sums_ref[2:3, :] += col_sum(dm)
    lane = lax.broadcasted_iota(jnp.int32, (1, 128), 1)
    for i in range(pay_ref.shape[0] // (TILE // SEG)):

        @pl.when(pl.program_id(0) == i)
        def _(i=i):
            for s in range(TILE // SEG):
                here = slice(s * SEG, s * SEG + 1)
                few = slice(s * SEG, s * SEG + 16)
                at = slice(i * (TILE // SEG) + s, i * (TILE // SEG) + s + 1)
                pay_ref[at, 0:width] = y[here].astype(BF).astype(F32)
                pay_ref[at, width : 2 * width] = c_ref[few, :].astype(F32)[:1]
                pay_ref[at, 2 * width : 3 * width] = h[here].astype(BF).astype(F32)
                pay_ref[at, 3 * width : 4 * width] = o_ref[few, :].astype(F32)[:1]
                pay_ref[at, 4 * width : 5 * width] = n_ref[few, :].astype(F32)[:1]
                high = r_ref[here].astype(BF).astype(F32)
                pay_ref[at, 5 * width :] = jnp.where(lane == 0, high, jnp.where(lane == 1, r_ref[here] - high, 0.0))


def feed_call(origin, h, cot, o, n1, r1, vec, upb, load, ff):
    rows, width = h.shape
    n = load.count
    pay = 5 * width + 128
    return pl.pallas_call(
        partial(feed_kernel, load, width, ff),
        grid=(rows // TILE,),
        in_specs=[
            SMEM,
            tile(TILE, width),
            tile(TILE, width),
            tile(TILE, width),
            tile(TILE, width),
            tile(TILE, 1),
            whole(vec.shape),
            whole(upb.shape),
        ]
        + [ANY] * n,
        out_specs=[
            tile(TILE, width),
            tile(TILE, ff),
            tile(TILE, ff),
            tile(TILE, width),
            tile(TILE, width),
            whole_out((rows // SEG, pay)),
            whole_out((8, width)),
        ],
        out_shape=[
            jax.ShapeDtypeStruct((rows, width), BF),
            jax.ShapeDtypeStruct((rows, ff), BF),
            jax.ShapeDtypeStruct((rows, ff), BF),
            jax.ShapeDtypeStruct((rows, width), F32),
            jax.ShapeDtypeStruct((rows, width), BF),
            jax.ShapeDtypeStruct((rows // SEG, pay), F32),
            jax.ShapeDtypeStruct((8, width), F32),
        ],
        scratch_shapes=load.scratch(),
        compiler_params=pltpu.CompilerParams(vmem_limit_bytes=VMEM_LIMIT),
        cost_estimate=cost(4 * rows * width * ff, 4 * rows * ff),
        name="segment_feed",
    )(origin, h, cot, o, n1, r1, vec, upb, *load.arrays)


def feed_back_kernel(load, width, ff, *refs):
    n = load.count
    origin, dz_ref, gp_ref, n_ref, r_ref, vec = refs[:6]
    srcs = refs[6 : 6 + n]
    du_ref, dz1_ref, db_ref, do_ref, sums_ref, upsum_ref = refs[6 + n : 12 + n]
    scratch = refs[12 + n :]
    wdown, wup, wout = scratch[:3]

    @pl.when(pl.program_id(0) == 0)
    def _():
        for wait in load.start(srcs, origin, scratch):
            wait()
        sums_ref[...] = jnp.zeros_like(sums_ref)
        upsum_ref[...] = jnp.zeros_like(upsum_ref)

    dz = dz_ref[...]
    dm = dz.astype(BF)
    block = 512
    total = dz
    dg = dot_nt(dm, wdown[:block, :])
    for j in range(ff // block):
        cols = slice(j * block, (j + 1) * block)
        if (j + 1) * block < ff:
            dg_next = dot_nt(dm, wdown[(j + 1) * block : (j + 2) * block, :])
        du = (dg * gp_ref[:, cols].astype(F32)).astype(BF)
        du_ref[:, cols] = du
        upsum_ref[0:1, cols] += col_sum(du)
        total = total + dot_nt(du, wup[:, cols])
        dg = dg_next
    normed = n_ref[...].astype(F32)
    dz1 = norm_back(total * vec[GAIN1 : GAIN1 + 1, :], normed, r_ref[...])
    dz1_ref[...] = dz1
    db = dz1.astype(BF)
    db_ref[...] = db
    do_ref[...] = dot_nt(db, wout[...]).astype(BF)
    sums_ref[0:1, :] += col_sum(total * normed)
    sums_ref[1:2, :] += col_sum(total)
    sums_ref[2:3, :] += col_sum(db)


def feed_back_call(origin, dz, gp, n1, r1, vec, load):
    rows, width = dz.shape
    ff = gp.shape[1]
    n = load.count
    return pl.pallas_call(
        partial(feed_back_kernel, load, width, ff),
        grid=(rows // TILE,),
        in_specs=[SMEM, tile(TILE, width), tile(TILE, ff), tile(TILE, width), tile(TILE, 1), whole(vec.shape)] + [ANY] * n,
        out_specs=[
            tile(TILE, ff),
            tile(TILE, width),
            tile(TILE, width),
            tile(TILE, width),
            whole_out((8, width)),
            whole_out((8, ff)),
        ],
        out_shape=[
            jax.ShapeDtypeStruct((rows, ff), BF),
            jax.ShapeDtypeStruct((rows, width), F32),
            jax.ShapeDtypeStruct((rows, width), BF),
            jax.ShapeDtypeStruct((rows, width), BF),
            jax.ShapeDtypeStruct((8, width), F32),
            jax.ShapeDtypeStruct((8, ff), F32),
        ],
        scratch_shapes=load.scratch(),
        compiler_params=pltpu.CompilerParams(vmem_limit_bytes=VMEM_LIMIT),
        cost_estimate=cost(4 * rows * width * ff + 2 * rows * width * width, 4 * rows * ff),
        name="segment_feed_back",
    )(origin, dz, gp, n1, r1, vec, *load.arrays)


def spread(table, chips, cores, chunk, first_chip, count, source, outs, put):
    core = table[chips]
    for q in range(count):
        slot = table[first_chip + q]
        for c in range(cores):
            device = q * cores + (jnp.bitwise_xor(core, c) if cores > 1 else 0)
            start = pl.multiple_of(device * chunk, 16)
            put(outs[c], slot, source[pl.ds(start, chunk), :].astype(BF))


def once(shape):
    return pl.BlockSpec(shape, lambda i: (0,) * len(shape), pipeline_mode=pl.Buffered(1))


def grads_feed_kernel(chips, cores, chunk, width, group, *refs):
    table, g_ref, dm_ref, hb_ref, du_ref = refs[:5]
    outs = refs[5 : 5 + cores]
    scratch = refs[5 + cores]
    step = pl.program_id(0)

    @pl.when(step < group)
    def _():
        scratch[...] = dot_tn(g_ref[...], dm_ref[...])
        if chips > 1:
            per = width // (chunk * group * cores)
            core = table[chips]
            for q in range(per):
                slot = table[step * per + q]
                for c in range(cores):
                    device = q * cores + jnp.bitwise_xor(core, c)
                    for j in range(group):
                        start = pl.multiple_of((device * group + j) * chunk, 16)
                        outs[c][slot, :, j * width : (j + 1) * width] = scratch[pl.ds(start, chunk), :].astype(BF)
        else:
            outs[0][0, :, pl.ds(pl.multiple_of(step * width, width), width)] = scratch[...].astype(BF)

    @pl.when(step >= group)
    def _():
        scratch[...] = dot_tn(hb_ref[...], du_ref[...])
        cols = pl.ds(pl.multiple_of(step * width, width), width)

        def put(out, slot, values):
            out[slot, :, cols] = values

        spread(table, chips, cores, chunk, 0, chips, scratch, outs, put)


def grads_feed_call(table, g, dm, hb, du, chips, cores, chunk):
    rows, ff = g.shape
    width = dm.shape[1]
    group = ff // width
    return pl.pallas_call(
        partial(grads_feed_kernel, chips, cores, chunk, width, group),
        grid=(2 * group,),
        in_specs=[
            SMEM,
            pl.BlockSpec((rows, width), lambda i: (0, jnp.minimum(i, group - 1))),
            whole((rows, width)),
            whole((rows, width)),
            pl.BlockSpec((rows, width), lambda i: (0, jnp.maximum(i - group, 0))),
        ],
        out_specs=[once((chips, chunk, 2 * ff))] * cores,
        out_shape=[jax.ShapeDtypeStruct((chips, chunk, 2 * ff), BF)] * cores,
        scratch_shapes=[pltpu.VMEM((width, width), F32)],
        compiler_params=pltpu.CompilerParams(vmem_limit_bytes=VMEM_LIMIT),
        cost_estimate=cost(4 * rows * width * ff, 4 * rows * ff + 4 * width * ff),
        name="grads_feed",
    )(table, g, dm, hb, du)


def grads_out_kernel(chips, cores, chunk, *refs):
    table, o_ref, db_ref = refs[:3]
    outs = refs[3 : 3 + cores]
    scratch = refs[3 + cores]
    scratch[...] = dot_tn(o_ref[...], db_ref[...])

    def put(out, slot, values):
        out[slot] = values

    spread(table, chips, cores, chunk, 0, chips, scratch, outs, put)


def grads_out_call(table, o, db, chips, cores, chunk):
    width = o.shape[1]
    full = pl.BlockSpec(memory_space=pltpu.VMEM)
    return pl.pallas_call(
        partial(grads_out_kernel, chips, cores, chunk),
        in_specs=[SMEM, full, full],
        out_specs=[full] * cores,
        out_shape=[jax.ShapeDtypeStruct((chips, chunk, width), BF)] * cores,
        scratch_shapes=[pltpu.VMEM((width, width), F32)],
        compiler_params=pltpu.CompilerParams(vmem_limit_bytes=VMEM_LIMIT),
        cost_estimate=cost(2 * o.shape[0] * width * width, 8 * width * width),
        name="grads_out",
    )(table, o, db)


def attention_back_kernel(chips, cores, chunk, width, group, *refs):
    table, qkv_ref, a_ref, do_ref, x_ref, do_first, sums1, sums2, up_sums = refs[:9]
    dqkv, sums_ref = refs[9:11]
    outs = refs[11 : 11 + cores]
    total, d_o = refs[11 + cores :]
    step = pl.program_id(0)

    @pl.when(step == 0)
    def _():
        total[...] = jnp.zeros_like(total)
        sums_ref[...] = jnp.zeros_like(sums_ref)

    d_o[...] = do_ref[...].astype(F32)
    for s in range(TILE // SEG):
        at = pl.ds(table[chips + 1] + step * (TILE // SEG) + s, 1)
        d_o[s * SEG : s * SEG + 1, :] = do_first[at, :]
    for s in range(TILE // SEG):
        rows = pl.ds(s * SEG, SEG)
        pairs = range(width // 128)
        q = [qkv_ref[rows, pl.ds(p * 128, 128)] for p in pairs]
        k = [qkv_ref[rows, pl.ds(width + p * 128, 128)] for p in pairs]
        v = [qkv_ref[rows, pl.ds(2 * width + p * 128, 128)] for p in pairs]
        w = [a_ref[s, p] for p in pairs]
        d_out = [d_o[rows, pl.ds(p * 128, 128)].astype(BF) for p in pairs]
        for p, (d_q, d_k, d_v) in enumerate(pairs_backward(q, k, v, w, d_out)):
            dqkv[rows, pl.ds(p * 128, 128)] = d_q
            dqkv[rows, pl.ds(width + p * 128, 128)] = d_k
            dqkv[rows, pl.ds(2 * width + p * 128, 128)] = d_v
    sums_ref[0:1, :] += col_sum(dqkv[:, 2 * width :])
    total[...] += dot_tn(x_ref[...], dqkv[...])

    @pl.when(step == pl.num_programs(0) - 1)
    def _():
        def put(out, slot, values):
            out[slot, :, : 3 * width] = values

        spread(table, chips, cores, chunk, 0, chips, total, outs, put)
        if cores > 1:
            vec = [sums1[0:1], sums2[0:1], sums_ref[0:1], sums1[2:3], sums2[2:3], sums1[1:2], sums2[1:2]]
            vec = jnp.concatenate(vec + [jnp.zeros((1, width), F32)], axis=0)
            pad = jnp.zeros((chunk - UP0 - group, chunk), F32)
            for q in range(chips):
                blocks = []
                for device in (2 * q, 2 * q + 1):
                    own = slice(device * chunk, (device + 1) * chunk)
                    ups = [up_sums[0:1, group * chunk * device + chunk * j : group * chunk * device + chunk * (j + 1)] for j in range(group)]
                    block = jnp.concatenate([vec[:UP0, own]] + ups + [pad], axis=0)
                    blocks.append(jnp.concatenate([block, jnp.zeros((chunk, 128 - chunk), F32)], axis=1))
                for c in range(2):
                    picked = jnp.where(table[chips] == c, blocks[0], blocks[1]).astype(BF)
                    outs[c][table[q], :, 3 * width :] = picked


def attention_back_call(table, qkv, a, do, x, do_first, sums1, sums2, up_sums, chips, cores, chunk):
    rows, width = x.shape
    pairs = width // 128
    cols = 3 * width + (128 if cores > 1 else 0)
    group = up_sums.shape[1] // width
    return pl.pallas_call(
        partial(attention_back_kernel, chips, cores, chunk, width, group),
        grid=(rows // TILE,),
        in_specs=[
            SMEM,
            tile(TILE, 3 * width),
            tile(TILE // SEG, pairs, 2 * SEG, SEG),
            tile(TILE, width),
            tile(TILE, width),
            whole(do_first.shape),
            whole(sums1.shape),
            whole(sums2.shape),
            whole(up_sums.shape),
        ],
        out_specs=[tile(TILE, 3 * width), whole_out((8, width))] + [once((chips, chunk, cols))] * cores,
        out_shape=[jax.ShapeDtypeStruct((rows, 3 * width), BF), jax.ShapeDtypeStruct((8, width), F32)]
        + [jax.ShapeDtypeStruct((chips, chunk, cols), BF)] * cores,
        scratch_shapes=[pltpu.VMEM((width, 3 * width), F32), pltpu.VMEM((TILE, width), F32)],
        compiler_params=pltpu.CompilerParams(vmem_limit_bytes=VMEM_LIMIT),
        cost_estimate=cost(2 * rows * width * 5 * width, 20 * rows * width),
        name="segment_attention_back",
    )(table, qkv, a, do, x, do_first, sums1, sums2, up_sums)


def input_grad_kernel(load, width, *refs):
    n = load.count
    origin, table, dqkv_ref, dz_ref, dz_first = refs[:5]
    srcs = refs[5 : 5 + n]
    dx_ref, d_z = refs[5 + n : 7 + n]
    scratch = refs[7 + n :]
    step = pl.program_id(0)

    @pl.when(step == 0)
    def _():
        for wait in load.start(srcs, origin, scratch):
            wait()

    d_z[...] = dz_ref[...]
    for s in range(TILE // SEG):
        at = pl.ds(table[0] + step * (TILE // SEG) + s, 1)
        d_z[s * SEG : s * SEG + 1, :] = dz_first[at, :]
    dx_ref[...] = (d_z[...] + dot_nt(dqkv_ref[...], scratch[0][...])).astype(BF)


def input_grad_call(origin, first_row, dqkv, dz, dz_first, load):
    rows, width = dz.shape
    n = load.count
    return pl.pallas_call(
        partial(input_grad_kernel, load, width),
        grid=(rows // TILE,),
        in_specs=[SMEM, SMEM, tile(TILE, 3 * width), tile(TILE, width), whole(dz_first.shape)] + [ANY] * n,
        out_specs=tile(TILE, width),
        out_shape=jax.ShapeDtypeStruct((rows, width), BF),
        scratch_shapes=[pltpu.VMEM((TILE, width), F32)] + load.scratch(),
        compiler_params=pltpu.CompilerParams(vmem_limit_bytes=VMEM_LIMIT),
        cost_estimate=cost(2 * rows * width * 3 * width, 12 * rows * width),
        name="input_grad",
    )(origin, first_row, dqkv, dz, dz_first, *load.arrays)


def one_hot(rows, cols, base):
    r = lax.broadcasted_iota(jnp.int32, (rows, cols), 0)
    c = lax.broadcasted_iota(jnp.int32, (rows, cols), 1)
    return (r == c + base).astype(F32).astype(BF)


def window(ref, first, width, base, count):
    size = min(256, width)
    start = jnp.minimum((base // 128) * 128, width - size)
    values = ref[:, pl.ds(pl.multiple_of(start + first, 128), size)]
    return dot_nn(values.astype(BF), one_hot(size, count, base - start))


def few_feed_forward(hb, h, vec, up_row, wup, wdown, g_ref, gp_ref, ff, wait_up, wait_down):
    block = 512
    total = jnp.zeros(h.shape, F32)
    wait_up()
    for j in range(ff // block):
        cols = slice(j * block, (j + 1) * block)
        active, slope = gelu_both(dot_nn(hb, wup[:, cols]) + up_row[:, cols])
        g_ref[:, cols] = active.astype(BF)
        gp_ref[:, cols] = slope.astype(BF)
    wait_down()
    for j in range(ff // block):
        cols = slice(j * block, (j + 1) * block)
        total = total + dot_nn(g_ref[:, cols], wdown[cols, :])
    return norm_rows(h + total + vec[BIAS_D : BIAS_D + 1, :])


def few_backward(dy, n2, r2, n1, r1, vec, wup, wdown, wout, gp_ref, du_ref, ff, wait_down, wait_up, wait_out):
    block = 512
    dz = norm_back(dy * vec[GAIN2 : GAIN2 + 1, :], n2, r2)
    dm = dz.astype(BF)
    total = dz
    wait_down()
    for j in range(ff // block):
        cols = slice(j * block, (j + 1) * block)
        du_ref[:, cols] = (dot_nt(dm, wdown[cols, :]) * gp_ref[:, cols].astype(F32)).astype(BF)
    wait_up()
    for j in range(ff // block):
        cols = slice(j * block, (j + 1) * block)
        total = total + dot_nt(du_ref[:, cols], wup[:, cols])
    dz1 = norm_back(total * vec[GAIN1 : GAIN1 + 1, :], n1, r1)
    db = dz1.astype(BF)
    wait_out()
    return dm, total, dz1, db, dot_nt(db, wout[...])


def few_grads(me, chunk, ff, hb, o, g_ref, du_ref, dm, db, sums, wide, grads):
    block = 512
    width = dm.shape[1]
    group = ff // width
    base = me * chunk
    own_h = window(*hb, width, base, chunk).astype(BF)
    own_o = window(*o, width, base, chunk).astype(BF)
    own_g = window(g_ref, 0, ff, base * group, group * chunk).astype(BF)
    down = dot_tn(own_g, dm).astype(BF)
    for j in range(group):
        grads[:, j * width : (j + 1) * width] = down[j * chunk : (j + 1) * chunk]
    for j in range(ff // block):
        cols = slice(j * block, (j + 1) * block)
        grads[:, ff + j * block : ff + (j + 1) * block] = dot_tn(own_h, du_ref[:, cols]).astype(BF)
    grads[:, 2 * ff : 2 * ff + width] = dot_tn(own_o, db).astype(BF)
    wide[...] = jnp.zeros_like(wide)
    for i, x in enumerate(sums):
        if x is not None:
            wide[i : i + 1, :width] = x
    wide[8:9, :] = col_sum(du_ref[...])
    own_sums = window(wide, 0, width, base, chunk)
    own_up = window(wide, 0, ff, base * group, group * chunk)
    ups = [own_up[8:9, j * chunk : (j + 1) * chunk] for j in range(group)]
    return jnp.concatenate([own_sums[:UP0]] + ups + [jnp.zeros((VEC_ROWS - UP0 - group, chunk), F32)], axis=0)


def cross_kernel(load, width, ff, chunk, places_n, *refs):
    n = load.count
    origin, table, pay_ref, doc_row, tab_ref, vec, upb = refs[:7]
    srcs = refs[7 : 7 + n]
    out_ref, dx_ref, grads, sums_ref, gtab_ref = refs[7 + n : 12 + n]
    qkv, a_ref, o_s, d_s, g_ref, gp_ref, du_ref, low_ref, hb_ref, wide, tab_own = refs[12 + n : 23 + n]
    scratch = refs[23 + n :]
    wqkv, wout, wup, wdown = scratch[:4]
    rows = pay_ref.shape[0]
    me = table[0]
    wait_qkv, wait_out, wait_up, wait_down = load.start(srcs, origin, scratch)
    row_at = lax.broadcasted_iota(jnp.int32, (rows, rows), 0)
    col_at = lax.broadcasted_iota(jnp.int32, (rows, rows), 1)
    earlier = row_at > col_at
    docs = jnp.broadcast_to(doc_row[...].astype(F32), (rows, rows))
    same = docs == jnp.sum(jnp.where(row_at == col_at, docs, 0.0), axis=1, keepdims=True)
    position = jnp.sum(jnp.where(same & earlier, 1.0, 0.0), axis=1, keepdims=True)
    slot = lax.broadcasted_iota(jnp.int32, (rows, places_n), 1).astype(F32)
    lookup = (slot == position).astype(F32).astype(BF)
    entry = pay_ref[:, :width] + dot_nn(lookup, tab_ref[...].astype(BF))
    low = entry.astype(BF)
    low_ref[...] = low
    allowed = jnp.concatenate([same, same], axis=0)
    wait_qkv()
    proj = dot_nn(low, wqkv[...])
    qkv[:, : 2 * width] = proj[:, : 2 * width].astype(BF)
    qkv[:, 2 * width :] = (proj[:, 2 * width :] + vec[BIAS_V : BIAS_V + 1, :]).astype(BF)
    pairs = range(width // 128)

    def lanes(ref, p, first=0):
        return ref[:, first + p * 128 : first + (p + 1) * 128]

    together = len(pairs) if rows <= 128 else 1
    for at in range(0, len(pairs), together):
        some = range(at, at + together)
        q = [lanes(qkv, p) for p in some]
        k = [lanes(qkv, p, width) for p in some]
        v = [lanes(qkv, p, 2 * width) for p in some]
        for p, (weights, out) in zip(some, pairs_forward(q, k, v, allowed)):
            a_ref[p] = weights
            o_s[:, p * 128 : (p + 1) * 128] = out
    wait_out()
    o = o_s[...]
    n1, r1 = norm_rows(entry + dot_nn(o, wout[...]) + vec[BIAS_O : BIAS_O + 1, :])
    h = n1 * vec[GAIN1 : GAIN1 + 1, :] + vec[SHIFT1 : SHIFT1 + 1, :]
    hb = h.astype(BF)
    n2, r2 = few_feed_forward(hb, h, vec, upb.at[1:2, :], wup, wdown, g_ref, gp_ref, ff, wait_up, wait_down)
    out_ref[...] = n2 * vec[GAIN2 : GAIN2 + 1, :] + vec[SHIFT2 : SHIFT2 + 1, :]
    dy = pay_ref[:, width:]

    def ready():
        return None

    hb_ref[...] = hb
    dm, total, dz1, db, do = few_backward(
        dy, n2, r2, n1, r1, vec, wup, wdown, wout, gp_ref, du_ref, ff, ready, ready, ready
    )
    do = do.astype(BF)
    for at in range(0, len(pairs), together):
        some = range(at, at + together)
        q = [lanes(qkv, p) for p in some]
        k = [lanes(qkv, p, width) for p in some]
        v = [lanes(qkv, p, 2 * width) for p in some]
        w = [a_ref[p] for p in some]
        d_out = [do[:, p * 128 : (p + 1) * 128] for p in some]
        for p, (d_q, d_k, d_v) in zip(some, pairs_backward(q, k, v, w, d_out)):
            d_s[:, p * 128 : (p + 1) * 128] = d_q
            d_s[:, width + p * 128 : width + (p + 1) * 128] = d_k
            d_s[:, 2 * width + p * 128 : 2 * width + (p + 1) * 128] = d_v
    d_all = d_s[...]
    d_in = dz1 + dot_nt(d_all, wqkv[...])
    dx_ref[...] = d_in
    dv = col_sum(d_all[:, 2 * width :])
    sums = [col_sum(total * n1), col_sum(dy * n2), dv, col_sum(db), col_sum(dm), col_sum(total), col_sum(dy)]
    sums = few_grads(me, chunk, ff, (hb_ref, 0), (o_s, 0), g_ref, du_ref, dm, db, sums, wide, grads)
    base = 2 * ff + width
    own_low = window(low_ref, 0, width, me * chunk, chunk).astype(BF)
    grads[:, base : base + 3 * width] = dot_tn(own_low, d_all).astype(BF)
    high = d_in.astype(BF)
    rest = (d_in - high.astype(F32)).astype(BF)
    tab_own[...] = dot_tn(lookup, high) + dot_tn(lookup, rest)
    own_tab = window(tab_own, 0, width, me * chunk, chunk)
    sums_ref[...] = sums
    gtab_ref[...] = own_tab
    if grads.shape[1] > base + 3 * width:
        high = 2 * VEC_ROWS
        gap = jnp.zeros((chunk, 64 - chunk), F32)
        left = jnp.concatenate([sums, jnp.zeros((VEC_ROWS, chunk), F32), own_tab[: chunk - high]], axis=0)
        grads[:, base + 3 * width :] = jnp.concatenate([left, gap, own_tab[chunk - high :], gap], axis=1).astype(BF)


def cross_call(origin, table, pay, docs, tab, vec, upb, load, ff, chunk, extra):
    rows, width = pay.shape[0], vec.shape[1]
    n = load.count
    group = ff // width
    pairs = width // 128
    full = pl.BlockSpec(memory_space=pltpu.VMEM)
    return pl.pallas_call(
        partial(cross_kernel, load, width, ff, chunk, tab.shape[0]),
        in_specs=[SMEM, SMEM] + [full] * 5 + [ANY] * n,
        out_specs=[full] * 5,
        out_shape=[
            jax.ShapeDtypeStruct((rows, width), F32),
            jax.ShapeDtypeStruct((rows, width), F32),
            jax.ShapeDtypeStruct((chunk, 2 * ff + 4 * width + extra), BF),
            jax.ShapeDtypeStruct((VEC_ROWS, chunk), F32),
            jax.ShapeDtypeStruct((tab.shape[0], chunk), F32),
        ],
        scratch_shapes=[
            pltpu.VMEM((rows, 3 * width), BF),
            pltpu.VMEM((pairs, 2 * rows, rows), BF),
            pltpu.VMEM((rows, width), BF),
            pltpu.VMEM((rows, 3 * width), BF),
            pltpu.VMEM((rows, ff), BF),
            pltpu.VMEM((rows, ff), BF),
            pltpu.VMEM((rows, ff), BF),
            pltpu.VMEM((rows, width), BF),
            pltpu.VMEM((rows, width), BF),
            pltpu.VMEM((VEC_ROWS, ff), F32),
            pltpu.VMEM((tab.shape[0], width), F32),
        ]
        + load.scratch(),
        compiler_params=pltpu.CompilerParams(vmem_limit_bytes=VMEM_LIMIT),
        cost_estimate=cost(16 * rows * width * ff, 20 * width * width),
        name="cross_block",
    )(origin, table, pay, docs.reshape(1, rows), tab, vec, upb, *load.arrays)


def first_forward_kernel(load, pay_pieces, width, ff, *refs):
    n, m = load.count, len(pay_pieces.arrays)
    origin, pay_origin, vec, upb = refs[:4]
    srcs = refs[4 : 4 + n]
    pay_srcs = refs[4 + n : 4 + n + m]
    cross_ref, pay_ref, g_ref, gp_ref, n_ref, r_ref = refs[4 + n + m : 10 + n + m]
    held, sem = refs[10 + n + m : 12 + n + m]
    scratch = refs[12 + n + m :]
    wup, wdown = scratch[:2]
    copies = pay_pieces.copies(pay_srcs, pay_origin, sem, 0, held.shape[2], held, by_origin=True)
    copies.start()
    wait_up, wait_down = load.start(srcs, origin, scratch)
    copies.wait()
    pay = held[...].astype(F32).reshape(pay_ref.shape[0], held.shape[2])
    cross_ref[...] = pay[:, : 2 * width]
    pay_ref[...] = pay[:, 2 * width :]
    hb = pay_ref[:, :width].astype(BF)
    normed, inverse = few_feed_forward(
        hb, hb.astype(F32), vec, upb.at[0:1, :], wup, wdown, g_ref, gp_ref, ff, wait_up, wait_down
    )
    n_ref[...] = normed
    r_ref[...] = inverse


def first_forward_call(origin, pay_origin, pay_pieces, vec, upb, load, ff):
    width = vec.shape[1]
    rows = pay_pieces.rows
    n, m = load.count, len(pay_pieces.arrays)
    full = pl.BlockSpec(memory_space=pltpu.VMEM)
    return pl.pallas_call(
        partial(first_forward_kernel, load, pay_pieces, width, ff),
        in_specs=[SMEM, SMEM] + [full] * 2 + [ANY] * (n + m),
        out_specs=[full] * 6,
        out_shape=[
            jax.ShapeDtypeStruct((rows, 2 * width), F32),
            jax.ShapeDtypeStruct((rows, pay_pieces.arrays[0].shape[1] - 2 * width), F32),
            jax.ShapeDtypeStruct((rows, ff), BF),
            jax.ShapeDtypeStruct((rows, ff), BF),
            jax.ShapeDtypeStruct((rows, width), F32),
            jax.ShapeDtypeStruct((rows, 1), F32),
        ],
        scratch_shapes=[
            pltpu.VMEM((pay_pieces.origins, pay_pieces.chunk, pay_pieces.arrays[0].shape[1]), BF),
            pltpu.SemaphoreType.DMA((pay_pieces.count,)),
        ]
        + load.scratch(),
        compiler_params=pltpu.CompilerParams(vmem_limit_bytes=VMEM_LIMIT),
        cost_estimate=cost(6 * rows * width * ff, 4 * width * ff),
        name="first_rows_forward",
    )(origin, pay_origin, vec, upb, *load.arrays, *pay_pieces.arrays)


def first_kernel(load, width, ff, *refs):
    n = load.count
    origin, pay_ref, dy_ref, gp_ref, n2_ref, r2_ref, vec = refs[:7]
    srcs = refs[7 : 7 + n]
    dz1_ref, do_ref, du_ref, dm_ref, db_ref, total_ref = refs[7 + n : 13 + n]
    scratch = refs[13 + n :]
    wdown, wup, wout = scratch[:3]
    waits = load.start(srcs, origin, scratch)
    n1 = pay_ref[:, 2 * width : 3 * width]
    r1 = jnp.sum(pay_ref[:, 3 * width :], axis=1, keepdims=True)
    dm, total, dz1, db, do = few_backward(
        dy_ref[...], n2_ref[...], r2_ref[...], n1, r1, vec, wup, wdown, wout, gp_ref, du_ref, ff, *waits
    )
    dm_ref[...] = dm
    db_ref[...] = db
    total_ref[...] = total
    dz1_ref[...] = dz1
    do_ref[...] = do


def first_call(origin, pay, dy, gp, n2, r2, vec, load):
    rows, width = dy.shape
    ff = gp.shape[1]
    n = load.count
    full = pl.BlockSpec(memory_space=pltpu.VMEM)
    return pl.pallas_call(
        partial(first_kernel, load, width, ff),
        in_specs=[SMEM] + [full] * 6 + [ANY] * n,
        out_specs=[full] * 6,
        out_shape=[
            jax.ShapeDtypeStruct((rows, width), F32),
            jax.ShapeDtypeStruct((rows, width), F32),
            jax.ShapeDtypeStruct((rows, ff), BF),
            jax.ShapeDtypeStruct((rows, width), BF),
            jax.ShapeDtypeStruct((rows, width), BF),
            jax.ShapeDtypeStruct((rows, width), F32),
        ],
        scratch_shapes=load.scratch(),
        compiler_params=pltpu.CompilerParams(vmem_limit_bytes=VMEM_LIMIT),
        cost_estimate=cost(8 * rows * width * ff, 4 * width * ff),
        name="first_rows_back",
    )(origin, pay, dy, gp, n2, r2, vec, *load.arrays)


def first_grads_kernel(width, ff, chunk, *refs):
    table, pay_ref, dy_ref, g_ref, n2_ref, du_ref, dm_ref, db_ref, total_ref, grads, sums_ref, wide = refs
    dm, db, total, dy = dm_ref[...], db_ref[...], total_ref[...], dy_ref[...]
    n1 = pay_ref[:, 2 * width : 3 * width]
    sums = [col_sum(total * n1), col_sum(dy * n2_ref[...]), None, col_sum(db), col_sum(dm), col_sum(total), col_sum(dy)]
    sums = few_grads(
        table[0], chunk, ff, (pay_ref, 0), (pay_ref, width), g_ref, du_ref, dm, db, sums, wide, grads
    )
    if sums_ref.shape[1] > chunk:
        sums = jnp.concatenate([sums, jnp.zeros((sums_ref.shape[0] - VEC_ROWS, chunk), F32)], axis=0)
        sums_ref[:, : sums_ref.shape[1] - 128] = jnp.zeros((sums_ref.shape[0], sums_ref.shape[1] - 128), BF)
        sums = jnp.concatenate([sums, jnp.zeros((sums_ref.shape[0], 128 - chunk), F32)], axis=1)
        sums_ref[:, sums_ref.shape[1] - 128 :] = sums.astype(BF)
    else:
        sums_ref[...] = sums


def first_grads_call(table, pay, dy, g, n2, du, dm, db, total, chunk, sums_shape):
    rows, width = dy.shape
    ff = g.shape[1]
    full = pl.BlockSpec(memory_space=pltpu.VMEM)
    return pl.pallas_call(
        partial(first_grads_kernel, width, ff, chunk),
        in_specs=[SMEM] + [full] * 8,
        out_specs=[full] * 2,
        out_shape=[jax.ShapeDtypeStruct((chunk, 2 * ff + width), BF), sums_shape],
        scratch_shapes=[pltpu.VMEM((VEC_ROWS, ff), F32)],
        compiler_params=pltpu.CompilerParams(vmem_limit_bytes=VMEM_LIMIT),
        cost_estimate=cost(2 * rows * width * ff // 4, 8 * rows * ff),
        name="first_rows_grads",
    )(table, pay, dy, g, n2, du, dm, db, total)


def vector_kernel(pieces, col, own, width, ff, *refs):
    n = len(pieces.arrays)
    origin = refs[0]
    srcs = refs[1 : 1 + n]
    vec0, vec1, tab, upb = refs[1 + n : 5 + n]
    held, sem = refs[5 + n :]
    copies = pieces.copies(srcs, origin, sem, col, 128, held, by_origin=True)
    copies.start()
    upb[...] = jnp.zeros_like(upb)
    copies.wait()
    high = 2 * VEC_ROWS
    group = ff // width
    for i in range(pieces.origins):
        block = held[i].astype(F32)
        cols = slice(own * i, own * (i + 1))
        vec0[:, cols] = block[:VEC_ROWS, :own]
        vec1[:, cols] = block[VEC_ROWS:high, :own]
        tab[: own - high, cols] = block[high:own, :own]
        tab[own - high :, cols] = block[:, 64 : 64 + own]
        for b in range(2):
            for j in range(group):
                at = group * own * i + own * j
                upb[b : b + 1, at : at + own] = block[b * VEC_ROWS + UP0 + j : b * VEC_ROWS + UP0 + j + 1, :own]


def vector_call(origin, pieces, col, own, width, ff, places_n):
    n = len(pieces.arrays)
    full = pl.BlockSpec(memory_space=pltpu.VMEM)
    return pl.pallas_call(
        partial(vector_kernel, pieces, col, own, width, ff),
        in_specs=[SMEM] + [ANY] * n,
        out_specs=[full] * 4,
        out_shape=[
            jax.ShapeDtypeStruct((VEC_ROWS, width), F32),
            jax.ShapeDtypeStruct((VEC_ROWS, width), F32),
            jax.ShapeDtypeStruct((places_n, width), F32),
            jax.ShapeDtypeStruct((8, ff), F32),
        ],
        scratch_shapes=[pltpu.VMEM((pieces.origins, own, 128), BF), pltpu.SemaphoreType.DMA((pieces.count,))],
        compiler_params=pltpu.CompilerParams(vmem_limit_bytes=VMEM_LIMIT),
        cost_estimate=cost(1000, 128 * width * 8),
        name="vectors",
    )(origin, *pieces.arrays)


def pack_kernel(own, width, ff, places_n, *refs):
    qkv, out, up, down, gains, biases, upb, table, first, feed, other, side = refs
    group = ff // width
    first[:, : 3 * width] = qkv[0]
    first[:, 3 * width : 4 * width] = out[0]
    other[:, : 3 * width] = qkv[1]
    other[:, 3 * width : 4 * width] = out[1]
    for b, (pack, at) in enumerate(((feed, 0), (other, 4 * width))):
        pack[:, at : at + ff] = up[b]
        for j in range(group):
            pack[:, at + ff + j * width : at + ff + (j + 1) * width] = down[b, j * own : (j + 1) * own, :]
    side[...] = jnp.zeros_like(side)
    for b in range(2):
        at = b * VEC_ROWS
        side[at : at + 2, :own] = gains[b].astype(F32)
        side[at + 2 : at + 7, :own] = biases[b].astype(F32)
        row = upb[...].astype(F32)[b : b + 1]
        for j in range(group):
            side[at + UP0 + j : at + UP0 + j + 1, :own] = row[:, j * own : (j + 1) * own]
    places = table[...].astype(F32)
    high = 2 * VEC_ROWS
    side[high:own, :own] = places[: own - high]
    side[:, 64 : 64 + own] = places[own - high :]
    first[:, 4 * width :] = side[...].astype(BF)


def pack_call(own, width, ff, qkv, out, up, down, gains, biases, upb, table):
    full = pl.BlockSpec(memory_space=pltpu.VMEM)
    return pl.pallas_call(
        partial(pack_kernel, own, width, ff, table.shape[0]),
        in_specs=[full] * 8,
        out_specs=[full] * 3,
        out_shape=[
            jax.ShapeDtypeStruct((own, 4 * width + 128), BF),
            jax.ShapeDtypeStruct((own, 2 * ff), BF),
            jax.ShapeDtypeStruct((own, 4 * width + 2 * ff), BF),
        ],
        scratch_shapes=[pltpu.VMEM((own, 128), F32)],
        compiler_params=pltpu.CompilerParams(vmem_limit_bytes=VMEM_LIMIT),
        cost_estimate=cost(1000, 8 * own * 8 * width),
        name="pack_weights",
    )(qkv, out, up, down, gains, biases, upb, table)


def sum_kernel(plan, widths, *refs):
    groups = len(widths)
    count = sum(2 * groups + len(more) for _, more in plan)
    at = 0
    for out, (shift, more) in zip(refs[count:], plan):
        slots = refs[at : at + 2 * groups]
        at += 2 * groups
        extra = [(ref, first) for ref, first in zip(refs[at : at + len(more)], more)]
        at += len(more)
        rows = out.shape[0]
        edges = sorted({0, rows} | {e for ref, first in extra for e in (first, first + ref.shape[0])})
        for low, high in zip(edges, edges[1:]):
            col = 0
            for g, width in enumerate(widths):
                value = slots[2 * g][0, shift + low : shift + high, :].astype(F32)
                value = value + slots[2 * g + 1][0, shift + low : shift + high, :].astype(F32)
                for ref, first in extra:
                    if first <= low and high <= first + ref.shape[0]:
                        value = value + ref[low - first : high - first, col : col + width].astype(F32)
                out[low:high, col : col + width] = value.astype(BF)
                col += width


def sum_call(groups, outputs):
    args, specs, plan, shapes = [], [], [], []
    widths = [x.shape[2] for x, _ in groups]
    for slot, shift, rows, more in outputs:
        for pair in groups:
            for x in pair:
                args.append(x)
                specs.append(pl.BlockSpec((1,) + x.shape[1:], lambda i, k=slot: (k, 0, 0)))
        for x, _ in more:
            args.append(x)
            specs.append(pl.BlockSpec(x.shape, lambda i: (0, 0)))
        plan.append((shift, [first for _, first in more]))
        shapes.append(jax.ShapeDtypeStruct((rows, sum(widths)), BF))
    return pl.pallas_call(
        partial(sum_kernel, plan, widths),
        grid=(1,),
        in_specs=specs,
        out_specs=[pl.BlockSpec(x.shape, lambda i: (0, 0)) for x in shapes],
        out_shape=shapes,
        compiler_params=pltpu.CompilerParams(vmem_limit_bytes=VMEM_LIMIT),
        cost_estimate=cost(1000, sum(8 * x.shape[0] * x.shape[1] for x in shapes)),
        name="add_pieces",
    )(*args)


def finish_kernel(ff, width, *refs):
    x0, y0, x1, y1, grad_up, grad_out, grad_down = refs
    own = x0.shape[0]
    for b, (x, y) in enumerate(((x0, y0), (x1, y1))):
        for j in range(ff // width):
            cols = slice(j * width, (j + 1) * width)
            grad_down[b, j * own : (j + 1) * own, :] = x[:, cols].astype(F32) + y[:, cols].astype(F32)
        grad_up[b] = x[:, ff : 2 * ff].astype(F32) + y[:, ff : 2 * ff].astype(F32)
        grad_out[b] = x[:, 2 * ff : 2 * ff + width].astype(F32) + y[:, 2 * ff : 2 * ff + width].astype(F32)


def finish_call(ff, width, *args):
    own = args[0].shape[0]
    full = pl.BlockSpec(memory_space=pltpu.VMEM)
    return pl.pallas_call(
        partial(finish_kernel, ff, width),
        in_specs=[full] * 4,
        out_specs=[full] * 3,
        out_shape=[
            jax.ShapeDtypeStruct((2, own, ff), F32),
            jax.ShapeDtypeStruct((2, own, width), F32),
            jax.ShapeDtypeStruct((2, own * ff // width, width), F32),
        ],
        compiler_params=pltpu.CompilerParams(vmem_limit_bytes=VMEM_LIMIT),
        cost_estimate=cost(1000, 16 * own * (2 * ff + width)),
        name="finish_feed",
    )(*args)


def finish_last_kernel(own, width, group, places_n, *refs):
    q0, q0s, q1, q1s, grad_qkv, grad_gains, grad_biases, grad_up_bias, grad_table = refs
    blocks = []
    for b, (x, y) in enumerate(((q0, q0s), (q1, q1s))):
        at = x.shape[1] - 3 * width - 128
        cols = slice(at, at + 3 * width)
        grad_qkv[b] = x[:, cols].astype(F32) + y[:, cols].astype(F32)
        blocks.append(x[:, at + 3 * width :].astype(F32) + y[:, at + 3 * width :].astype(F32))
    for b, block in enumerate(blocks):
        grad_gains[b] = block[:2, :own]
        grad_biases[b] = block[2:7, :own]
        for j in range(group):
            grad_up_bias[b : b + 1, j * own : (j + 1) * own] = block[UP0 + j : UP0 + j + 1, :own]
    high = 2 * VEC_ROWS
    grad_table[: own - high, :] = blocks[1][high:own, :own]
    grad_table[own - high :, :] = blocks[1][:, 64 : 64 + own]


def finish_last_call(own, width, group, places_n, *args):
    full = pl.BlockSpec(memory_space=pltpu.VMEM)
    return pl.pallas_call(
        partial(finish_last_kernel, own, width, group, places_n),
        in_specs=[full] * 4,
        out_specs=[full] * 5,
        out_shape=[
            jax.ShapeDtypeStruct((2, own, 3 * width), F32),
            jax.ShapeDtypeStruct((2, 2, own), F32),
            jax.ShapeDtypeStruct((2, 5, own), F32),
            jax.ShapeDtypeStruct((2, group * own), F32),
            jax.ShapeDtypeStruct((places_n, own), F32),
        ],
        compiler_params=pltpu.CompilerParams(vmem_limit_bytes=VMEM_LIMIT),
        cost_estimate=cost(1000, 48 * own * width),
        name="finish_qkv",
    )(*args)


def tie(x, *others):
    return lax.optimization_barrier((x, others))[0] if others else x


class Ring:
    def __init__(self, shards):
        chips = shards // 2
        self.shards, self.chips = shards, chips
        self.order = list(range(0, chips, 2)) + list(range(chips - 1, 0, -2))
        self.place = {chip: i for i, chip in enumerate(self.order)}

    def shift(self, by):
        pairs = []
        for i, chip in enumerate(self.order):
            to = self.order[(i + by) % self.chips]
            pairs += [(2 * chip, 2 * to), (2 * chip + 1, 2 * to + 1)]
        return pairs

    def forward(self, x):
        return lax.ppermute(x, "shard", self.shift(1))

    def backward(self, x):
        return lax.ppermute(x, "shard", self.shift(-1))

    def sibling(self, x):
        return lax.ppermute(x, "shard", [(i, i ^ 1) for i in range(self.shards)])

    def behind_table(self):
        return [
            [self.order[(self.place[d // 2] - k) % self.chips] for k in range(self.chips)] for d in range(self.shards)
        ]

    def slot_table(self):
        rows = []
        for d in range(self.shards):
            chip = d // 2
            rows.append([(self.place[q] - self.place[chip]) % self.chips for q in range(self.chips)] + [d % 2])
        return rows


def half_of(rows):
    return (rows // 32) * 16 if rows >= 32 else rows


class Gather:
    def __init__(self, ring, x):
        self.ring, self.steps = ring, 0
        self.ahead = self.behind = x
        self.rows = x.shape[0]
        self.entries, self.pending = [], []

    def take(self, *others):
        values = (self.ahead, self.behind, [e[0] for e in self.pending])
        ahead, behind, shared = tie(values, *others)
        for e, x in zip(self.pending, shared):
            self.entries.append((x,) + e[1:])
        self.sent = (ahead, behind)
        far = self.ring.chips // 2
        if self.steps == 0:
            fresh = [(ahead, 0, 0)]
        elif self.steps < far:
            fresh = [(ahead, self.steps, 0), (behind, self.ring.chips - self.steps, 0)]
        else:
            fresh = [(ahead, far, 0), (behind, far, half_of(self.rows))]
        self.entries += [(x, 2 * back, first, 0, x.shape[0]) for x, back, first in fresh]
        return ahead, behind, fresh

    def share(self, fresh):
        self.pending = [(self.ring.sibling(x), 2 * back + 1, first, 0, x.shape[0]) for x, back, first in fresh]

    def step(self, *others):
        self.take_arrived(*others)
        self.send()
        self.share_arrived()

    def take_arrived(self, *others):
        self.ahead, self.behind, self.fresh = self.take(*others)
        self.steps += 1

    def share_arrived(self, others=()):
        self.share([(tie(x, *others), back, first) for x, back, first in self.fresh])

    def send(self, *others):
        ahead, behind = tie((self.ahead, self.behind), *others)
        self.sent = (ahead, behind)
        half = half_of(self.rows)
        last = self.steps == self.ring.chips // 2
        self.ahead = self.ring.forward(ahead[:half] if last else ahead)
        self.behind = self.ring.backward(behind[half:] if last else behind)

    def finish(self, *others):
        self.share(self.take(*others)[2])
        return Pieces(self.entries + self.pending, self.rows, self.ring.shards)


class Exchange:
    def __init__(self, ring, x, bits):
        self.ring, self.rows, self.bits = ring, x.shape[0], bits
        self.parts, self.new, self.masks = [], [x], [0]

    def take(self, *others):
        self.parts, new = tie((self.parts, self.new), *others)
        self.parts = list(self.parts) + list(new)
        if len(self.masks) == 2:
            self.parts = [jnp.stack(self.parts).reshape(2 * self.rows, -1)]

    def step(self, *others):
        bit = self.bits[len(self.masks).bit_length() - 1]
        self.take(*others)
        self.sent = tuple(self.parts)
        pairs = [(d, d ^ (2 * bit)) for d in range(self.ring.shards)]
        self.new = [lax.ppermute(x, "shard", pairs) for x in self.parts]
        self.masks += [m ^ bit for m in self.masks]

    def finish(self, *others):
        self.take(*others)
        entries, at = [], 0
        for own in self.parts:
            other = self.ring.sibling(own)
            for i in range(own.shape[0] // self.rows):
                entries.append((own, at, 0, i * self.rows, self.rows))
                entries.append((other, len(self.masks) + at, 0, i * self.rows, self.rows))
                at += 1
        return Pieces(entries, self.rows, self.ring.shards)

    def origin_table(self, me):
        core = me % 2
        own = jnp.bitwise_xor(me // 2, jnp.asarray(self.masks, jnp.int32))
        return jnp.concatenate([2 * own + core, 2 * own + 1 - core])


class Reduce:
    def __init__(self, ring, *groups):
        self.ring, self.steps = ring, 0
        self.groups = list(groups)

    def step(self, *others):
        ring, far = self.ring, self.ring.chips // 2
        rows = self.groups[0][0].shape[1]
        half = half_of(rows)
        self.steps += 1
        k = far - self.steps + 1
        if self.steps == 1:
            groups = tie(self.groups, *others)
            outputs = [(far, 0, half, []), (far, half, rows - half, [])]
        else:
            groups, ahead, behind = tie((self.groups, self.ahead, self.behind), *others)
            first = half if self.steps == 2 else 0
            outputs = [(k, 0, rows, [(ahead, 0)]), (ring.chips - k, 0, rows, [(behind, first)])]
        self.sent = tuple(sum_call(groups, outputs))
        self.ahead = ring.forward(self.sent[0])
        self.behind = ring.backward(self.sent[1])

    def ahead_behind(self):
        return self.ahead, self.behind

    def result(self, more, *others):
        groups, ahead, behind = tie((self.groups, self.ahead, self.behind), *others)
        rows = groups[0][0].shape[1]
        return sum_call(groups, [(0, 0, rows, [(ahead, 0), (behind, 0), (more, 0)])])[0]


def swap_seq(x):
    return lax.ppermute(x, "seq", [(0, 1), (1, 0)])


def over_seq(x):
    low = x.astype(BF)
    return low.astype(F32) + swap_seq(low).astype(F32)


def body(
    tokens,
    qkv_weight,
    out_weight,
    up_weight,
    down_weight,
    norm_gains,
    biases,
    up_bias,
    position_table,
    segment_docs,
    cotangent,
):
    shards = lax.axis_size("shard")
    me = lax.axis_index("shard")
    rows, width = tokens.shape
    segs = rows // SEG
    ff = up_weight.shape[2]
    group = ff // width
    own = width // shards
    places_n = position_table.shape[0]
    docs = segment_docs[0]
    ringed = own == 48 and places_n == 64 and shards % 4 == 0
    ring = Ring(shards)
    place = me[None]

    if ringed:
        chips, cores, chunk = ring.chips, 2, own
        behind = jnp.asarray(ring.behind_table(), jnp.int32)[me]
        core = me % 2
        origin = jnp.stack([2 * behind + core, 2 * behind + 1 - core], axis=1).reshape(-1)
        table = jnp.concatenate([jnp.asarray(ring.slot_table(), jnp.int32)[me], (me * segs)[None]])
        first, feed, other = pack_call(
            own, width, ff, qkv_weight, out_weight, up_weight, down_weight, norm_gains, biases, up_bias, position_table
        )
        g_a, g_f, x_w = Gather(ring, first), Gather(ring, feed), Gather(ring, other)
        g_a.step()
        g_a.step()
        g_a.step()
        g_f.step(*g_a.sent)
        g_a.step()
        p_a = g_a.finish()
        g_f.step(*g_a.sent)
        vec0, vec1, tab, upb = vector_call(origin, p_a, 4 * width, own, width, ff, places_n)
        l_qkv, l_out = (p_a, 0, 3 * width), (p_a, 3 * width, width)
    else:
        chips, cores, chunk = 1, 1, width
        origin = jnp.zeros((1,), jnp.int32)
        table = jnp.stack([jnp.int32(0), jnp.int32(0), me * segs])
        full = [
            [lax.all_gather(w[b], "shard", axis=0, tiled=True) for w in (qkv_weight, out_weight, up_weight, down_weight)]
            for b in range(2)
        ]
        small = []
        for b in range(2):
            small += [norm_gains[b], biases[b], up_bias[b].reshape(group, own), jnp.zeros((VEC_ROWS - UP0 - group, own), BF)]
        small = jnp.concatenate(small + [position_table], axis=0)
        small_all = lax.all_gather(small, "shard", axis=1, tiled=True).astype(F32)
        vec0, vec1, tab = small_all[:VEC_ROWS], small_all[VEC_ROWS : 2 * VEC_ROWS], small_all[2 * VEC_ROWS :]
        upb = [
            v[UP0 : UP0 + group].reshape(group, shards, own).transpose(1, 0, 2).reshape(1, ff) for v in (vec0, vec1)
        ]
        upb = jnp.concatenate(upb + [jnp.zeros((6, ff), F32)], axis=0)

        def single(x):
            return Pieces([(x, 0, 0, 0, x.shape[0])], x.shape[0], 1)

        w0, w1 = [[(single(x), 0, x.shape[1]) for x in full[b]] for b in range(2)]
        l_qkv, l_out, l_up, l_down = w0

    def gated(x, *sent):
        return tie(x, *[y for z in sent for y in z]) if ringed else x

    gate = gated(origin, g_f.sent) if ringed else origin
    qkv = project_call(gate, tokens, vec0, Loader(l_qkv))
    if ringed:
        g_f.step(qkv)
        gate = gated(origin, g_f.sent)
    a, o, h, hb, n1, r1 = attention_call(gate, tokens, qkv, vec0, Loader(l_out))
    if ringed:
        g_f.step(o)
        x_w.step(*g_f.sent)
        p_f = g_f.finish()
        l_up, l_down = (p_f, 0, ff), (p_f, ff, width, group)
        gate = gated(origin, x_w.sent)
    y, g, gp, dz, dm, pay, sums2 = feed_call(gate, h, cotangent, o, n1, r1, vec0, upb, Loader(l_up, l_down), ff)

    pay = pay.astype(BF)
    gate = origin
    if ringed:
        exchange = Exchange(ring, pay, (1, 4, 2))
        exchange.step()
        x_w.step(dm)
        gate = gated(origin, exchange.sent, x_w.sent)
    du, dz1, db, do, sums1, up_sums = feed_back_call(gate, dz, gp, n1, r1, vec0, Loader(l_down, l_up, l_out))
    gate = table
    if ringed:
        exchange.step(du)
        x_w.step(du, *exchange.sent)
        gate = gated(table, exchange.sent, x_w.sent)
    main = list(grads_feed_call(tie(gate, du), g, dm, hb, du, chips, cores, chunk))
    gate = table
    if ringed:
        x_w.take_arrived(main[0])
        exchange.step(main[0], *x_w.sent)
        x_w.share_arrived(exchange.sent)
        main[1] = ring.sibling(tie(main[1], *exchange.sent))
        gate = gated(table, exchange.sent)
    main_o = list(grads_out_call(tie(gate, main[0]), o, db, chips, cores, chunk))
    gate = origin
    if ringed:
        p_p = exchange.finish(main_o[0])
        x_w.send(main_o[0], *p_p.arrays, *[e[0] for e in x_w.pending])
        main_o[1] = ring.sibling(tie(main_o[1], *x_w.sent))
        pay_origin = exchange.origin_table(me)
        gate = gated(origin, x_w.sent)
    else:
        p_p = single(lax.all_gather(pay, "shard", axis=0, tiled=True))
        pay_origin = origin

    pay_cross, pay_all, g_f, gp_f, n2_f, r2_f = first_forward_call(
        tie(gate, main_o[0]), pay_origin, p_p, vec0, upb, Loader(l_up, l_down), ff
    )
    gate = origin
    if ringed:
        r_m = Reduce(ring, tuple(main), tuple(main_o))
        r_m.step(g_f)
        p_x = x_w.finish(g_f)
        at = 4 * width
        w1 = (p_x, 0, 3 * width), (p_x, 3 * width, width), (p_x, at, ff), (p_x, at + ff, width, group)
        gate = gated(origin, r_m.sent)
    cross_out, d_cross, c_all, c_sums, c_tab = cross_call(
        tie(gate, g_f), place, pay_cross, docs, tab, vec1, upb, Loader(*w1), ff, own, 128 if ringed else 0
    )
    gate = origin
    if ringed:
        r_m.step(d_cross)
        c_swap = swap_seq(tie(c_all, *r_m.sent))
        gate = gated(origin, r_m.sent)
    dz1_first, do_first, du_f, dm_f, db_f, total_f = first_call(
        gate, pay_all, d_cross, gp_f, n2_f, r2_f, vec0, Loader(l_down, l_up, l_out)
    )
    gate = table
    if ringed:
        r_m.step(do_first)
        gate = gated(table, r_m.sent)
    dqkv, sums_v, *tail = attention_back_call(
        gate, qkv, a, do, tokens, do_first, sums1, sums2, up_sums, chips, cores, chunk
    )
    gate = origin
    if ringed:
        tail[1] = ring.sibling(tie(tail[1], *r_m.ahead_behind()))
        r_m.step(tail[0])
        r_q = Reduce(ring, tuple(tail))
        r_q.step(*r_m.sent)
        gate = gated(origin, r_q.sent)
    d_tokens = input_grad_call(gate, table[-1:], dqkv, dz1, dz1_first, Loader(l_qkv))
    sent = ()
    if ringed:
        r_q.step(d_tokens, c_swap)
        sent = r_q.sent
    sums_shape = jax.ShapeDtypeStruct((own, 3 * width + 128), BF) if ringed else jax.ShapeDtypeStruct((VEC_ROWS, own), F32)
    f_all, f_sums = first_grads_call(
        gated(place, sent), pay_all, d_cross, g_f, n2_f, du_f, dm_f, db_f, total_f, own, sums_shape
    )
    if ringed:
        m_all = r_m.result(f_all)
        r_q.step(m_all)
        m_swap = swap_seq(tie(m_all, *r_q.sent))
        y, cross_out = tie((y, cross_out), *r_q.sent)
    own_rows = lax.dynamic_slice_in_dim(cross_out, me * segs, segs, 0)
    merged = y.reshape(segs, SEG, width).at[:, 0, :].set(own_rows.astype(BF)).reshape(rows, width)
    if ringed:
        r_q.step()
        grad_up, grad_out, grad_down = finish_call(ff, width, m_all, tie(m_swap, *r_q.sent), c_all, c_swap)
        q_all = r_q.result(f_sums)
        grad_qkv, grad_gains, grad_biases, grad_up_bias, grad_table = finish_last_call(
            own, width, group, places_n, q_all, swap_seq(q_all), c_all, c_swap
        )
    else:

        def scattered(x):
            return lax.psum_scatter(x, "shard", scatter_dimension=0, tiled=True)

        def blocks(x):
            return jnp.concatenate([x[:, j * width : (j + 1) * width] for j in range(group)], axis=0)

        feed_sum, main_u, q_sum = main[0][0], scattered(jnp.concatenate([main[0][0][:, ff:], main_o[0][0]], axis=1)), scattered(tail[0][0])
        main_d = scattered(blocks(feed_sum[:, :ff]))
        c_down, c_feed, c_qkv = blocks(c_all[:, :ff]), c_all[:, ff : 2 * ff + width], c_all[:, 2 * ff + width :]
        grad_down = jnp.stack([over_seq(main_d.astype(F32) + blocks(f_all[:, :ff]).astype(F32)), over_seq(c_down)])
        both = jnp.stack([over_seq(main_u.astype(F32) + f_all[:, ff:].astype(F32)), over_seq(c_feed)])
        grad_up, grad_out = both[:, :, :ff], both[:, :, ff:]
        grad_qkv = jnp.stack([over_seq(q_sum), over_seq(c_qkv)])
        vec_sums = jnp.concatenate(
            [sums1[0:1], sums2[0:1], sums_v[0:1], sums1[2:3], sums2[2:3], sums1[1:2], sums2[1:2], jnp.zeros((1, width), F32)]
            + [up_sums[0].reshape(group, width)],
            axis=0,
        )
        vec_sums = lax.psum(vec_sums, ("seq", "shard"))
        seg_vec = lax.dynamic_slice_in_dim(vec_sums[:8], me * own, own, 1)
        seg_up = lax.dynamic_slice_in_dim(vec_sums[8:].reshape(ff), me * own * group, own * group, 0)
        few = over_seq(jnp.concatenate([f_sums, c_sums, c_tab], axis=0))
        first_vec, cross_vec, grad_table = few[:VEC_ROWS], few[VEC_ROWS : 2 * VEC_ROWS], few[2 * VEC_ROWS :]
        seg_vec = seg_vec + first_vec[:8]
        grad_gains = jnp.stack([seg_vec[:2], cross_vec[:2]])
        grad_biases = jnp.stack([seg_vec[2:7], cross_vec[2:7]])
        seg_up = seg_up + first_vec[UP0 : UP0 + group].reshape(-1)
        grad_up_bias = jnp.stack([seg_up, cross_vec[UP0 : UP0 + group].reshape(-1)])
    return (
        merged,
        d_tokens,
        grad_qkv,
        grad_out,
        grad_up,
        grad_down,
        grad_gains,
        grad_biases,
        grad_up_bias,
        grad_table,
    )


def solution(mesh):
    in_specs = (
        P(("seq", "shard"), None),
        P(None, "shard", None),
        P(None, "shard", None),
        P(None, "shard", None),
        P(None, "shard", None),
        P(None, None, "shard"),
        P(None, None, "shard"),
        P(None, "shard"),
        P(None, "shard"),
        P("seq", None),
        P(("seq", "shard"), None),
    )
    out_specs = (
        P(("seq", "shard"), None),
        P(("seq", "shard"), None),
        P(None, "shard", None),
        P(None, "shard", None),
        P(None, "shard", None),
        P(None, "shard", None),
        P(None, None, "shard"),
        P(None, None, "shard"),
        P(None, "shard"),
        P(None, "shard"),
    )
    return jax.shard_map(body, mesh=mesh, in_specs=in_specs, out_specs=out_specs, check_vma=False)
```

```python
from functools import partial

import jax
import jax.numpy as jnp
from jax import lax
from jax.experimental import pallas as pl
from jax.experimental.pallas import tpu as pltpu
from jax.sharding import PartitionSpec as P

HEAD = 64
SEG = 128
EPSILON = 1e-05
MASKED = -1e30
BF = jnp.bfloat16
F32 = jnp.float32
TILE = 256
VMEM_LIMIT = 67043328

GAIN1, GAIN2, BIAS_V, BIAS_O, BIAS_D, SHIFT1, SHIFT2, UP0 = 0, 1, 2, 3, 4, 5, 6, 7
VEC_ROWS = 16


def dot_nn(a, b):
    return lax.dot_general(a, b, (((1,), (0,)), ((), ())), preferred_element_type=F32)


def dot_nt(a, b):
    return lax.dot_general(a, b, (((1,), (1,)), ((), ())), preferred_element_type=F32)


def dot_tn(a, b):
    return lax.dot_general(a, b, (((0,), (0,)), ((), ())), preferred_element_type=F32)


def row_mean(x):
    return jnp.mean(x, axis=-1, keepdims=True)


def col_sum(x):
    return jnp.sum(x.astype(F32), axis=0, keepdims=True)


def norm_rows(z):
    centred = z - row_mean(z)
    inverse = lax.rsqrt(row_mean(centred * centred) + EPSILON)
    return centred * inverse, inverse


def norm_back(scaled, normed, inverse):
    return inverse * (scaled - row_mean(scaled) - normed * row_mean(scaled * normed))


def gelu_both(u):
    phi = 0.5 + 0.5 * lax.erf(u * (2.0**-0.5))
    return u * phi, phi + u * jnp.exp(-0.5 * u * u) * 0.3989422804014327


def halves(pair):
    lane = lax.broadcasted_iota(jnp.int32, pair.shape, 1)
    zero = jnp.zeros_like(pair)
    return jnp.concatenate([jnp.where(lane < HEAD, pair, zero), jnp.where(lane < HEAD, zero, pair)], axis=0)


def side_by_side(stacked):
    rows = stacked.shape[0] // 2
    return jnp.concatenate([stacked[:rows], stacked[rows:]], axis=1)


def pairs_forward(q, k, v, allowed):
    scores = [dot_nt(halves(a), b) * (HEAD**-0.5) for a, b in zip(q, k)]
    if allowed is not None:
        scores = [jnp.where(allowed, x, MASKED) for x in scores]
    powers = [jnp.exp(x - jnp.max(x, axis=-1, keepdims=True)) for x in scores]
    weights = [(x / jnp.sum(x, axis=-1, keepdims=True)).astype(BF) for x in powers]
    return [(w, dot_nn(side_by_side(w), halves(x)).astype(BF)) for w, x in zip(weights, v)]


def pairs_backward(q, k, v, weights, d_out):
    d_stacks = [halves(x) for x in d_out]
    d_weights = [dot_nt(x, y) for x, y in zip(d_stacks, v)]
    wide = [w.astype(F32) for w in weights]
    inner = [jnp.sum(w * x, axis=-1, keepdims=True) for w, x in zip(wide, d_weights)]
    d_scores = [(w * (x - y)).astype(BF) for w, x, y in zip(wide, d_weights, inner)]
    scale = HEAD**-0.5
    d_q = [(dot_nn(side_by_side(x), halves(y)) * scale).astype(BF) for x, y in zip(d_scores, k)]
    d_k = [(dot_tn(x, halves(y)) * scale).astype(BF) for x, y in zip(d_scores, q)]
    d_v = [dot_tn(w, x).astype(BF) for w, x in zip(weights, d_stacks)]
    return zip(d_q, d_k, d_v)


class Copies:
    def __init__(self, copies):
        self.all = copies

    def start(self):
        start_all(self.all)

    def wait(self):
        wait_all(self.all)


class Pieces:
    def __init__(self, entries, chunk, origins):
        self.entries = list(entries)
        self.chunk, self.origins = chunk, origins
        self.rows = chunk * origins
        self.count = len(self.entries)
        self.arrays, self.which = [], []
        for x, *_ in self.entries:
            at = [i for i, y in enumerate(self.arrays) if y is x]
            if not at:
                self.arrays.append(x)
            self.which.append(at[0] if at else len(self.arrays) - 1)

    def copies(self, refs, origin, sems, col, width, dst, by_origin=False, blocks=1):
        def build(refs, entries, sem0):
            out = []
            for n, (ref, (x, entry, first, top, rows)) in enumerate(zip(refs, entries)):
                for j in range(blocks):
                    if by_origin:
                        to = dst.at[origin[entry], pl.ds(first, rows), :]
                    else:
                        start = (origin[entry] * blocks + j) * self.chunk + first
                        to = dst.at[pl.ds(pl.multiple_of(start, 16 if rows % 16 == 0 else 8), rows), :]
                    source = ref.at[pl.ds(top, rows), pl.ds(col + j * width, width)]
                    out.append(pltpu.make_async_copy(source, to, sems.at[(sem0 + n) * blocks + j]))
            return out

        return Copies(build([refs[i] for i in self.which], self.entries, 0))


class Loader:
    def __init__(self, *items):
        self.items = [(*item, 1)[:4] for item in items]
        self.groups = []
        for pieces, *_ in items:
            if pieces not in self.groups:
                self.groups.append(pieces)
        self.arrays = [x for g in self.groups for x in g.arrays]
        self.count = len(self.arrays)

    def scratch(self):
        buffers = [pltpu.VMEM((p.rows * blocks, width), BF) for p, _, width, blocks in self.items]
        return buffers + [pltpu.SemaphoreType.DMA((p.count * blocks,)) for p, _, _, blocks in self.items]

    def start(self, srcs, origin, scratch):
        at, where = 0, {}
        for g in self.groups:
            where[id(g)] = srcs[at : at + len(g.arrays)]
            at += len(g.arrays)
        m = len(self.items)
        sets = [
            p.copies(where[id(p)], origin, scratch[m + i], col, width, scratch[i], blocks=blocks)
            for i, (p, col, width, blocks) in enumerate(self.items)
        ]
        for copies in sets:
            copies.start()
        return [copies.wait for copies in sets]


def start_all(copies):
    for c in copies:
        c.start()


def wait_all(copies):
    for c in copies:
        c.wait()


ANY = pl.BlockSpec(memory_space=pl.ANY)
SMEM = pl.BlockSpec(memory_space=pltpu.SMEM)


def whole(shape):
    return pl.BlockSpec(shape, lambda *i: (0,) * len(shape), pipeline_mode=pl.Buffered(1))


def whole_out(shape):
    return pl.BlockSpec(shape, lambda *i: (0,) * len(shape))


def tile(*shape):
    return pl.BlockSpec(shape, lambda i: (i,) + (0,) * (len(shape) - 1))


def cost(flops, nbytes):
    return pl.CostEstimate(flops=int(flops * 0.01), bytes_accessed=int(nbytes * 0.01), transcendentals=0)


def project_kernel(load, width, *refs):
    n = load.count
    origin, x_ref, vec = refs[0], refs[1], refs[2]
    srcs = refs[3 : 3 + n]
    qkv_ref = refs[3 + n]
    scratch = refs[4 + n :]
    wqkv = scratch[0]

    @pl.when(pl.program_id(0) == 0)
    def _():
        for wait in load.start(srcs, origin, scratch):
            wait()

    qkv = dot_nn(x_ref[...], wqkv[...])
    qkv_ref[:, : 2 * width] = qkv[:, : 2 * width].astype(BF)
    qkv_ref[:, 2 * width :] = (qkv[:, 2 * width :] + vec[BIAS_V : BIAS_V + 1, :]).astype(BF)


def project_call(origin, x, vec, load):
    rows, width = x.shape
    return pl.pallas_call(
        partial(project_kernel, load, width),
        grid=(rows // TILE,),
        in_specs=[SMEM, tile(TILE, width), whole(vec.shape)] + [ANY] * load.count,
        out_specs=tile(TILE, 3 * width),
        out_shape=jax.ShapeDtypeStruct((rows, 3 * width), BF),
        scratch_shapes=load.scratch(),
        compiler_params=pltpu.CompilerParams(vmem_limit_bytes=VMEM_LIMIT),
        cost_estimate=cost(2 * rows * width * 3 * width, 10 * rows * width),
        name="segment_project",
    )(origin, x, vec, *load.arrays)


def attention_kernel(load, width, *refs):
    n = load.count
    origin, x_ref, qkv_ref, vec = refs[:4]
    srcs = refs[4 : 4 + n]
    a_ref, o_ref, h_ref, hb_ref, n_ref, r_ref = refs[4 + n : 10 + n]
    scratch = refs[10 + n :]
    wout = scratch[0]

    @pl.when(pl.program_id(0) == 0)
    def _():
        for wait in load.start(srcs, origin, scratch):
            wait()

    for s in range(TILE // SEG):
        rows = pl.ds(s * SEG, SEG)
        pairs = range(width // 128)
        q = [qkv_ref[rows, pl.ds(p * 128, 128)] for p in pairs]
        k = [qkv_ref[rows, pl.ds(width + p * 128, 128)] for p in pairs]
        v = [qkv_ref[rows, pl.ds(2 * width + p * 128, 128)] for p in pairs]
        for p, (weights, out) in enumerate(pairs_forward(q, k, v, None)):
            a_ref[s, p] = weights
            o_ref[rows, pl.ds(p * 128, 128)] = out
    z = x_ref[...].astype(F32) + dot_nn(o_ref[...], wout[...]) + vec[BIAS_O : BIAS_O + 1, :]
    normed, inverse = norm_rows(z)
    h = normed * vec[GAIN1 : GAIN1 + 1, :] + vec[SHIFT1 : SHIFT1 + 1, :]
    h_ref[...] = h
    hb_ref[...] = h.astype(BF)
    n_ref[...] = normed.astype(BF)
    r_ref[...] = inverse


def attention_call(origin, x, qkv, vec, load):
    rows, width = x.shape
    n = load.count
    segs = rows // SEG
    pairs = width // 128
    return pl.pallas_call(
        partial(attention_kernel, load, width),
        grid=(rows // TILE,),
        in_specs=[SMEM, tile(TILE, width), tile(TILE, 3 * width), whole(vec.shape)] + [ANY] * n,
        out_specs=[
            tile(TILE // SEG, pairs, 2 * SEG, SEG),
            tile(TILE, width),
            tile(TILE, width),
            tile(TILE, width),
            tile(TILE, width),
            tile(TILE, 1),
        ],
        out_shape=[
            jax.ShapeDtypeStruct((segs, pairs, 2 * SEG, SEG), BF),
            jax.ShapeDtypeStruct((rows, width), BF),
            jax.ShapeDtypeStruct((rows, width), F32),
            jax.ShapeDtypeStruct((rows, width), BF),
            jax.ShapeDtypeStruct((rows, width), BF),
            jax.ShapeDtypeStruct((rows, 1), F32),
        ],
        scratch_shapes=load.scratch(),
        compiler_params=pltpu.CompilerParams(vmem_limit_bytes=VMEM_LIMIT),
        cost_estimate=cost(2 * rows * width * 2 * width, 16 * rows * width),
        name="segment_attention",
    )(origin, x, qkv, vec, *load.arrays)


def feed_kernel(load, width, ff, *refs):
    n = load.count
    origin, h_ref, c_ref, o_ref, n_ref, r_ref, vec, upb = refs[:8]
    srcs = refs[8 : 8 + n]
    y_ref, g_ref, gp_ref, dz_ref, dm_ref, pay_ref, sums_ref = refs[8 + n : 15 + n]
    scratch = refs[15 + n :]
    wup, wdown = scratch[:2]

    @pl.when(pl.program_id(0) == 0)
    def _():
        for wait in load.start(srcs, origin, scratch):
            wait()
        sums_ref[...] = jnp.zeros_like(sums_ref)

    h = h_ref[...]
    hb = h.astype(BF)
    block = 512
    total = jnp.zeros((TILE, width), F32)
    u = dot_nn(hb, wup[:, :block]) + upb[0:1, :block]
    for j in range(ff // block):
        cols = slice(j * block, (j + 1) * block)
        if (j + 1) * block < ff:
            later = slice((j + 1) * block, (j + 2) * block)
            u_next = dot_nn(hb, wup[:, later]) + upb[0:1, later]
        active, slope = gelu_both(u)
        active = active.astype(BF)
        g_ref[:, cols] = active
        gp_ref[:, cols] = slope.astype(BF)
        total = total + dot_nn(active, wdown[cols, :])
        u = u_next
    normed, inverse = norm_rows(h + total + vec[BIAS_D : BIAS_D + 1, :])
    gain = vec[GAIN2 : GAIN2 + 1, :]
    y = normed * gain + vec[SHIFT2 : SHIFT2 + 1, :]
    y_ref[...] = y.astype(BF)
    row = lax.broadcasted_iota(jnp.int32, (TILE, 1), 0)
    dy = jnp.where(row % SEG == 0, 0.0, c_ref[...].astype(F32))
    dz = norm_back(dy * gain, normed, inverse)
    dz_ref[...] = dz
    dm = dz.astype(BF)
    dm_ref[...] = dm
    sums_ref[0:1, :] += col_sum(dy * normed)
    sums_ref[1:2, :] += col_sum(dy)
    sums_ref[2:3, :] += col_sum(dm)
    lane = lax.broadcasted_iota(jnp.int32, (1, 128), 1)
    for i in range(pay_ref.shape[0] // (TILE // SEG)):

        @pl.when(pl.program_id(0) == i)
        def _(i=i):
            for s in range(TILE // SEG):
                here = slice(s * SEG, s * SEG + 1)
                few = slice(s * SEG, s * SEG + 16)
                at = slice(i * (TILE // SEG) + s, i * (TILE // SEG) + s + 1)
                pay_ref[at, 0:width] = y[here].astype(BF)
                pay_ref[at, width : 2 * width] = c_ref[few, :][:1]
                pay_ref[at, 2 * width : 3 * width] = h[here].astype(BF)
                pay_ref[at, 3 * width : 4 * width] = o_ref[few, :][:1]
                pay_ref[at, 4 * width : 5 * width] = n_ref[few, :][:1]
                high = r_ref[here].astype(BF).astype(F32)
                parts = jnp.where(lane == 0, high, jnp.where(lane == 1, r_ref[here] - high, 0.0))
                pay_ref[at, 5 * width :] = parts.astype(BF)


def feed_call(origin, h, cot, o, n1, r1, vec, upb, load, ff):
    rows, width = h.shape
    n = load.count
    pay = 5 * width + 128
    return pl.pallas_call(
        partial(feed_kernel, load, width, ff),
        grid=(rows // TILE,),
        in_specs=[
            SMEM,
            tile(TILE, width),
            tile(TILE, width),
            tile(TILE, width),
            tile(TILE, width),
            tile(TILE, 1),
            whole(vec.shape),
            whole(upb.shape),
        ]
        + [ANY] * n,
        out_specs=[
            tile(TILE, width),
            tile(TILE, ff),
            tile(TILE, ff),
            tile(TILE, width),
            tile(TILE, width),
            whole_out((rows // SEG, pay)),
            whole_out((8, width)),
        ],
        out_shape=[
            jax.ShapeDtypeStruct((rows, width), BF),
            jax.ShapeDtypeStruct((rows, ff), BF),
            jax.ShapeDtypeStruct((rows, ff), BF),
            jax.ShapeDtypeStruct((rows, width), F32),
            jax.ShapeDtypeStruct((rows, width), BF),
            jax.ShapeDtypeStruct((rows // SEG, pay), BF),
            jax.ShapeDtypeStruct((8, width), F32),
        ],
        scratch_shapes=load.scratch(),
        compiler_params=pltpu.CompilerParams(vmem_limit_bytes=VMEM_LIMIT),
        cost_estimate=cost(4 * rows * width * ff, 4 * rows * ff),
        name="segment_feed",
    )(origin, h, cot, o, n1, r1, vec, upb, *load.arrays)


def feed_back_kernel(load, width, ff, *refs):
    n = load.count
    origin, dz_ref, gp_ref, n_ref, r_ref, vec = refs[:6]
    srcs = refs[6 : 6 + n]
    du_ref, dz1_ref, db_ref, do_ref, sums_ref, upsum_ref = refs[6 + n : 12 + n]
    scratch = refs[12 + n :]
    wdown, wup, wout = scratch[:3]

    @pl.when(pl.program_id(0) == 0)
    def _():
        for wait in load.start(srcs, origin, scratch):
            wait()
        sums_ref[...] = jnp.zeros_like(sums_ref)
        upsum_ref[...] = jnp.zeros_like(upsum_ref)

    dz = dz_ref[...]
    dm = dz.astype(BF)
    block = 512
    total = dz
    dg = dot_nt(dm, wdown[:block, :])
    for j in range(ff // block):
        cols = slice(j * block, (j + 1) * block)
        if (j + 1) * block < ff:
            dg_next = dot_nt(dm, wdown[(j + 1) * block : (j + 2) * block, :])
        du = (dg * gp_ref[:, cols].astype(F32)).astype(BF)
        du_ref[:, cols] = du
        upsum_ref[0:1, cols] += col_sum(du)
        total = total + dot_nt(du, wup[:, cols])
        dg = dg_next
    normed = n_ref[...].astype(F32)
    dz1 = norm_back(total * vec[GAIN1 : GAIN1 + 1, :], normed, r_ref[...])
    dz1_ref[...] = dz1
    db = dz1.astype(BF)
    db_ref[...] = db
    do_ref[...] = dot_nt(db, wout[...]).astype(BF)
    sums_ref[0:1, :] += col_sum(total * normed)
    sums_ref[1:2, :] += col_sum(total)
    sums_ref[2:3, :] += col_sum(db)


def feed_back_call(origin, dz, gp, n1, r1, vec, load):
    rows, width = dz.shape
    ff = gp.shape[1]
    n = load.count
    return pl.pallas_call(
        partial(feed_back_kernel, load, width, ff),
        grid=(rows // TILE,),
        in_specs=[SMEM, tile(TILE, width), tile(TILE, ff), tile(TILE, width), tile(TILE, 1), whole(vec.shape)] + [ANY] * n,
        out_specs=[
            tile(TILE, ff),
            tile(TILE, width),
            tile(TILE, width),
            tile(TILE, width),
            whole_out((8, width)),
            whole_out((8, ff)),
        ],
        out_shape=[
            jax.ShapeDtypeStruct((rows, ff), BF),
            jax.ShapeDtypeStruct((rows, width), F32),
            jax.ShapeDtypeStruct((rows, width), BF),
            jax.ShapeDtypeStruct((rows, width), BF),
            jax.ShapeDtypeStruct((8, width), F32),
            jax.ShapeDtypeStruct((8, ff), F32),
        ],
        scratch_shapes=load.scratch(),
        compiler_params=pltpu.CompilerParams(vmem_limit_bytes=VMEM_LIMIT),
        cost_estimate=cost(4 * rows * width * ff + 2 * rows * width * width, 4 * rows * ff),
        name="segment_feed_back",
    )(origin, dz, gp, n1, r1, vec, *load.arrays)


def spread(table, chips, cores, chunk, first_chip, count, source, outs, put):
    core = table[chips]
    for q in range(count):
        slot = table[first_chip + q]
        for c in range(cores):
            device = q * cores + (jnp.bitwise_xor(core, c) if cores > 1 else 0)
            start = pl.multiple_of(device * chunk, 16)
            put(outs[c], slot, source[pl.ds(start, chunk), :].astype(BF))


def once(shape):
    return pl.BlockSpec(shape, lambda i: (0,) * len(shape), pipeline_mode=pl.Buffered(1))


def grads_feed_kernel(chips, cores, chunk, width, group, *refs):
    table, g_ref, dm_ref, hb_ref, du_ref = refs[:5]
    outs = refs[5 : 5 + cores]
    scratch = refs[5 + cores]
    step = pl.program_id(0)

    @pl.when(step < group)
    def _():
        scratch[...] = dot_tn(g_ref[...], dm_ref[...])
        if chips > 1:
            per = width // (chunk * group * cores)
            core = table[chips]
            for q in range(per):
                slot = table[step * per + q]
                for c in range(cores):
                    device = q * cores + jnp.bitwise_xor(core, c)
                    for j in range(group):
                        start = pl.multiple_of((device * group + j) * chunk, 16)
                        outs[c][slot, :, j * width : (j + 1) * width] = scratch[pl.ds(start, chunk), :].astype(BF)
        else:
            outs[0][0, :, pl.ds(pl.multiple_of(step * width, width), width)] = scratch[...].astype(BF)

    @pl.when(step >= group)
    def _():
        scratch[...] = dot_tn(hb_ref[...], du_ref[...])
        cols = pl.ds(pl.multiple_of(step * width, width), width)

        def put(out, slot, values):
            out[slot, :, cols] = values

        spread(table, chips, cores, chunk, 0, chips, scratch, outs, put)


def grads_feed_call(table, g, dm, hb, du, chips, cores, chunk):
    rows, ff = g.shape
    width = dm.shape[1]
    group = ff // width
    return pl.pallas_call(
        partial(grads_feed_kernel, chips, cores, chunk, width, group),
        grid=(2 * group,),
        in_specs=[
            SMEM,
            pl.BlockSpec((rows, width), lambda i: (0, jnp.minimum(i, group - 1))),
            whole((rows, width)),
            whole((rows, width)),
            pl.BlockSpec((rows, width), lambda i: (0, jnp.maximum(i - group, 0))),
        ],
        out_specs=[once((chips, chunk, 2 * ff))] * cores,
        out_shape=[jax.ShapeDtypeStruct((chips, chunk, 2 * ff), BF)] * cores,
        scratch_shapes=[pltpu.VMEM((width, width), F32)],
        compiler_params=pltpu.CompilerParams(vmem_limit_bytes=VMEM_LIMIT),
        cost_estimate=cost(4 * rows * width * ff, 4 * rows * ff + 4 * width * ff),
        name="grads_feed",
    )(table, g, dm, hb, du)


def grads_out_kernel(chips, cores, chunk, *refs):
    table, o_ref, db_ref = refs[:3]
    outs = refs[3 : 3 + cores]
    scratch = refs[3 + cores]
    scratch[...] = dot_tn(o_ref[...], db_ref[...])

    def put(out, slot, values):
        out[slot] = values

    spread(table, chips, cores, chunk, 0, chips, scratch, outs, put)


def grads_out_call(table, o, db, chips, cores, chunk):
    width = o.shape[1]
    full = pl.BlockSpec(memory_space=pltpu.VMEM)
    return pl.pallas_call(
        partial(grads_out_kernel, chips, cores, chunk),
        in_specs=[SMEM, full, full],
        out_specs=[full] * cores,
        out_shape=[jax.ShapeDtypeStruct((chips, chunk, width), BF)] * cores,
        scratch_shapes=[pltpu.VMEM((width, width), F32)],
        compiler_params=pltpu.CompilerParams(vmem_limit_bytes=VMEM_LIMIT),
        cost_estimate=cost(2 * o.shape[0] * width * width, 8 * width * width),
        name="grads_out",
    )(table, o, db)


def attention_back_kernel(chips, cores, chunk, width, group, *refs):
    table, qkv_ref, a_ref, do_ref, x_ref, do_first, sums1, sums2, up_sums = refs[:9]
    dqkv, sums_ref = refs[9:11]
    outs = refs[11 : 11 + cores]
    total, d_o = refs[11 + cores :]
    step = pl.program_id(0)

    @pl.when(step == 0)
    def _():
        total[...] = jnp.zeros_like(total)
        sums_ref[...] = jnp.zeros_like(sums_ref)

    d_o[...] = do_ref[...].astype(F32)
    for s in range(TILE // SEG):
        at = pl.ds(table[chips + 1] + step * (TILE // SEG) + s, 1)
        d_o[s * SEG : s * SEG + 1, :] = do_first[at, :]
    for s in range(TILE // SEG):
        rows = pl.ds(s * SEG, SEG)
        pairs = range(width // 128)
        q = [qkv_ref[rows, pl.ds(p * 128, 128)] for p in pairs]
        k = [qkv_ref[rows, pl.ds(width + p * 128, 128)] for p in pairs]
        v = [qkv_ref[rows, pl.ds(2 * width + p * 128, 128)] for p in pairs]
        w = [a_ref[s, p] for p in pairs]
        d_out = [d_o[rows, pl.ds(p * 128, 128)].astype(BF) for p in pairs]
        for p, (d_q, d_k, d_v) in enumerate(pairs_backward(q, k, v, w, d_out)):
            dqkv[rows, pl.ds(p * 128, 128)] = d_q
            dqkv[rows, pl.ds(width + p * 128, 128)] = d_k
            dqkv[rows, pl.ds(2 * width + p * 128, 128)] = d_v
    sums_ref[0:1, :] += col_sum(dqkv[:, 2 * width :])
    total[...] += dot_tn(x_ref[...], dqkv[...])

    @pl.when(step == pl.num_programs(0) - 1)
    def _():
        def put(out, slot, values):
            out[slot, :, : 3 * width] = values

        spread(table, chips, cores, chunk, 0, chips, total, outs, put)
        if cores > 1:
            vec = [sums1[0:1], sums2[0:1], sums_ref[0:1], sums1[2:3], sums2[2:3], sums1[1:2], sums2[1:2]]
            vec = jnp.concatenate(vec + [jnp.zeros((1, width), F32)], axis=0)
            pad = jnp.zeros((chunk - UP0 - group, chunk), F32)
            for q in range(chips):
                blocks = []
                for device in (2 * q, 2 * q + 1):
                    own = slice(device * chunk, (device + 1) * chunk)
                    ups = [up_sums[0:1, group * chunk * device + chunk * j : group * chunk * device + chunk * (j + 1)] for j in range(group)]
                    block = jnp.concatenate([vec[:UP0, own]] + ups + [pad], axis=0)
                    blocks.append(jnp.concatenate([block, jnp.zeros((chunk, 128 - chunk), F32)], axis=1))
                for c in range(2):
                    picked = jnp.where(table[chips] == c, blocks[0], blocks[1]).astype(BF)
                    outs[c][table[q], :, 3 * width :] = picked


def attention_back_call(table, qkv, a, do, x, do_first, sums1, sums2, up_sums, chips, cores, chunk):
    rows, width = x.shape
    pairs = width // 128
    cols = 3 * width + (128 if cores > 1 else 0)
    group = up_sums.shape[1] // width
    return pl.pallas_call(
        partial(attention_back_kernel, chips, cores, chunk, width, group),
        grid=(rows // TILE,),
        in_specs=[
            SMEM,
            tile(TILE, 3 * width),
            tile(TILE // SEG, pairs, 2 * SEG, SEG),
            tile(TILE, width),
            tile(TILE, width),
            whole(do_first.shape),
            whole(sums1.shape),
            whole(sums2.shape),
            whole(up_sums.shape),
        ],
        out_specs=[tile(TILE, 3 * width), whole_out((8, width))] + [once((chips, chunk, cols))] * cores,
        out_shape=[jax.ShapeDtypeStruct((rows, 3 * width), BF), jax.ShapeDtypeStruct((8, width), F32)]
        + [jax.ShapeDtypeStruct((chips, chunk, cols), BF)] * cores,
        scratch_shapes=[pltpu.VMEM((width, 3 * width), F32), pltpu.VMEM((TILE, width), F32)],
        compiler_params=pltpu.CompilerParams(vmem_limit_bytes=VMEM_LIMIT),
        cost_estimate=cost(2 * rows * width * 5 * width, 20 * rows * width),
        name="segment_attention_back",
    )(table, qkv, a, do, x, do_first, sums1, sums2, up_sums)


def input_grad_kernel(load, width, *refs):
    n = load.count
    origin, table, dqkv_ref, dz_ref, dz_first = refs[:5]
    srcs = refs[5 : 5 + n]
    dx_ref, d_z = refs[5 + n : 7 + n]
    scratch = refs[7 + n :]
    step = pl.program_id(0)

    @pl.when(step == 0)
    def _():
        for wait in load.start(srcs, origin, scratch):
            wait()

    d_z[...] = dz_ref[...]
    for s in range(TILE // SEG):
        at = pl.ds(table[0] + step * (TILE // SEG) + s, 1)
        d_z[s * SEG : s * SEG + 1, :] = dz_first[at, :]
    dx_ref[...] = (d_z[...] + dot_nt(dqkv_ref[...], scratch[0][...])).astype(BF)


def input_grad_call(origin, first_row, dqkv, dz, dz_first, load):
    rows, width = dz.shape
    n = load.count
    return pl.pallas_call(
        partial(input_grad_kernel, load, width),
        grid=(rows // TILE,),
        in_specs=[SMEM, SMEM, tile(TILE, 3 * width), tile(TILE, width), whole(dz_first.shape)] + [ANY] * n,
        out_specs=tile(TILE, width),
        out_shape=jax.ShapeDtypeStruct((rows, width), BF),
        scratch_shapes=[pltpu.VMEM((TILE, width), F32)] + load.scratch(),
        compiler_params=pltpu.CompilerParams(vmem_limit_bytes=VMEM_LIMIT),
        cost_estimate=cost(2 * rows * width * 3 * width, 12 * rows * width),
        name="input_grad",
    )(origin, first_row, dqkv, dz, dz_first, *load.arrays)


def one_hot(rows, cols, base):
    r = lax.broadcasted_iota(jnp.int32, (rows, cols), 0)
    c = lax.broadcasted_iota(jnp.int32, (rows, cols), 1)
    return (r == c + base).astype(F32).astype(BF)


def window(ref, first, width, base, count):
    size = min(256, width)
    start = jnp.minimum((base // 128) * 128, width - size)
    values = ref[:, pl.ds(pl.multiple_of(start + first, 128), size)]
    return dot_nn(values.astype(BF), one_hot(size, count, base - start))


def few_feed_forward(hb, h, vec, up_row, wup, wdown, g_ref, gp_ref, ff, wait_up, wait_down):
    block = 512
    total = jnp.zeros(h.shape, F32)
    wait_up()
    for j in range(ff // block):
        cols = slice(j * block, (j + 1) * block)
        active, slope = gelu_both(dot_nn(hb, wup[:, cols]) + up_row[:, cols])
        g_ref[:, cols] = active.astype(BF)
        gp_ref[:, cols] = slope.astype(BF)
    wait_down()
    for j in range(ff // block):
        cols = slice(j * block, (j + 1) * block)
        total = total + dot_nn(g_ref[:, cols], wdown[cols, :])
    return norm_rows(h + total + vec[BIAS_D : BIAS_D + 1, :])


def few_backward(dy, n2, r2, n1, r1, vec, wup, wdown, wout, gp_ref, du_ref, ff, wait_down, wait_up, wait_out):
    block = 512
    dz = norm_back(dy * vec[GAIN2 : GAIN2 + 1, :], n2, r2)
    dm = dz.astype(BF)
    total = dz
    wait_down()
    for j in range(ff // block):
        cols = slice(j * block, (j + 1) * block)
        du_ref[:, cols] = (dot_nt(dm, wdown[cols, :]) * gp_ref[:, cols].astype(F32)).astype(BF)
    wait_up()
    for j in range(ff // block):
        cols = slice(j * block, (j + 1) * block)
        total = total + dot_nt(du_ref[:, cols], wup[:, cols])
    dz1 = norm_back(total * vec[GAIN1 : GAIN1 + 1, :], n1, r1)
    db = dz1.astype(BF)
    wait_out()
    return dm, total, dz1, db, dot_nt(db, wout[...])


def few_grads(me, chunk, ff, hb, o, g_ref, du_ref, dm, db, sums, wide, grads):
    block = 512
    width = dm.shape[1]
    group = ff // width
    base = me * chunk
    own_h = window(*hb, width, base, chunk).astype(BF)
    own_o = window(*o, width, base, chunk).astype(BF)
    own_g = window(g_ref, 0, ff, base * group, group * chunk).astype(BF)
    down = dot_tn(own_g, dm).astype(BF)
    for j in range(group):
        grads[:, j * width : (j + 1) * width] = down[j * chunk : (j + 1) * chunk]
    for j in range(ff // block):
        cols = slice(j * block, (j + 1) * block)
        grads[:, ff + j * block : ff + (j + 1) * block] = dot_tn(own_h, du_ref[:, cols]).astype(BF)
    grads[:, 2 * ff : 2 * ff + width] = dot_tn(own_o, db).astype(BF)
    wide[...] = jnp.zeros_like(wide)
    for i, x in enumerate(sums):
        if x is not None:
            wide[i : i + 1, :width] = x
    wide[8:9, :] = col_sum(du_ref[...])
    own_sums = window(wide, 0, width, base, chunk)
    own_up = window(wide, 0, ff, base * group, group * chunk)
    ups = [own_up[8:9, j * chunk : (j + 1) * chunk] for j in range(group)]
    return jnp.concatenate([own_sums[:UP0]] + ups + [jnp.zeros((VEC_ROWS - UP0 - group, chunk), F32)], axis=0)


def cross_kernel(load, width, ff, chunk, places_n, *refs):
    n = load.count
    origin, table, pay_ref, doc_row, tab_ref, vec, upb = refs[:7]
    srcs = refs[7 : 7 + n]
    out_ref, dx_ref, grads, sums_ref, gtab_ref = refs[7 + n : 12 + n]
    qkv, a_ref, o_s, d_s, g_ref, gp_ref, du_ref, low_ref, hb_ref, wide, tab_own = refs[12 + n : 23 + n]
    scratch = refs[23 + n :]
    wqkv, wout, wup, wdown = scratch[:4]
    rows = pay_ref.shape[0]
    me = table[0]
    wait_qkv, wait_out, wait_up, wait_down = load.start(srcs, origin, scratch)
    row_at = lax.broadcasted_iota(jnp.int32, (rows, rows), 0)
    col_at = lax.broadcasted_iota(jnp.int32, (rows, rows), 1)
    earlier = row_at > col_at
    docs = jnp.broadcast_to(doc_row[...].astype(F32), (rows, rows))
    same = docs == jnp.sum(jnp.where(row_at == col_at, docs, 0.0), axis=1, keepdims=True)
    position = jnp.sum(jnp.where(same & earlier, 1.0, 0.0), axis=1, keepdims=True)
    slot = lax.broadcasted_iota(jnp.int32, (rows, places_n), 1).astype(F32)
    lookup = (slot == position).astype(F32).astype(BF)
    entry = pay_ref[:, :width] + dot_nn(lookup, tab_ref[...].astype(BF))
    low = entry.astype(BF)
    low_ref[...] = low
    allowed = jnp.concatenate([same, same], axis=0)
    wait_qkv()
    proj = dot_nn(low, wqkv[...])
    qkv[:, : 2 * width] = proj[:, : 2 * width].astype(BF)
    qkv[:, 2 * width :] = (proj[:, 2 * width :] + vec[BIAS_V : BIAS_V + 1, :]).astype(BF)
    pairs = range(width // 128)

    def lanes(ref, p, first=0):
        return ref[:, first + p * 128 : first + (p + 1) * 128]

    together = len(pairs) if rows <= 128 else 1
    for at in range(0, len(pairs), together):
        some = range(at, at + together)
        q = [lanes(qkv, p) for p in some]
        k = [lanes(qkv, p, width) for p in some]
        v = [lanes(qkv, p, 2 * width) for p in some]
        for p, (weights, out) in zip(some, pairs_forward(q, k, v, allowed)):
            a_ref[p] = weights
            o_s[:, p * 128 : (p + 1) * 128] = out
    wait_out()
    o = o_s[...]
    n1, r1 = norm_rows(entry + dot_nn(o, wout[...]) + vec[BIAS_O : BIAS_O + 1, :])
    h = n1 * vec[GAIN1 : GAIN1 + 1, :] + vec[SHIFT1 : SHIFT1 + 1, :]
    hb = h.astype(BF)
    n2, r2 = few_feed_forward(hb, h, vec, upb.at[1:2, :], wup, wdown, g_ref, gp_ref, ff, wait_up, wait_down)
    out_ref[...] = n2 * vec[GAIN2 : GAIN2 + 1, :] + vec[SHIFT2 : SHIFT2 + 1, :]
    dy = pay_ref[:, width:]

    def ready():
        return None

    hb_ref[...] = hb
    dm, total, dz1, db, do = few_backward(
        dy, n2, r2, n1, r1, vec, wup, wdown, wout, gp_ref, du_ref, ff, ready, ready, ready
    )
    do = do.astype(BF)
    for at in range(0, len(pairs), together):
        some = range(at, at + together)
        q = [lanes(qkv, p) for p in some]
        k = [lanes(qkv, p, width) for p in some]
        v = [lanes(qkv, p, 2 * width) for p in some]
        w = [a_ref[p] for p in some]
        d_out = [do[:, p * 128 : (p + 1) * 128] for p in some]
        for p, (d_q, d_k, d_v) in zip(some, pairs_backward(q, k, v, w, d_out)):
            d_s[:, p * 128 : (p + 1) * 128] = d_q
            d_s[:, width + p * 128 : width + (p + 1) * 128] = d_k
            d_s[:, 2 * width + p * 128 : 2 * width + (p + 1) * 128] = d_v
    d_all = d_s[...]
    d_in = dz1 + dot_nt(d_all, wqkv[...])
    dx_ref[...] = d_in
    dv = col_sum(d_all[:, 2 * width :])
    sums = [col_sum(total * n1), col_sum(dy * n2), dv, col_sum(db), col_sum(dm), col_sum(total), col_sum(dy)]
    sums = few_grads(me, chunk, ff, (hb_ref, 0), (o_s, 0), g_ref, du_ref, dm, db, sums, wide, grads)
    base = 2 * ff + width
    own_low = window(low_ref, 0, width, me * chunk, chunk).astype(BF)
    grads[:, base : base + 3 * width] = dot_tn(own_low, d_all).astype(BF)
    high = d_in.astype(BF)
    rest = (d_in - high.astype(F32)).astype(BF)
    tab_own[...] = dot_tn(lookup, high) + dot_tn(lookup, rest)
    own_tab = window(tab_own, 0, width, me * chunk, chunk)
    sums_ref[...] = sums
    gtab_ref[...] = own_tab
    if grads.shape[1] > base + 3 * width:
        high = 2 * VEC_ROWS
        gap = jnp.zeros((chunk, 64 - chunk), F32)
        left = jnp.concatenate([sums, jnp.zeros((VEC_ROWS, chunk), F32), own_tab[: chunk - high]], axis=0)
        grads[:, base + 3 * width :] = jnp.concatenate([left, gap, own_tab[chunk - high :], gap], axis=1).astype(BF)


def cross_call(origin, table, pay, docs, tab, vec, upb, load, ff, chunk, extra):
    rows, width = pay.shape[0], vec.shape[1]
    n = load.count
    group = ff // width
    pairs = width // 128
    full = pl.BlockSpec(memory_space=pltpu.VMEM)
    return pl.pallas_call(
        partial(cross_kernel, load, width, ff, chunk, tab.shape[0]),
        in_specs=[SMEM, SMEM] + [full] * 5 + [ANY] * n,
        out_specs=[full] * 5,
        out_shape=[
            jax.ShapeDtypeStruct((rows, width), F32),
            jax.ShapeDtypeStruct((rows, width), F32),
            jax.ShapeDtypeStruct((chunk, 2 * ff + 4 * width + extra), BF),
            jax.ShapeDtypeStruct((VEC_ROWS, chunk), F32),
            jax.ShapeDtypeStruct((tab.shape[0], chunk), F32),
        ],
        scratch_shapes=[
            pltpu.VMEM((rows, 3 * width), BF),
            pltpu.VMEM((pairs, 2 * rows, rows), BF),
            pltpu.VMEM((rows, width), BF),
            pltpu.VMEM((rows, 3 * width), BF),
            pltpu.VMEM((rows, ff), BF),
            pltpu.VMEM((rows, ff), BF),
            pltpu.VMEM((rows, ff), BF),
            pltpu.VMEM((rows, width), BF),
            pltpu.VMEM((rows, width), BF),
            pltpu.VMEM((VEC_ROWS, ff), F32),
            pltpu.VMEM((tab.shape[0], width), F32),
        ]
        + load.scratch(),
        compiler_params=pltpu.CompilerParams(vmem_limit_bytes=VMEM_LIMIT),
        cost_estimate=cost(16 * rows * width * ff, 20 * width * width),
        name="cross_block",
    )(origin, table, pay, docs.reshape(1, rows), tab, vec, upb, *load.arrays)


def first_forward_kernel(load, pay_pieces, width, ff, *refs):
    n, m = load.count, len(pay_pieces.arrays)
    origin, pay_origin, vec, upb = refs[:4]
    srcs = refs[4 : 4 + n]
    pay_srcs = refs[4 + n : 4 + n + m]
    cross_ref, pay_ref, g_ref, gp_ref, n_ref, r_ref = refs[4 + n + m : 10 + n + m]
    held, sem = refs[10 + n + m : 12 + n + m]
    scratch = refs[12 + n + m :]
    wup, wdown = scratch[:2]
    copies = pay_pieces.copies(pay_srcs, pay_origin, sem, 0, held.shape[2], held, by_origin=True)
    copies.start()
    wait_up, wait_down = load.start(srcs, origin, scratch)
    copies.wait()
    pay = held[...].astype(F32).reshape(pay_ref.shape[0], held.shape[2])
    cross_ref[...] = pay[:, : 2 * width]
    pay_ref[...] = pay[:, 2 * width :]
    hb = pay_ref[:, :width].astype(BF)
    normed, inverse = few_feed_forward(
        hb, hb.astype(F32), vec, upb.at[0:1, :], wup, wdown, g_ref, gp_ref, ff, wait_up, wait_down
    )
    n_ref[...] = normed
    r_ref[...] = inverse


def first_forward_call(origin, pay_origin, pay_pieces, vec, upb, load, ff):
    width = vec.shape[1]
    rows = pay_pieces.rows
    n, m = load.count, len(pay_pieces.arrays)
    full = pl.BlockSpec(memory_space=pltpu.VMEM)
    return pl.pallas_call(
        partial(first_forward_kernel, load, pay_pieces, width, ff),
        in_specs=[SMEM, SMEM] + [full] * 2 + [ANY] * (n + m),
        out_specs=[full] * 6,
        out_shape=[
            jax.ShapeDtypeStruct((rows, 2 * width), F32),
            jax.ShapeDtypeStruct((rows, pay_pieces.arrays[0].shape[1] - 2 * width), F32),
            jax.ShapeDtypeStruct((rows, ff), BF),
            jax.ShapeDtypeStruct((rows, ff), BF),
            jax.ShapeDtypeStruct((rows, width), F32),
            jax.ShapeDtypeStruct((rows, 1), F32),
        ],
        scratch_shapes=[
            pltpu.VMEM((pay_pieces.origins, pay_pieces.chunk, pay_pieces.arrays[0].shape[1]), BF),
            pltpu.SemaphoreType.DMA((pay_pieces.count,)),
        ]
        + load.scratch(),
        compiler_params=pltpu.CompilerParams(vmem_limit_bytes=VMEM_LIMIT),
        cost_estimate=cost(6 * rows * width * ff, 4 * width * ff),
        name="first_rows_forward",
    )(origin, pay_origin, vec, upb, *load.arrays, *pay_pieces.arrays)


def first_kernel(load, width, ff, *refs):
    n = load.count
    origin, pay_ref, dy_ref, gp_ref, n2_ref, r2_ref, vec = refs[:7]
    srcs = refs[7 : 7 + n]
    dz1_ref, do_ref, du_ref, dm_ref, db_ref, total_ref = refs[7 + n : 13 + n]
    scratch = refs[13 + n :]
    wdown, wup, wout = scratch[:3]
    waits = load.start(srcs, origin, scratch)
    n1 = pay_ref[:, 2 * width : 3 * width]
    r1 = jnp.sum(pay_ref[:, 3 * width :], axis=1, keepdims=True)
    dm, total, dz1, db, do = few_backward(
        dy_ref[...], n2_ref[...], r2_ref[...], n1, r1, vec, wup, wdown, wout, gp_ref, du_ref, ff, *waits
    )
    dm_ref[...] = dm
    db_ref[...] = db
    total_ref[...] = total
    dz1_ref[...] = dz1
    do_ref[...] = do


def first_call(origin, pay, dy, gp, n2, r2, vec, load):
    rows, width = dy.shape
    ff = gp.shape[1]
    n = load.count
    full = pl.BlockSpec(memory_space=pltpu.VMEM)
    return pl.pallas_call(
        partial(first_kernel, load, width, ff),
        in_specs=[SMEM] + [full] * 6 + [ANY] * n,
        out_specs=[full] * 6,
        out_shape=[
            jax.ShapeDtypeStruct((rows, width), F32),
            jax.ShapeDtypeStruct((rows, width), F32),
            jax.ShapeDtypeStruct((rows, ff), BF),
            jax.ShapeDtypeStruct((rows, width), BF),
            jax.ShapeDtypeStruct((rows, width), BF),
            jax.ShapeDtypeStruct((rows, width), F32),
        ],
        scratch_shapes=load.scratch(),
        compiler_params=pltpu.CompilerParams(vmem_limit_bytes=VMEM_LIMIT),
        cost_estimate=cost(8 * rows * width * ff, 4 * width * ff),
        name="first_rows_back",
    )(origin, pay, dy, gp, n2, r2, vec, *load.arrays)


def first_grads_kernel(width, ff, chunk, *refs):
    table, pay_ref, dy_ref, g_ref, n2_ref, du_ref, dm_ref, db_ref, total_ref, grads, sums_ref, wide = refs
    dm, db, total, dy = dm_ref[...], db_ref[...], total_ref[...], dy_ref[...]
    n1 = pay_ref[:, 2 * width : 3 * width]
    sums = [col_sum(total * n1), col_sum(dy * n2_ref[...]), None, col_sum(db), col_sum(dm), col_sum(total), col_sum(dy)]
    sums = few_grads(
        table[0], chunk, ff, (pay_ref, 0), (pay_ref, width), g_ref, du_ref, dm, db, sums, wide, grads
    )
    if sums_ref.shape[1] > chunk:
        sums = jnp.concatenate([sums, jnp.zeros((sums_ref.shape[0] - VEC_ROWS, chunk), F32)], axis=0)
        sums_ref[:, : sums_ref.shape[1] - 128] = jnp.zeros((sums_ref.shape[0], sums_ref.shape[1] - 128), BF)
        sums = jnp.concatenate([sums, jnp.zeros((sums_ref.shape[0], 128 - chunk), F32)], axis=1)
        sums_ref[:, sums_ref.shape[1] - 128 :] = sums.astype(BF)
    else:
        sums_ref[...] = sums


def first_grads_call(table, pay, dy, g, n2, du, dm, db, total, chunk, sums_shape):
    rows, width = dy.shape
    ff = g.shape[1]
    full = pl.BlockSpec(memory_space=pltpu.VMEM)
    return pl.pallas_call(
        partial(first_grads_kernel, width, ff, chunk),
        in_specs=[SMEM] + [full] * 8,
        out_specs=[full] * 2,
        out_shape=[jax.ShapeDtypeStruct((chunk, 2 * ff + width), BF), sums_shape],
        scratch_shapes=[pltpu.VMEM((VEC_ROWS, ff), F32)],
        compiler_params=pltpu.CompilerParams(vmem_limit_bytes=VMEM_LIMIT),
        cost_estimate=cost(2 * rows * width * ff // 4, 8 * rows * ff),
        name="first_rows_grads",
    )(table, pay, dy, g, n2, du, dm, db, total)


def vector_kernel(pieces, col, own, width, ff, *refs):
    n = len(pieces.arrays)
    origin = refs[0]
    srcs = refs[1 : 1 + n]
    vec0, vec1, tab, upb = refs[1 + n : 5 + n]
    held, sem = refs[5 + n :]
    copies = pieces.copies(srcs, origin, sem, col, 128, held, by_origin=True)
    copies.start()
    upb[...] = jnp.zeros_like(upb)
    copies.wait()
    high = 2 * VEC_ROWS
    group = ff // width
    for i in range(pieces.origins):
        block = held[i].astype(F32)
        cols = slice(own * i, own * (i + 1))
        vec0[:, cols] = block[:VEC_ROWS, :own]
        vec1[:, cols] = block[VEC_ROWS:high, :own]
        tab[: own - high, cols] = block[high:own, :own]
        tab[own - high :, cols] = block[:, 64 : 64 + own]
        for b in range(2):
            for j in range(group):
                at = group * own * i + own * j
                upb[b : b + 1, at : at + own] = block[b * VEC_ROWS + UP0 + j : b * VEC_ROWS + UP0 + j + 1, :own]


def vector_call(origin, pieces, col, own, width, ff, places_n):
    n = len(pieces.arrays)
    full = pl.BlockSpec(memory_space=pltpu.VMEM)
    return pl.pallas_call(
        partial(vector_kernel, pieces, col, own, width, ff),
        in_specs=[SMEM] + [ANY] * n,
        out_specs=[full] * 4,
        out_shape=[
            jax.ShapeDtypeStruct((VEC_ROWS, width), F32),
            jax.ShapeDtypeStruct((VEC_ROWS, width), F32),
            jax.ShapeDtypeStruct((places_n, width), F32),
            jax.ShapeDtypeStruct((8, ff), F32),
        ],
        scratch_shapes=[pltpu.VMEM((pieces.origins, own, 128), BF), pltpu.SemaphoreType.DMA((pieces.count,))],
        compiler_params=pltpu.CompilerParams(vmem_limit_bytes=VMEM_LIMIT),
        cost_estimate=cost(1000, 128 * width * 8),
        name="vectors",
    )(origin, *pieces.arrays)


def pack_kernel(own, width, ff, places_n, *refs):
    qkv, out, up, down, gains, biases, upb, table, first, feed, other, side = refs
    group = ff // width
    first[:, : 3 * width] = qkv[0]
    first[:, 3 * width : 4 * width] = out[0]
    other[:, : 3 * width] = qkv[1]
    other[:, 3 * width : 4 * width] = out[1]
    for b, (pack, at) in enumerate(((feed, 0), (other, 4 * width))):
        pack[:, at : at + ff] = up[b]
        for j in range(group):
            pack[:, at + ff + j * width : at + ff + (j + 1) * width] = down[b, j * own : (j + 1) * own, :]
    side[...] = jnp.zeros_like(side)
    for b in range(2):
        at = b * VEC_ROWS
        side[at : at + 2, :own] = gains[b].astype(F32)
        side[at + 2 : at + 7, :own] = biases[b].astype(F32)
        row = upb[...].astype(F32)[b : b + 1]
        for j in range(group):
            side[at + UP0 + j : at + UP0 + j + 1, :own] = row[:, j * own : (j + 1) * own]
    places = table[...].astype(F32)
    high = 2 * VEC_ROWS
    side[high:own, :own] = places[: own - high]
    side[:, 64 : 64 + own] = places[own - high :]
    first[:, 4 * width :] = side[...].astype(BF)


def pack_call(own, width, ff, qkv, out, up, down, gains, biases, upb, table):
    full = pl.BlockSpec(memory_space=pltpu.VMEM)
    return pl.pallas_call(
        partial(pack_kernel, own, width, ff, table.shape[0]),
        in_specs=[full] * 8,
        out_specs=[full] * 3,
        out_shape=[
            jax.ShapeDtypeStruct((own, 4 * width + 128), BF),
            jax.ShapeDtypeStruct((own, 2 * ff), BF),
            jax.ShapeDtypeStruct((own, 4 * width + 2 * ff), BF),
        ],
        scratch_shapes=[pltpu.VMEM((own, 128), F32)],
        compiler_params=pltpu.CompilerParams(vmem_limit_bytes=VMEM_LIMIT),
        cost_estimate=cost(1000, 8 * own * 8 * width),
        name="pack_weights",
    )(qkv, out, up, down, gains, biases, upb, table)


def sum_kernel(plan, widths, *refs):
    groups = len(widths)
    count = sum(2 * groups + len(more) for _, more in plan)
    at = 0
    for out, (shift, more) in zip(refs[count:], plan):
        slots = refs[at : at + 2 * groups]
        at += 2 * groups
        extra = [(ref, first) for ref, first in zip(refs[at : at + len(more)], more)]
        at += len(more)
        rows = out.shape[0]
        edges = sorted({0, rows} | {e for ref, first in extra for e in (first, first + ref.shape[0])})
        for low, high in zip(edges, edges[1:]):
            col = 0
            for g, width in enumerate(widths):
                value = slots[2 * g][0, shift + low : shift + high, :].astype(F32)
                value = value + slots[2 * g + 1][0, shift + low : shift + high, :].astype(F32)
                for ref, first in extra:
                    if first <= low and high <= first + ref.shape[0]:
                        value = value + ref[low - first : high - first, col : col + width].astype(F32)
                out[low:high, col : col + width] = value.astype(BF)
                col += width


def sum_call(groups, outputs):
    args, specs, plan, shapes = [], [], [], []
    widths = [x.shape[2] for x, _ in groups]
    for slot, shift, rows, more in outputs:
        for pair in groups:
            for x in pair:
                args.append(x)
                specs.append(pl.BlockSpec((1,) + x.shape[1:], lambda i, k=slot: (k, 0, 0)))
        for x, _ in more:
            args.append(x)
            specs.append(pl.BlockSpec(x.shape, lambda i: (0, 0)))
        plan.append((shift, [first for _, first in more]))
        shapes.append(jax.ShapeDtypeStruct((rows, sum(widths)), BF))
    return pl.pallas_call(
        partial(sum_kernel, plan, widths),
        grid=(1,),
        in_specs=specs,
        out_specs=[pl.BlockSpec(x.shape, lambda i: (0, 0)) for x in shapes],
        out_shape=shapes,
        compiler_params=pltpu.CompilerParams(vmem_limit_bytes=VMEM_LIMIT),
        cost_estimate=cost(1000, sum(8 * x.shape[0] * x.shape[1] for x in shapes)),
        name="add_pieces",
    )(*args)


def finish_kernel(ff, width, *refs):
    x0, y0, x1, y1, grad_up, grad_out, grad_down = refs
    own = x0.shape[0]
    for b, (x, y) in enumerate(((x0, y0), (x1, y1))):
        for j in range(ff // width):
            cols = slice(j * width, (j + 1) * width)
            grad_down[b, j * own : (j + 1) * own, :] = x[:, cols].astype(F32) + y[:, cols].astype(F32)
        grad_up[b] = x[:, ff : 2 * ff].astype(F32) + y[:, ff : 2 * ff].astype(F32)
        grad_out[b] = x[:, 2 * ff : 2 * ff + width].astype(F32) + y[:, 2 * ff : 2 * ff + width].astype(F32)


def finish_call(ff, width, *args):
    own = args[0].shape[0]
    full = pl.BlockSpec(memory_space=pltpu.VMEM)
    return pl.pallas_call(
        partial(finish_kernel, ff, width),
        in_specs=[full] * 4,
        out_specs=[full] * 3,
        out_shape=[
            jax.ShapeDtypeStruct((2, own, ff), F32),
            jax.ShapeDtypeStruct((2, own, width), F32),
            jax.ShapeDtypeStruct((2, own * ff // width, width), F32),
        ],
        compiler_params=pltpu.CompilerParams(vmem_limit_bytes=VMEM_LIMIT),
        cost_estimate=cost(1000, 16 * own * (2 * ff + width)),
        name="finish_feed",
    )(*args)


def finish_last_kernel(own, width, group, places_n, *refs):
    q0, q0s, q1, q1s, grad_qkv, grad_gains, grad_biases, grad_up_bias, grad_table = refs
    blocks = []
    for b, (x, y) in enumerate(((q0, q0s), (q1, q1s))):
        at = x.shape[1] - 3 * width - 128
        cols = slice(at, at + 3 * width)
        grad_qkv[b] = x[:, cols].astype(F32) + y[:, cols].astype(F32)
        blocks.append(x[:, at + 3 * width :].astype(F32) + y[:, at + 3 * width :].astype(F32))
    for b, block in enumerate(blocks):
        grad_gains[b] = block[:2, :own]
        grad_biases[b] = block[2:7, :own]
        for j in range(group):
            grad_up_bias[b : b + 1, j * own : (j + 1) * own] = block[UP0 + j : UP0 + j + 1, :own]
    high = 2 * VEC_ROWS
    grad_table[: own - high, :] = blocks[1][high:own, :own]
    grad_table[own - high :, :] = blocks[1][:, 64 : 64 + own]


def finish_last_call(own, width, group, places_n, *args):
    full = pl.BlockSpec(memory_space=pltpu.VMEM)
    return pl.pallas_call(
        partial(finish_last_kernel, own, width, group, places_n),
        in_specs=[full] * 4,
        out_specs=[full] * 5,
        out_shape=[
            jax.ShapeDtypeStruct((2, own, 3 * width), F32),
            jax.ShapeDtypeStruct((2, 2, own), F32),
            jax.ShapeDtypeStruct((2, 5, own), F32),
            jax.ShapeDtypeStruct((2, group * own), F32),
            jax.ShapeDtypeStruct((places_n, own), F32),
        ],
        compiler_params=pltpu.CompilerParams(vmem_limit_bytes=VMEM_LIMIT),
        cost_estimate=cost(1000, 48 * own * width),
        name="finish_qkv",
    )(*args)


def tie(x, *others):
    return lax.optimization_barrier((x, others))[0] if others else x


class Ring:
    def __init__(self, shards):
        chips = shards // 2
        self.shards, self.chips = shards, chips
        self.order = list(range(0, chips, 2)) + list(range(chips - 1, 0, -2))
        self.place = {chip: i for i, chip in enumerate(self.order)}

    def shift(self, by):
        pairs = []
        for i, chip in enumerate(self.order):
            to = self.order[(i + by) % self.chips]
            pairs += [(2 * chip, 2 * to), (2 * chip + 1, 2 * to + 1)]
        return pairs

    def forward(self, x):
        return lax.ppermute(x, "shard", self.shift(1))

    def backward(self, x):
        return lax.ppermute(x, "shard", self.shift(-1))

    def sibling(self, x):
        return lax.ppermute(x, "shard", [(i, i ^ 1) for i in range(self.shards)])

    def behind_table(self):
        return [
            [self.order[(self.place[d // 2] - k) % self.chips] for k in range(self.chips)] for d in range(self.shards)
        ]

    def slot_table(self):
        rows = []
        for d in range(self.shards):
            chip = d // 2
            rows.append([(self.place[q] - self.place[chip]) % self.chips for q in range(self.chips)] + [d % 2])
        return rows


def half_of(rows):
    return (rows // 32) * 16 if rows >= 32 else rows


class Gather:
    def __init__(self, ring, x):
        self.ring, self.steps = ring, 0
        self.ahead = self.behind = x
        self.rows = x.shape[0]
        self.entries, self.pending = [], []

    def take(self, *others):
        values = (self.ahead, self.behind, [e[0] for e in self.pending])
        ahead, behind, shared = tie(values, *others)
        for e, x in zip(self.pending, shared):
            self.entries.append((x,) + e[1:])
        self.sent = (ahead, behind)
        far = self.ring.chips // 2
        if self.steps == 0:
            fresh = [(ahead, 0, 0)]
        elif self.steps < far:
            fresh = [(ahead, self.steps, 0), (behind, self.ring.chips - self.steps, 0)]
        else:
            fresh = [(ahead, far, 0), (behind, far, half_of(self.rows))]
        self.entries += [(x, 2 * back, first, 0, x.shape[0]) for x, back, first in fresh]
        return ahead, behind, fresh

    def share(self, fresh):
        self.pending = [(self.ring.sibling(x), 2 * back + 1, first, 0, x.shape[0]) for x, back, first in fresh]

    def step(self, *others):
        self.take_arrived(*others)
        self.send()
        self.share_arrived()

    def take_arrived(self, *others):
        self.ahead, self.behind, self.fresh = self.take(*others)
        self.steps += 1

    def share_arrived(self, others=()):
        self.share([(tie(x, *others), back, first) for x, back, first in self.fresh])

    def send(self, *others):
        ahead, behind = tie((self.ahead, self.behind), *others)
        self.sent = (ahead, behind)
        half = half_of(self.rows)
        last = self.steps == self.ring.chips // 2
        self.ahead = self.ring.forward(ahead[:half] if last else ahead)
        self.behind = self.ring.backward(behind[half:] if last else behind)

    def finish(self, *others):
        self.share(self.take(*others)[2])
        return Pieces(self.entries + self.pending, self.rows, self.ring.shards)


class Exchange:
    def __init__(self, ring, x, bits):
        self.ring, self.rows, self.bits = ring, x.shape[0], bits
        self.parts, self.new, self.masks = [], [x], [0]

    def take(self, *others):
        self.parts, new = tie((self.parts, self.new), *others)
        self.parts = list(self.parts) + list(new)
        if len(self.masks) == 2:
            self.parts = [jnp.stack(self.parts).reshape(2 * self.rows, -1)]

    def step(self, *others):
        bit = self.bits[len(self.masks).bit_length() - 1]
        self.take(*others)
        self.sent = tuple(self.parts)
        pairs = [(d, d ^ (2 * bit)) for d in range(self.ring.shards)]
        self.new = [lax.ppermute(x, "shard", pairs) for x in self.parts]
        self.masks += [m ^ bit for m in self.masks]

    def finish(self, *others):
        self.take(*others)
        entries, at = [], 0
        for own in self.parts:
            other = self.ring.sibling(own)
            for i in range(own.shape[0] // self.rows):
                entries.append((own, at, 0, i * self.rows, self.rows))
                entries.append((other, len(self.masks) + at, 0, i * self.rows, self.rows))
                at += 1
        return Pieces(entries, self.rows, self.ring.shards)

    def origin_table(self, me):
        core = me % 2
        own = jnp.bitwise_xor(me // 2, jnp.asarray(self.masks, jnp.int32))
        return jnp.concatenate([2 * own + core, 2 * own + 1 - core])


class Reduce:
    def __init__(self, ring, *groups):
        self.ring, self.steps = ring, 0
        self.groups = list(groups)

    def step(self, *others):
        ring, far = self.ring, self.ring.chips // 2
        rows = self.groups[0][0].shape[1]
        half = half_of(rows)
        self.steps += 1
        k = far - self.steps + 1
        if self.steps == 1:
            groups = tie(self.groups, *others)
            outputs = [(far, 0, half, []), (far, half, rows - half, [])]
        else:
            groups, ahead, behind = tie((self.groups, self.ahead, self.behind), *others)
            first = half if self.steps == 2 else 0
            outputs = [(k, 0, rows, [(ahead, 0)]), (ring.chips - k, 0, rows, [(behind, first)])]
        self.sent = tuple(sum_call(groups, outputs))
        self.ahead = ring.forward(self.sent[0])
        self.behind = ring.backward(self.sent[1])

    def ahead_behind(self):
        return self.ahead, self.behind

    def result(self, more, *others):
        groups, ahead, behind = tie((self.groups, self.ahead, self.behind), *others)
        rows = groups[0][0].shape[1]
        return sum_call(groups, [(0, 0, rows, [(ahead, 0), (behind, 0), (more, 0)])])[0]


def swap_seq(x):
    return lax.ppermute(x, "seq", [(0, 1), (1, 0)])


def over_seq(x):
    low = x.astype(BF)
    return low.astype(F32) + swap_seq(low).astype(F32)


def body(
    tokens,
    qkv_weight,
    out_weight,
    up_weight,
    down_weight,
    norm_gains,
    biases,
    up_bias,
    position_table,
    segment_docs,
    cotangent,
):
    shards = lax.axis_size("shard")
    me = lax.axis_index("shard")
    rows, width = tokens.shape
    segs = rows // SEG
    ff = up_weight.shape[2]
    group = ff // width
    own = width // shards
    places_n = position_table.shape[0]
    docs = segment_docs[0]
    ringed = own == 48 and places_n == 64 and shards % 4 == 0
    ring = Ring(shards)
    place = me[None]

    if ringed:
        chips, cores, chunk = ring.chips, 2, own
        behind = jnp.asarray(ring.behind_table(), jnp.int32)[me]
        core = me % 2
        origin = jnp.stack([2 * behind + core, 2 * behind + 1 - core], axis=1).reshape(-1)
        table = jnp.concatenate([jnp.asarray(ring.slot_table(), jnp.int32)[me], (me * segs)[None]])
        first, feed, other = pack_call(
            own, width, ff, qkv_weight, out_weight, up_weight, down_weight, norm_gains, biases, up_bias, position_table
        )
        g_a, g_f, x_w = Gather(ring, first), Gather(ring, feed), Gather(ring, other)
        g_a.step()
        g_a.step()
        g_a.step()
        g_f.step(*g_a.sent)
        g_a.step()
        p_a = g_a.finish()
        g_f.step(*g_a.sent)
        vec0, vec1, tab, upb = vector_call(origin, p_a, 4 * width, own, width, ff, places_n)
        l_qkv, l_out = (p_a, 0, 3 * width), (p_a, 3 * width, width)
    else:
        chips, cores, chunk = 1, 1, width
        origin = jnp.zeros((1,), jnp.int32)
        table = jnp.stack([jnp.int32(0), jnp.int32(0), me * segs])
        full = [
            [lax.all_gather(w[b], "shard", axis=0, tiled=True) for w in (qkv_weight, out_weight, up_weight, down_weight)]
            for b in range(2)
        ]
        small = []
        for b in range(2):
            small += [norm_gains[b], biases[b], up_bias[b].reshape(group, own), jnp.zeros((VEC_ROWS - UP0 - group, own), BF)]
        small = jnp.concatenate(small + [position_table], axis=0)
        small_all = lax.all_gather(small, "shard", axis=1, tiled=True).astype(F32)
        vec0, vec1, tab = small_all[:VEC_ROWS], small_all[VEC_ROWS : 2 * VEC_ROWS], small_all[2 * VEC_ROWS :]
        upb = [
            v[UP0 : UP0 + group].reshape(group, shards, own).transpose(1, 0, 2).reshape(1, ff) for v in (vec0, vec1)
        ]
        upb = jnp.concatenate(upb + [jnp.zeros((6, ff), F32)], axis=0)

        def single(x):
            return Pieces([(x, 0, 0, 0, x.shape[0])], x.shape[0], 1)

        w0, w1 = [[(single(x), 0, x.shape[1]) for x in full[b]] for b in range(2)]
        l_qkv, l_out, l_up, l_down = w0

    def gated(x, *sent):
        return tie(x, *[y for z in sent for y in z]) if ringed else x

    gate = gated(origin, g_f.sent) if ringed else origin
    qkv = project_call(gate, tokens, vec0, Loader(l_qkv))
    if ringed:
        g_f.step(qkv)
        gate = gated(origin, g_f.sent)
    a, o, h, hb, n1, r1 = attention_call(gate, tokens, qkv, vec0, Loader(l_out))
    if ringed:
        g_f.step(o)
        x_w.step(*g_f.sent)
        p_f = g_f.finish()
        l_up, l_down = (p_f, 0, ff), (p_f, ff, width, group)
        gate = gated(origin, x_w.sent)
    y, g, gp, dz, dm, pay, sums2 = feed_call(gate, h, cotangent, o, n1, r1, vec0, upb, Loader(l_up, l_down), ff)

    gate = origin
    if ringed:
        exchange = Exchange(ring, pay, (1, 4, 2))
        exchange.step()
        x_w.step(dm)
        gate = gated(origin, exchange.sent, x_w.sent)
    du, dz1, db, do, sums1, up_sums = feed_back_call(gate, dz, gp, n1, r1, vec0, Loader(l_down, l_up, l_out))
    gate = table
    if ringed:
        exchange.step(du)
        x_w.step(du, *exchange.sent)
        gate = gated(table, exchange.sent, x_w.sent)
    main = list(grads_feed_call(tie(gate, du), g, dm, hb, du, chips, cores, chunk))
    gate = table
    if ringed:
        x_w.take_arrived(main[0])
        exchange.step(main[0], *x_w.sent)
        x_w.share_arrived(exchange.sent)
        main[1] = ring.sibling(tie(main[1], *exchange.sent))
        gate = gated(table, exchange.sent)
    main_o = list(grads_out_call(tie(gate, main[0]), o, db, chips, cores, chunk))
    gate = origin
    if ringed:
        p_p = exchange.finish(main_o[0])
        x_w.send(main_o[0], *p_p.arrays, *[e[0] for e in x_w.pending])
        main_o[1] = ring.sibling(tie(main_o[1], *x_w.sent))
        pay_origin = exchange.origin_table(me)
        gate = gated(origin, x_w.sent)
    else:
        p_p = single(lax.all_gather(pay, "shard", axis=0, tiled=True))
        pay_origin = origin

    pay_cross, pay_all, g_f, gp_f, n2_f, r2_f = first_forward_call(
        tie(gate, main_o[0]), pay_origin, p_p, vec0, upb, Loader(l_up, l_down), ff
    )
    gate = origin
    if ringed:
        r_m = Reduce(ring, tuple(main), tuple(main_o))
        r_m.step(g_f)
        p_x = x_w.finish(g_f)
        at = 4 * width
        w1 = (p_x, 0, 3 * width), (p_x, 3 * width, width), (p_x, at, ff), (p_x, at + ff, width, group)
        gate = gated(origin, r_m.sent)
    cross_out, d_cross, c_all, c_sums, c_tab = cross_call(
        tie(gate, g_f), place, pay_cross, docs, tab, vec1, upb, Loader(*w1), ff, own, 128 if ringed else 0
    )
    gate = origin
    if ringed:
        r_m.step(d_cross)
        c_swap = swap_seq(tie(c_all, *r_m.sent))
        gate = gated(origin, r_m.sent)
    dz1_first, do_first, du_f, dm_f, db_f, total_f = first_call(
        gate, pay_all, d_cross, gp_f, n2_f, r2_f, vec0, Loader(l_down, l_up, l_out)
    )
    gate = table
    if ringed:
        r_m.step(do_first)
        gate = gated(table, r_m.sent)
    dqkv, sums_v, *tail = attention_back_call(
        gate, qkv, a, do, tokens, do_first, sums1, sums2, up_sums, chips, cores, chunk
    )
    gate = origin
    if ringed:
        tail[1] = ring.sibling(tie(tail[1], *r_m.ahead_behind()))
        r_m.step(tail[0])
        r_q = Reduce(ring, tuple(tail))
        r_q.step(*r_m.sent)
        gate = gated(origin, r_q.sent)
    d_tokens = input_grad_call(gate, table[-1:], dqkv, dz1, dz1_first, Loader(l_qkv))
    sent = ()
    if ringed:
        r_q.step(d_tokens, c_swap)
        sent = r_q.sent
    sums_shape = jax.ShapeDtypeStruct((own, 3 * width + 128), BF) if ringed else jax.ShapeDtypeStruct((VEC_ROWS, own), F32)
    f_all, f_sums = first_grads_call(
        gated(place, sent), pay_all, d_cross, g_f, n2_f, du_f, dm_f, db_f, total_f, own, sums_shape
    )
    if ringed:
        m_all = r_m.result(f_all)
        r_q.step(m_all)
        m_swap = swap_seq(tie(m_all, *r_q.sent))
        y, cross_out = tie((y, cross_out), *r_q.sent)
    own_rows = lax.dynamic_slice_in_dim(cross_out, me * segs, segs, 0)
    merged = y.reshape(segs, SEG, width).at[:, 0, :].set(own_rows.astype(BF)).reshape(rows, width)
    if ringed:
        r_q.step()
        grad_up, grad_out, grad_down = finish_call(ff, width, m_all, tie(m_swap, *r_q.sent), c_all, c_swap)
        q_all = r_q.result(f_sums)
        grad_qkv, grad_gains, grad_biases, grad_up_bias, grad_table = finish_last_call(
            own, width, group, places_n, q_all, swap_seq(q_all), c_all, c_swap
        )
    else:

        def scattered(x):
            return lax.psum_scatter(x, "shard", scatter_dimension=0, tiled=True)

        def blocks(x):
            return jnp.concatenate([x[:, j * width : (j + 1) * width] for j in range(group)], axis=0)

        feed_sum, main_u, q_sum = main[0][0], scattered(jnp.concatenate([main[0][0][:, ff:], main_o[0][0]], axis=1)), scattered(tail[0][0])
        main_d = scattered(blocks(feed_sum[:, :ff]))
        c_down, c_feed, c_qkv = blocks(c_all[:, :ff]), c_all[:, ff : 2 * ff + width], c_all[:, 2 * ff + width :]
        grad_down = jnp.stack([over_seq(main_d.astype(F32) + blocks(f_all[:, :ff]).astype(F32)), over_seq(c_down)])
        both = jnp.stack([over_seq(main_u.astype(F32) + f_all[:, ff:].astype(F32)), over_seq(c_feed)])
        grad_up, grad_out = both[:, :, :ff], both[:, :, ff:]
        grad_qkv = jnp.stack([over_seq(q_sum), over_seq(c_qkv)])
        vec_sums = jnp.concatenate(
            [sums1[0:1], sums2[0:1], sums_v[0:1], sums1[2:3], sums2[2:3], sums1[1:2], sums2[1:2], jnp.zeros((1, width), F32)]
            + [up_sums[0].reshape(group, width)],
            axis=0,
        )
        vec_sums = lax.psum(vec_sums, ("seq", "shard"))
        seg_vec = lax.dynamic_slice_in_dim(vec_sums[:8], me * own, own, 1)
        seg_up = lax.dynamic_slice_in_dim(vec_sums[8:].reshape(ff), me * own * group, own * group, 0)
        few = over_seq(jnp.concatenate([f_sums, c_sums, c_tab], axis=0))
        first_vec, cross_vec, grad_table = few[:VEC_ROWS], few[VEC_ROWS : 2 * VEC_ROWS], few[2 * VEC_ROWS :]
        seg_vec = seg_vec + first_vec[:8]
        grad_gains = jnp.stack([seg_vec[:2], cross_vec[:2]])
        grad_biases = jnp.stack([seg_vec[2:7], cross_vec[2:7]])
        seg_up = seg_up + first_vec[UP0 : UP0 + group].reshape(-1)
        grad_up_bias = jnp.stack([seg_up, cross_vec[UP0 : UP0 + group].reshape(-1)])
    return (
        merged,
        d_tokens,
        grad_qkv,
        grad_out,
        grad_up,
        grad_down,
        grad_gains,
        grad_biases,
        grad_up_bias,
        grad_table,
    )


def solution(mesh):
    in_specs = (
        P(("seq", "shard"), None),
        P(None, "shard", None),
        P(None, "shard", None),
        P(None, "shard", None),
        P(None, "shard", None),
        P(None, None, "shard"),
        P(None, None, "shard"),
        P(None, "shard"),
        P(None, "shard"),
        P("seq", None),
        P(("seq", "shard"), None),
    )
    out_specs = (
        P(("seq", "shard"), None),
        P(("seq", "shard"), None),
        P(None, "shard", None),
        P(None, "shard", None),
        P(None, "shard", None),
        P(None, "shard", None),
        P(None, None, "shard"),
        P(None, None, "shard"),
        P(None, "shard"),
        P(None, "shard"),
    )
    return jax.shard_map(body, mesh=mesh, in_specs=in_specs, out_specs=out_specs, check_vma=False)
```
